32 devices in a mesh: dp: 8 (over z, x), mp: 4 (over y, core).
Axes of the slice: x: 2, y: 2, z: 4, core: 2. Of those that a mesh axis runs over, the one named last changes fastest.
Arguments:
- tokens_in: bfloat16 [8, 1024, 2048], P('dp'), may hold values from -6 to 6
- cotangent: bfloat16 [8, 1024, 2048], P('dp'), may hold values from -6 to 6
- select_mask: int32 [8, 1024], P('dp'), may hold values 0 or 1
- doc_ids: int32 [8, 1024], P('dp'), may hold values from 0 to 3, never falling along the last dimension, each value on 1 to 512 neighbouring positions
- norm_gains: float32 [2, 2048], replicated, may hold values from 0.5 to 1.5
- weight_blocks: float32 [2688, 128, 128], P(('dp', 'mp'))
- ema_blocks: float32 [2688, 128, 128], P(('dp', 'mp')), may hold values from -1.5 to 1.5
- left_stats: float32 [2688, 128, 128], P(('dp', 'mp')), as said below
- right_stats: float32 [2688, 128, 128], P(('dp', 'mp')), as said below
- left_roots: float32 [2688, 128, 128], P(('dp', 'mp')), as said below
- right_roots: float32 [2688, 128, 128], P(('dp', 'mp')), as said below
Outputs:
- block_out: bfloat16 [8, 1024, 2048], P('dp')
- input_grad: float32 [8, 1024, 2048], P('dp')
- block_grads: float32 [2688, 128, 128], P(('dp', 'mp'))
- new_weights: float32 [2688, 128, 128], P(('dp', 'mp'))
- new_ema: float32 [2688, 128, 128], P(('dp', 'mp'))
- new_left: float32 [2688, 128, 128], P(('dp', 'mp'))
- new_right: float32 [2688, 128, 128], P(('dp', 'mp'))
- gain_grads: float32 [2, 2048], P(None, 'dp')
- new_gains: float32 [2, 2048], P(None, 'dp')
The draws below stay inside these ranges and needn't reach their ends.
Inputs may be any that keep to these rules, and one draw needn't show every extreme that they name: `doc_ids`: within each sequence the ids never fall; every one of the 4 documents has 1 to 512 positions. `left_stats`: each block is symmetric. `right_stats`: each block is symmetric. `left_roots`: each block is symmetric. `right_roots`: each block is symmetric.
All inputs are finite; a program needn't handle non-finite values. No bound on the sum of `select_mask` on one device may be relied on, other than what follows from the above.
Results may differ from the reference program's by a relative error of at most 0.015.
The reference program's roundings to bfloat16 on the way count: a program that leaves them out, or rounds other values in their place, can miss the bound.
Values may be sent and summed in bfloat16 or wider, within the bound.
No kernel may reach another device: no remote copies, remote signals or barrier semaphores. Data moves between devices by JAX's collectives and lax.ppermute only.
A program may use at most 320 MiB of HBM per device.

```python
import math
import jax
import jax.numpy as jnp
import numpy as np
from jax import lax

D = 2048
HEADS = 32
KV_HEADS = 4
HD = 64
BS = 128
SEQ_LEN = 1024
SEQS = 8
TOKENS = 8192
QCOLS = 512
KVCOLS = 64
FFS = 1408
IN_COLS = 3456
OUT_ROWS = 1920
NBLK_IN = 432
NBLK = 672
OWN = 84
BLOCKS_ALL = 2688
N_DP = 8
N_MP = 4


def draw_weight_blocks(key, part):
    group_count = BLOCKS_ALL // NBLK
    global_index = jnp.arange(BLOCKS_ALL, dtype=jnp.int32)
    local_index = global_index // (OWN * group_count) * OWN + global_index % OWN
    out_row = (local_index - NBLK_IN) // (D // BS)
    attention_rows = (local_index >= NBLK_IN) & (out_row < QCOLS // BS)
    scales = jnp.where(attention_rows, 4.0, 1.0) * float(D) ** (-0.5)
    samples = jax.random.normal(key, (BLOCKS_ALL, BS, BS), jnp.float32)
    return samples * scales[:, None, None]


def symmetric_draw(key, diagonal_scale, off_scale, low_end, high_end):
    diag_key, off_key = jax.random.split(key)
    diagonal = jnp.exp(jax.random.uniform(diag_key, (BLOCKS_ALL, BS), jnp.float32, math.log(low_end), math.log(high_end))) * diagonal_scale
    samples = jax.random.normal(off_key, (BLOCKS_ALL, BS, BS), jnp.float32)
    symmetric = (samples + jnp.swapaxes(samples, 1, 2)) * (0.5 * off_scale)
    identity = jnp.eye(BS, dtype=jnp.float32)
    return symmetric + identity[None, :, :] * diagonal[:, :, None]


def draw_left_stats(key, part):
    return symmetric_draw(jax.random.fold_in(key, 11), 0.1 * BS, 0.1 * math.sqrt(BS), 1.0, 4.0)


def draw_right_stats(key, part):
    return symmetric_draw(jax.random.fold_in(key, 12), 0.1 * BS, 0.1 * math.sqrt(BS), 1.0, 4.0)


def draw_left_roots(key, part):
    center = (0.2 * BS) ** (-0.25)
    return symmetric_draw(jax.random.fold_in(key, 13), center, 0.5 * center / math.sqrt(BS), 0.7, 1.4)


def draw_right_roots(key, part):
    center = (0.2 * BS) ** (-0.25)
    return symmetric_draw(jax.random.fold_in(key, 14), center, 0.5 * center / math.sqrt(BS), 0.7, 1.4)


def plant(array, key, low, high):
    longest = array.shape.index(max(array.shape))
    spots = []
    for shift in (0, 1):
        where = [jax.random.randint(jax.random.fold_in(key, axis), (), 0, length) for axis, length in enumerate(array.shape)]
        where[longest] = (where[longest] + shift) % array.shape[longest]
        spots.append(tuple(where))
    return array.at[spots[0]].set(low).at[spots[1]].set(high)


def levels(stream_key, extent, shards, low, largest):
    def one(position, shards_of):
        heights = jax.random.uniform(jax.random.fold_in(jax.random.fold_in(stream_key, 6), position), (shards_of,), jnp.float32, low / len(shards), largest / len(shards))
        return jnp.repeat(jnp.exp(heights), extent[position] // shards_of).reshape((-1,) + (1,) * (len(extent) - position - 1))

    loudness = one(*shards[0])
    for cut in shards[1:]:
        loudness = loudness * one(*cut)
    return loudness


def profile(count, total, bound, skew):
    loads = [(1 << 20) // math.isqrt(standing ** skew) + 1 for standing in range(2, count + 1)]
    spare, given = total - bound - (count - 1), [1] * (count - 1)
    while spare > 0:
        movable = [i for i in range(count - 1) if given[i] < bound]
        whole, remaining = sum([loads[i] for i in movable]), spare
        for i in movable:
            more = min(bound - given[i], max(1, remaining * loads[i] // whole), spare)
            given[i] = given[i] + more
            spare = spare - more
    return np.array([bound] + given)


def uneven_parts(key, number_of, total, bound, skew):
    if number_of == 2:
        one = jax.random.randint(key, (), max(1, total - bound), min(bound, total - 1) + 1)
        return jnp.stack([one, total - one])
    sizes = jnp.asarray(profile(number_of, total, bound, skew), jnp.int32)
    pairs = (number_of - 1) // 2
    source_of, receiver = sizes[1:1 + 2 * pairs:2], sizes[2:2 + 2 * pairs:2]
    margin = jnp.minimum(source_of - 1, bound - receiver)
    shifted = jax.random.randint(jax.random.fold_in(key, 1), (pairs,), 0, 1 << 20) % (margin + 1)
    sizes = sizes.at[1:1 + 2 * pairs:2].set(source_of - shifted).at[2:2 + 2 * pairs:2].set(receiver + shifted)
    return sizes[jax.random.permutation(jax.random.fold_in(key, 2), number_of)]


def centred(stream_key, dims, scale, bound, cuts=(), kind=jnp.bfloat16):
    factor_of = levels(stream_key, dims, cuts, -0.22, 0.18) if cuts else 1.0
    values = jax.random.normal(stream_key, dims, jnp.float32) * scale * factor_of
    return jnp.minimum(jnp.maximum(values, -bound), bound).astype(kind)


def setup_inputs(seed: int = 0) -> dict:
    seeds = jax.random.split(jax.random.key(seed), 12)
    tokens_in = centred(seeds[0], (SEQS, SEQ_LEN, D), 1.0, 6.0, ((0, 8),))
    cotangent = centred(seeds[1], (SEQS, SEQ_LEN, D), 1.0, 6.0, ((0, 8),))
    select_mask = plant((jax.random.randint(seeds[2], (SEQS, SEQ_LEN), 0, 4) < 3).astype(jnp.int32), jax.random.fold_in(seeds[2], 1), 0, 1)
    doc_ids = jax.vmap(lambda own: jnp.searchsorted(jnp.cumsum(uneven_parts(own, 4, SEQ_LEN, SEQ_LEN // 2, 2)), jnp.arange(SEQ_LEN), side="right"))(jax.random.split(seeds[3], SEQS)).reshape((SEQS, SEQ_LEN)).astype(jnp.int32)
    norm_gains = jnp.clip(1.0 + 0.1 * jax.random.normal(seeds[4], (2, D), jnp.float32), 0.5, 1.5)
    weight_blocks = draw_weight_blocks(jax.random.fold_in(seeds[11], 71), 0)
    ema_blocks = centred(seeds[6], (BLOCKS_ALL, BS, BS), 0.1, 1.5, ((0, 32),), jnp.float32)
    left_stats = draw_left_stats(jax.random.fold_in(seeds[11], 71), 0)
    right_stats = draw_right_stats(jax.random.fold_in(seeds[11], 71), 0)
    left_roots = draw_left_roots(jax.random.fold_in(seeds[11], 71), 0)
    right_roots = draw_right_roots(jax.random.fold_in(seeds[11], 71), 0)
    return {"tokens_in": tokens_in, "cotangent": cotangent, "select_mask": select_mask, "doc_ids": doc_ids, "norm_gains": norm_gains, "weight_blocks": weight_blocks, "ema_blocks": ema_blocks, "left_stats": left_stats, "right_stats": right_stats, "left_roots": left_roots, "right_roots": right_roots}


@jax.custom_vjp
def low(v):
    return lax.optimization_barrier(v.astype(jnp.bfloat16)).astype(jnp.float32)

@jax.custom_vjp
def low_back(v):
    return v

def low_keep(v):
    return (low(v), None)

def low_pass(kept, grad):
    return (grad,)

def back_keep(v):
    return (v, None)

def back_low(kept, grad):
    return (low(grad),)
low.defvjp(low_keep, low_pass)
low_back.defvjp(back_keep, back_low)
highest = lax.Precision.HIGHEST
weight_rate = 1.0
gain_rate = 0.2
average_decay = 0.9

def matmul(left_side, right_side):
    return jnp.dot(left_side, right_side, precision=highest, preferred_element_type=jnp.float32)

def doc_positions(doc_ids):
    length = doc_ids.shape[-1]
    offsets = jnp.arange(length, dtype=jnp.int32)
    starts = jnp.concatenate([jnp.ones(doc_ids.shape[:-1] + (1,), jnp.bool_), doc_ids[..., 1:] != doc_ids[..., :-1]], axis=-1)
    first_index = lax.cummax(jnp.where(starts, offsets, 0), axis=doc_ids.ndim - 1)
    return offsets - first_index

def rope_tables(positions, head_size):
    half_size = head_size // 2
    exponent = jnp.arange(half_size, dtype=jnp.float32) * (2.0 / head_size)
    inverse = jnp.power(jnp.float32(10000.0), -exponent)
    angles = positions.astype(jnp.float32)[..., None] * inverse
    return (jnp.cos(angles), jnp.sin(angles))

def rotate(values, cosine_table, sine_table):
    half_size = values.shape[-1] // 2
    first_half = values[..., :half_size]
    second_half = values[..., half_size:]
    return jnp.concatenate([first_half * cosine_table - second_half * sine_table, second_half * cosine_table + first_half * sine_table], axis=-1)

def normalize(values, gain):
    inverse_rms = lax.rsqrt(lax.optimization_barrier(jnp.mean(values * values, axis=-1, keepdims=True)) + 1e-05)
    return values * inverse_rms * gain

def unpack(blocks):
    grouped = blocks.reshape(N_DP, N_MP, OWN, BS, BS).transpose(1, 0, 2, 3, 4).reshape(N_MP, NBLK, BS, BS)
    in_mats = grouped[:, :NBLK_IN].reshape(N_MP, D // BS, IN_COLS // BS, BS, BS).transpose(0, 1, 3, 2, 4).reshape(N_MP, D, IN_COLS)
    out_mats = grouped[:, NBLK_IN:].reshape(N_MP, OUT_ROWS // BS, D // BS, BS, BS).transpose(0, 1, 3, 2, 4).reshape(N_MP, OUT_ROWS, D)

    def columns(begin, count):
        return in_mats[:, :, begin:begin + count].transpose(1, 0, 2).reshape(D, N_MP * count)
    w_query = columns(0, QCOLS)
    w_key = columns(QCOLS, KVCOLS)
    w_value = columns(QCOLS + KVCOLS, KVCOLS)
    w_gate = columns(QCOLS + 2 * KVCOLS, FFS)
    w_up = columns(QCOLS + 2 * KVCOLS + FFS, FFS)
    w_out = out_mats[:, :QCOLS].reshape(N_MP * QCOLS, D)
    w_down = out_mats[:, QCOLS:].reshape(N_MP * FFS, D)
    return (w_query, w_key, w_value, w_out, w_gate, w_up, w_down)

def layer(tokens, doc_ids, matrices, gains):
    w_query, w_key, w_value, w_out, w_gate, w_up, w_down = matrices
    length = tokens.shape[0]
    positions = doc_positions(doc_ids)
    cosine_table, sine_table = rope_tables(positions, HD)
    cosine_table = cosine_table[:, None, :]
    sine_table = sine_table[:, None, :]
    offsets = jnp.arange(length)
    allowed = (offsets[None, :] <= offsets[:, None]) & (doc_ids[None, :] == doc_ids[:, None])
    first_in = low(normalize(tokens, gains[0]))
    queries = low_back(matmul(first_in, w_query)).reshape(length, HEADS, HD)
    keys = low_back(matmul(first_in, w_key)).reshape(length, KV_HEADS, HD)
    values = low_back(matmul(first_in, w_value)).reshape(length, KV_HEADS, HD)
    queries = low(rotate(queries, cosine_table, sine_table))
    keys = low(rotate(keys, cosine_table, sine_table))
    values = low(values)
    group_size = HEADS // KV_HEADS
    grouped = queries.reshape(length, KV_HEADS, group_size, HD)
    scores = jnp.einsum('qgjd,kgd->gjqk', grouped, keys, precision=highest) * HD ** (-0.5)
    scores = low_back(jnp.where(allowed, scores, -1e+30))
    probs = low(jax.nn.softmax(scores, axis=-1))
    mixed = jnp.einsum('gjqk,kgd->qgjd', probs, values, precision=highest).reshape(length, HEADS * HD)
    mixed = low(low_back(mixed))
    middle = tokens + low_back(matmul(mixed, w_out))
    second_in = low(normalize(middle, gains[1]))
    gate = low_back(matmul(second_in, w_gate))
    up_part = low_back(matmul(second_in, w_up))
    hidden = low(jax.nn.silu(gate) * up_part)
    return middle + low_back(matmul(hidden, w_down))

def forward(tokens, blocks, gains, doc_ids):
    matrices = unpack(low(blocks))

    def single(items):
        return layer(items[0], items[1], matrices, gains)
    return lax.map(jax.checkpoint(single), (tokens, doc_ids))

def reference(tokens_in, cotangent, select_mask, doc_ids, norm_gains, weight_blocks, ema_blocks, left_stats, right_stats, left_roots, right_roots):
    tokens = tokens_in.astype(jnp.float32)

    def wrapped(token_values, block_values, gain_values):
        return forward(token_values, block_values, gain_values, doc_ids)
    outputs, pullback = jax.vjp(wrapped, tokens, weight_blocks, norm_gains)
    weighted = cotangent.astype(jnp.float32) * select_mask.astype(jnp.float32)[..., None]
    input_grad, block_sums, gain_sums = pullback(weighted)
    factor = float(TOKENS) ** (-0.5)
    grads = block_sums * factor
    gain_grads = gain_sums * factor
    new_left = 0.5 * left_stats + 0.5 * jnp.einsum('bij,bkj->bik', grads, grads, precision=highest)
    new_right = 0.5 * right_stats + 0.5 * jnp.einsum('bji,bjk->bik', grads, grads, precision=highest)
    right_part = jnp.einsum('bij,bjk->bik', grads, right_roots, precision=highest)
    direction = jnp.einsum('bij,bjk->bik', left_roots, right_part, precision=highest)
    new_weights = weight_blocks - weight_rate * direction
    new_ema = average_decay * ema_blocks + (1.0 - average_decay) * new_weights
    new_gains = norm_gains - gain_rate * gain_grads
    return (outputs.astype(jnp.bfloat16), input_grad, grads, new_weights, new_ema, new_left, new_right, gain_grads, new_gains)
```

```python
import jax
import jax.numpy as jnp
from jax import lax
from jax.sharding import PartitionSpec as P

HEADS = 32
KV_HEADS = 4
HD = 64
FF = 5632


highest = lax.Precision.HIGHEST
weight_rate = 1.0
gain_rate = 0.2
average_decay = 0.9


def doc_positions(doc_ids):
    length = doc_ids.shape[-1]
    offsets = jnp.arange(length, dtype=jnp.int32)
    starts = jnp.concatenate(
        [jnp.ones(doc_ids.shape[:-1] + (1,), jnp.bool_), doc_ids[..., 1:] != doc_ids[..., :-1]],
        axis=-1,
    )
    first_index = lax.cummax(jnp.where(starts, offsets, 0), axis=doc_ids.ndim - 1)
    return offsets - first_index


def rope_tables(positions, head_size):
    half_size = head_size // 2
    exponent = jnp.arange(half_size, dtype=jnp.float32) * (2.0 / head_size)
    inverse = jnp.power(jnp.float32(10000.0), -exponent)
    angles = positions.astype(jnp.float32)[..., None] * inverse
    return (jnp.cos(angles), jnp.sin(angles))


def rotate(values, cosine_table, sine_table):
    half_size = values.shape[-1] // 2
    first_half = values[..., :half_size]
    second_half = values[..., half_size:]
    return jnp.concatenate(
        [
            first_half * cosine_table - second_half * sine_table,
            second_half * cosine_table + first_half * sine_table,
        ],
        axis=-1,
    )


def rotate_back(grads, cosine_table, sine_table):
    half_size = grads.shape[-1] // 2
    first_half = grads[..., :half_size]
    second_half = grads[..., half_size:]
    return jnp.concatenate(
        [
            first_half * cosine_table + second_half * sine_table,
            second_half * cosine_table - first_half * sine_table,
        ],
        axis=-1,
    )


def normalize(values, gain):
    inverse_rms = lax.rsqrt(jnp.mean(values * values, axis=-1, keepdims=True) + 1e-05)
    unit = values * inverse_rms
    return (unit * gain, unit, inverse_rms)


def normalize_back(grad_out, unit, inverse_rms, gain):
    scaled = grad_out * gain
    return inverse_rms * (scaled - unit * jnp.mean(scaled * unit, axis=-1, keepdims=True))


def project(inputs, weights):
    row_count = inputs.shape[0]
    shaped = inputs.reshape(row_count, weights.shape[0], weights.shape[-1])
    return jnp.einsum("tri,rcij->tcj", shaped, weights, preferred_element_type=jnp.float32).reshape(
        row_count, -1
    )


def project_back(grads, weights):
    row_count = grads.shape[0]
    shaped = grads.reshape(row_count, weights.shape[1], weights.shape[-1])
    return jnp.einsum("tcj,rcij->tri", shaped, weights, preferred_element_type=jnp.float32).reshape(
        row_count, -1
    )


def weight_grad(inputs, grads, block_size):
    row_count = inputs.shape[0]
    left_shaped = inputs.reshape(row_count, -1, block_size)
    right_shaped = grads.reshape(row_count, -1, block_size)
    return jnp.einsum(
        "tri,tcj->rcij", left_shaped, right_shaped, preferred_element_type=jnp.float32
    )


def split_weights(gathered, row_blocks, attn_blocks, in_blocks, out_attn_blocks):
    block_size = gathered.shape[-1]
    in_count = row_blocks * in_blocks
    w_input = gathered[:in_count].reshape(row_blocks, in_blocks, block_size, block_size)
    w_output = gathered[in_count:].reshape(-1, row_blocks, block_size, block_size)
    return (
        w_input[:, :attn_blocks],
        w_input[:, attn_blocks:],
        w_output[:out_attn_blocks],
        w_output[out_attn_blocks:],
    )


def block_scores(query_part, keys, doc_ids, offset, scale):
    row_count = query_part.shape[0]
    query_index = offset + jnp.arange(row_count)
    key_index = jnp.arange(keys.shape[0])
    allowed = (key_index[None, :] <= query_index[:, None]) & (
        doc_ids[None, :] == doc_ids[offset : offset + row_count][:, None]
    )
    scores = (
        jnp.einsum("qgjd,kgd->gjqk", query_part, keys, preferred_element_type=jnp.float32) * scale
    )
    return jnp.where(allowed, scores, -1e30)


def attend_forward(queries, keys, values, doc_ids, query_block):
    length = queries.shape[0]
    scale = float(queries.shape[-1]) ** (-0.5)
    outputs = []
    totals = []
    for offset in range(0, length, query_block):
        scores = block_scores(queries[offset : offset + query_block], keys, doc_ids, offset, scale)
        maximum = jnp.max(scores, axis=-1, keepdims=True)
        expo_values = jnp.exp(scores - maximum)
        denominator = jnp.sum(expo_values, axis=-1, keepdims=True)
        probs = (expo_values / denominator).astype(jnp.bfloat16)
        outputs.append(
            jnp.einsum("gjqk,kgd->qgjd", probs, values, preferred_element_type=jnp.float32)
        )
        totals.append(maximum + jnp.log(denominator))
    return (jnp.concatenate(outputs, axis=0), jnp.concatenate(totals, axis=2))


def attend_backward(queries, keys, values, doc_ids, log_totals, out_grads, query_block):
    length = queries.shape[0]
    scale = float(queries.shape[-1]) ** (-0.5)
    key_grads = jnp.zeros(keys.shape, jnp.float32)
    value_grads = jnp.zeros(values.shape, jnp.float32)
    query_grads = []
    for offset in range(0, length, query_block):
        query_part = queries[offset : offset + query_block]
        scores = block_scores(query_part, keys, doc_ids, offset, scale)
        probs = jnp.exp(scores - log_totals[:, :, offset : offset + query_block])
        grad_part = out_grads[offset : offset + query_block]
        value_grads = value_grads + jnp.einsum(
            "gjqk,qgjd->kgd",
            probs.astype(jnp.bfloat16),
            grad_part,
            preferred_element_type=jnp.float32,
        )
        prob_grads = jnp.einsum(
            "qgjd,kgd->gjqk", grad_part, values, preferred_element_type=jnp.float32
        )
        inner = jnp.sum(probs * prob_grads, axis=-1, keepdims=True)
        score_grads = (probs * (prob_grads - inner)).astype(jnp.bfloat16)
        query_grads.append(
            jnp.einsum("gjqk,kgd->qgjd", score_grads, keys, preferred_element_type=jnp.float32)
            * scale
        )
        key_grads = (
            key_grads
            + jnp.einsum(
                "gjqk,qgjd->kgd", score_grads, query_part, preferred_element_type=jnp.float32
            )
            * scale
        )
    return (jnp.concatenate(query_grads, axis=0), key_grads, value_grads)


def ring_order(count):
    return list(range(0, count, 2)) + list(range(1, count, 2))[::-1]


def sum_rows(values):
    return lax.psum_scatter(
        values.astype(jnp.bfloat16), "mp", scatter_dimension=0, tiled=True
    ).astype(jnp.float32)


def on_device(
    tokens_in,
    cotangent,
    select_mask,
    doc_ids,
    norm_gains,
    weight_blocks,
    ema_blocks,
    left_stats,
    right_stats,
    left_roots,
    right_roots,
):
    mp_count = lax.axis_size("mp")
    dp_count = lax.axis_size("dp")
    sequences, length, model_width = tokens_in.shape
    row_count = sequences * length
    block_size = weight_blocks.shape[-1]
    query_cols = HEADS * HD // mp_count
    key_cols = KV_HEADS * HD // mp_count
    hidden_cols = FF // mp_count
    kv_local = KV_HEADS // mp_count
    group_size = HEADS // KV_HEADS
    row_blocks = model_width // block_size
    attn_blocks = (query_cols + 2 * key_cols) // block_size
    in_blocks = attn_blocks + 2 * hidden_cols // block_size
    out_attn_blocks = query_cols // block_size
    query_block = min(512, length)
    share_rows = row_count // mp_count
    share_start = lax.axis_index("mp") * share_rows

    def row_share(values):
        return lax.dynamic_slice_in_dim(values, share_start, share_rows, 0)

    ring = ring_order(dp_count)
    places = [ring.index(rank) for rank in range(dp_count)]
    own = weight_blocks.shape[0]
    weights_low = weight_blocks.astype(jnp.bfloat16)
    in_ring = lax.all_gather(weights_low, "dp", axis=0, tiled=True, axis_index_groups=[ring])
    gathered = jnp.concatenate(
        [in_ring[place * own : (place + 1) * own] for place in places], axis=0
    )
    w_qkv, w_gateup, w_attn_out, w_down = split_weights(
        gathered, row_blocks, attn_blocks, in_blocks, out_attn_blocks
    )
    positions = doc_positions(doc_ids)
    cosine_table, sine_table = rope_tables(positions, HD)
    query_cos = cosine_table[:, :, None, None, :]
    query_sin = sine_table[:, :, None, None, :]
    key_cos = cosine_table[:, :, None, :]
    key_sin = sine_table[:, :, None, :]
    tokens = tokens_in.astype(jnp.float32).reshape(row_count, model_width)
    first_norm, first_unit, first_scale = normalize(tokens, norm_gains[0])
    first_in = first_norm.astype(jnp.bfloat16)
    qkv = project(first_in, w_qkv)
    queries_raw = qkv[:, :query_cols].reshape(sequences, length, kv_local, group_size, HD)
    keys_raw = qkv[:, query_cols : query_cols + key_cols].reshape(sequences, length, kv_local, HD)
    values_raw = qkv[:, query_cols + key_cols :].reshape(sequences, length, kv_local, HD)
    query_use = rotate(queries_raw, query_cos, query_sin).astype(jnp.bfloat16)
    key_use = rotate(keys_raw, key_cos, key_sin).astype(jnp.bfloat16)
    value_use = values_raw.astype(jnp.bfloat16)

    def forward_one(items):
        return attend_forward(items[0], items[1], items[2], items[3], query_block)

    mixed, log_totals = lax.map(forward_one, (query_use, key_use, value_use, doc_ids))
    mixed_use = mixed.reshape(row_count, query_cols).astype(jnp.bfloat16)
    attended_part = sum_rows(project(mixed_use, w_attn_out))
    middle = row_share(tokens) + attended_part
    second_norm, second_unit, second_scale = normalize(middle, norm_gains[1])
    second_in = lax.all_gather(second_norm.astype(jnp.bfloat16), "mp", axis=0, tiled=True)
    gateup = project(second_in, w_gateup)
    gate = gateup[:, :hidden_cols]
    up_part = gateup[:, hidden_cols:]
    sigmoid_gate = jax.nn.sigmoid(gate)
    hidden = (gate * sigmoid_gate * up_part).astype(jnp.bfloat16)
    feed_part = sum_rows(project(hidden, w_down))
    out_whole = lax.all_gather((middle + feed_part).astype(jnp.bfloat16), "mp", axis=0, tiled=True)
    block_out = out_whole.reshape(sequences, length, model_width)
    out_grad = cotangent.astype(jnp.float32).reshape(row_count, model_width) * select_mask.astype(
        jnp.float32
    ).reshape(row_count, 1)
    mlp_grad = out_grad.astype(jnp.bfloat16)
    grad_down = weight_grad(hidden, mlp_grad, block_size)
    hidden_grad = project_back(mlp_grad, w_down)
    gate_grad = hidden_grad * up_part * sigmoid_gate * (1.0 + gate * (1.0 - sigmoid_gate))
    up_grad = hidden_grad * gate * sigmoid_gate
    gateup_grad = jnp.concatenate([gate_grad, up_grad], axis=1).astype(jnp.bfloat16)
    grad_gateup = weight_grad(second_in, gateup_grad, block_size)
    second_grad = sum_rows(project_back(gateup_grad, w_gateup))
    middle_grad = row_share(out_grad) + normalize_back(
        second_grad, second_unit, second_scale, norm_gains[1]
    )
    second_gain = jnp.sum(second_grad * second_unit, axis=0)
    attn_grad = lax.all_gather(middle_grad.astype(jnp.bfloat16), "mp", axis=0, tiled=True)
    grad_attn_out = weight_grad(mixed_use, attn_grad, block_size)
    mixed_grad = (
        project_back(attn_grad, w_attn_out)
        .astype(jnp.bfloat16)
        .reshape(sequences, length, kv_local, group_size, HD)
    )

    def backward_one(items):
        return attend_backward(
            items[0], items[1], items[2], items[3], items[4], items[5], query_block
        )

    query_grad, key_grad, value_grad = lax.map(
        backward_one, (query_use, key_use, value_use, doc_ids, log_totals, mixed_grad)
    )
    query_grad = rotate_back(query_grad, query_cos, query_sin).reshape(row_count, query_cols)
    key_grad = rotate_back(key_grad, key_cos, key_sin).reshape(row_count, key_cols)
    qkv_grad = jnp.concatenate(
        [query_grad, key_grad, value_grad.reshape(row_count, key_cols)], axis=1
    ).astype(jnp.bfloat16)
    grad_qkv = weight_grad(first_in, qkv_grad, block_size)
    first_grad = sum_rows(project_back(qkv_grad, w_qkv))
    unit_share = row_share(first_unit)
    input_part = middle_grad + normalize_back(
        first_grad, unit_share, row_share(first_scale), norm_gains[0]
    )
    first_gain = jnp.sum(first_grad * unit_share, axis=0)
    gain_part = jnp.stack([first_gain, second_gain], axis=0)
    input_grad, gain_rows = (
        lax.all_gather(input_part.astype(jnp.bfloat16), "mp", axis=0, tiled=True).astype(jnp.float32),
        lax.all_gather(gain_part, "mp", axis=0, tiled=True),
    )
    gain_terms = jnp.sum(gain_rows.reshape(mp_count, 2, model_width), axis=0)
    in_grads = jnp.concatenate([grad_qkv, grad_gateup], axis=1).reshape(-1, block_size, block_size)
    out_grads = jnp.concatenate([grad_attn_out, grad_down], axis=0).reshape(
        -1, block_size, block_size
    )
    all_grads = jnp.concatenate([in_grads, out_grads], axis=0).astype(jnp.bfloat16)
    reduced, gain_sums = (
        lax.psum_scatter(
            jnp.concatenate([all_grads[rank * own : (rank + 1) * own] for rank in ring], axis=0),
            "dp",
            scatter_dimension=0,
            tiled=True,
            axis_index_groups=[ring],
        ).astype(jnp.float32),
        lax.psum_scatter(gain_terms, "dp", scatter_dimension=1, tiled=True),
    )
    factor = float(row_count * dp_count) ** (-0.5)
    grads = reduced * factor
    gain_grads = gain_sums * factor
    new_left = 0.5 * left_stats + 0.5 * jnp.einsum("bij,bkj->bik", grads, grads, precision=highest)
    new_right = 0.5 * right_stats + 0.5 * jnp.einsum(
        "bji,bjk->bik", grads, grads, precision=highest
    )
    right_part = jnp.einsum("bij,bjk->bik", grads, right_roots, precision=highest)
    direction = jnp.einsum("bij,bjk->bik", left_roots, right_part, precision=highest)
    new_weights = weight_blocks - weight_rate * direction
    new_ema = average_decay * ema_blocks + (1.0 - average_decay) * new_weights
    share = model_width // dp_count
    gain_share = lax.dynamic_slice_in_dim(norm_gains, lax.axis_index("dp") * share, share, 1)
    new_gains = gain_share - gain_rate * gain_grads
    input_out = input_grad.reshape(sequences, length, model_width)
    return (
        block_out,
        input_out,
        grads,
        new_weights,
        new_ema,
        new_left,
        new_right,
        gain_grads,
        new_gains,
    )


def solution(mesh):
    in_specs = (
        P("dp", None, None),
        P("dp", None, None),
        P("dp", None),
        P("dp", None),
        P(),
        P(("dp", "mp"), None, None),
        P(("dp", "mp"), None, None),
        P(("dp", "mp"), None, None),
        P(("dp", "mp"), None, None),
        P(("dp", "mp"), None, None),
        P(("dp", "mp"), None, None),
    )
    out_specs = (
        P("dp", None, None),
        P("dp", None, None),
        P(("dp", "mp"), None, None),
        P(("dp", "mp"), None, None),
        P(("dp", "mp"), None, None),
        P(("dp", "mp"), None, None),
        P(("dp", "mp"), None, None),
        P(None, "dp"),
        P(None, "dp"),
    )
    return jax.shard_map(
        on_device, mesh=mesh, in_specs=in_specs, out_specs=out_specs, check_vma=False
    )
```

```python
import functools

import jax
import jax.numpy as jnp
import numpy as np
from jax import lax
from jax.experimental import pallas as pl
from jax.experimental.pallas import tpu as pltpu
from jax.sharding import PartitionSpec as P

HEADS = 32
KV_HEADS = 4
HD = 64
FF = 5632
LOW = jnp.bfloat16
F32 = jnp.float32

weight_rate = 1.0
gain_rate = 0.2
average_decay = 0.9
VMEM_LIMIT = 60 * 1024 * 1024


def ring_order(count):
    return list(range(0, count, 2)) + list(range(1, count, 2))[::-1]


class Layout:
    def __init__(self, dp, own, rows, attn_cols, in_cols, out_attn_rows):
        self.dp, self.own = dp, own
        self.ring = ring_order(dp)
        n_in = rows * in_cols
        kinds, spots = [], []
        for k in range(dp * own):
            if k < n_in:
                r, c = divmod(k, in_cols)
                if c < attn_cols:
                    kinds.append(0), spots.append((0, r, c))
                else:
                    kinds.append(2), spots.append((2, r, c - attn_cols))
            else:
                r, c = divmod(k - n_in, rows)
                if r < out_attn_rows:
                    kinds.append(1), spots.append((1, r, c))
                else:
                    kinds.append(2), spots.append((3, r - out_attn_rows, c))
        self.order = np.zeros((dp, own), np.int32)
        for d in range(dp):
            mine = kinds[d * own : (d + 1) * own]
            self.order[d] = sorted(range(own), key=lambda l: (mine[l], l))
        count = np.array(kinds).reshape(dp, own)
        first = int((count == 0).sum(1).max())
        second = int((count <= 1).sum(1).max())
        bounds = [0, first, max(first, second), own]
        self.chunks = [(a, b - a) for a, b in zip(bounds[:-1], bounds[1:]) if b > a]
        self.table = []
        for p, d in enumerate(self.ring):
            for j, l in enumerate(self.order[d]):
                (x,) = [i for i, (a, n) in enumerate(self.chunks) if a <= j < a + n]
                a, n = self.chunks[x]
                self.table.append(spots[d * own + int(l)] + (x, p * n + j - a))

    def of_chunk(self, x, matrix):
        rows = [(s, r, c) for m, r, c, y, s in self.table if y == x and m == matrix]
        return np.array(sorted(rows), np.int32).reshape(-1, 3)

    def of_matrix(self, matrix, rows, cols):
        out = np.zeros((cols, rows, 2), np.int32)
        for m, r, c, x, s in self.table:
            if m == matrix:
                out[c, r] = (x, s)
        return out


ANY = pl.BlockSpec(memory_space=pl.ANY)
SMEM = pl.BlockSpec(memory_space=pltpu.SMEM)
VMEM = pl.BlockSpec(memory_space=pltpu.VMEM)


def sort_blocks(weights, order, chunks):
    block = weights.shape[1:]

    def body(order_ref, w_ref, *outs):
        for (start, count), out in zip(chunks, outs):

            def one(j, carry, start=start, out=out):
                out[j] = w_ref[order_ref[start + j]].astype(LOW)
                return carry

            lax.fori_loop(0, count, one, 0)

    return pl.pallas_call(
        body,
        out_shape=[jax.ShapeDtypeStruct((n,) + block, LOW) for _, n in chunks],
        in_specs=[SMEM, VMEM],
        out_specs=[VMEM] * len(chunks),
        compiler_params=pltpu.CompilerParams(vmem_limit_bytes=VMEM_LIMIT),
        name="sort_blocks",
    )(order, weights)


def place_blocks(gathered, tables, shapes, partial):
    block = gathered.shape[-1]
    used = [i for i, t in enumerate(tables) if len(t)]
    count = sum(len(tables[i]) for i in used)
    known = [i for i in used if partial[i] is not None]

    def body(*refs):
        table_refs = refs[: len(used)]
        src = refs[len(used)]
        outs = refs[len(used) + 1 + len(known) : -3]
        stage, sem_in, sem_out = refs[-3:]
        load = pltpu.make_async_copy(src, stage, sem_in)
        load.start()
        load.wait()
        for i, table_ref, out in zip(used, table_refs, outs):

            def one(j, carry, table_ref=table_ref, out=out):
                row = pl.multiple_of(table_ref[3 * j + 1] * block, block)
                col = pl.multiple_of(table_ref[3 * j + 2] * block, block)
                pltpu.make_async_copy(
                    stage.at[table_ref[3 * j]],
                    out.at[pl.ds(row, block), pl.ds(col, block)],
                    sem_out,
                ).start()
                return carry

            lax.fori_loop(0, len(tables[i]), one, 0)
        pltpu.make_async_copy(stage, stage, sem_out).wait()

    assert count == gathered.shape[0]
    results = pl.pallas_call(
        body,
        out_shape=[jax.ShapeDtypeStruct(shapes[i], LOW) for i in used],
        in_specs=[SMEM] * len(used) + [ANY] * (1 + len(known)),
        out_specs=[ANY] * len(used),
        input_output_aliases={len(used) + 1 + j: used.index(i) for j, i in enumerate(known)},
        scratch_shapes=[
            pltpu.VMEM(gathered.shape, LOW),
            pltpu.SemaphoreType.DMA,
            pltpu.SemaphoreType.DMA,
        ],
        compiler_params=pltpu.CompilerParams(vmem_limit_bytes=VMEM_LIMIT),
        name="place_blocks",
    )(
        *[jnp.asarray(tables[i].reshape(-1)) for i in used],
        gathered,
        *[partial[i] for i in known],
    )
    merged = list(partial)
    for i, value in zip(used, results):
        merged[i] = value
    return merged


def grad_blocks(left, right, table, wide, buffers, sizes, block):
    tokens, height = left.shape
    width = right.shape[1]
    rows, cols = height // block, width // block
    steps = cols // wide
    per_step = rows * wide
    used = sorted(set(table[:, :, 0].reshape(-1).tolist()))
    known = [x for x in used if buffers[x] is not None]

    def body(*refs):
        table_ref, left_ref, right_ref = refs[:3]
        outs = refs[3 + len(known) : 3 + len(known) + len(used)]
        turned, stage, sems = refs[-3:]
        turned[...] = left_ref[...].T

        def finish(slot):
            pltpu.make_async_copy(stage.at[slot], stage.at[slot], sems.at[slot]).wait()

        def step(t, carry):
            slot = lax.rem(t, 2)

            @pl.when(t >= 2)
            def _():
                finish(slot)

            col = pl.multiple_of(t * (wide * block), wide * block)
            part = jnp.dot(
                turned[...], right_ref[:, pl.ds(col, wide * block)], preferred_element_type=F32
            ).astype(LOW)
            for r in range(rows):
                for c in range(wide):
                    stage[slot, c * rows + r] = part[
                        r * block : (r + 1) * block, c * block : (c + 1) * block
                    ]

            def send(j, carry):
                at = 2 * (t * per_step + j)
                for x, out in zip(used, outs):

                    @pl.when(table_ref[at] == x)
                    def _(out=out):
                        pltpu.make_async_copy(
                            stage.at[slot, j], out.at[table_ref[at + 1]], sems.at[slot]
                        ).start()

                return carry

            lax.fori_loop(0, per_step, send, 0)
            return carry

        lax.fori_loop(0, steps, step, 0)
        for t in range(max(0, steps - 2), steps):
            finish(t % 2)

    results = pl.pallas_call(
        body,
        out_shape=[jax.ShapeDtypeStruct((sizes[x], block, block), LOW) for x in used],
        in_specs=[SMEM, VMEM, VMEM] + [ANY] * len(known),
        out_specs=[ANY] * len(used),
        input_output_aliases={3 + j: used.index(x) for j, x in enumerate(known)},
        scratch_shapes=[
            pltpu.VMEM((height, tokens), LOW),
            pltpu.VMEM((2, per_step, block, block), LOW),
            pltpu.SemaphoreType.DMA((2,)),
        ],
        compiler_params=pltpu.CompilerParams(vmem_limit_bytes=VMEM_LIMIT),
        cost_estimate=pl.CostEstimate(
            flops=2 * tokens * height * width,
            bytes_accessed=2 * (tokens * (height + width) + height * width),
            transcendentals=0,
        ),
        name="grad_blocks",
    )(jnp.asarray(table.reshape(-1)), left, right, *[buffers[x] for x in known])
    merged = list(buffers)
    for x, value in zip(used, results):
        merged[x] = value
    return merged


def shampoo(sums, places, factor, weights, ema, left, right, left_roots, right_roots, before):
    count, block, _ = sums.shape

    def mm(a, b, dims):
        return lax.dot_general(
            a.astype(LOW), b.astype(LOW), (dims, ((), ())), preferred_element_type=F32
        )

    def body(places_ref, g_ref, w_ref, e_ref, l_ref, r_ref, lr_ref, rr_ref, *rest):
        og, ow, oe, ol, orr = rest[-5:]
        low = g_ref[0]
        og[0] = low.astype(F32) * factor
        both = 0.5 * factor * factor
        ol[0] = 0.5 * l_ref[0] + both * mm(low, low, ((1,), (1,)))
        orr[0] = 0.5 * r_ref[0] + both * mm(low, low, ((0,), (0,)))
        part = mm(low, rr_ref[0], ((1,), (0,))) * factor
        fresh = w_ref[0] - weight_rate * mm(lr_ref[0], part, ((1,), (0,)))
        ow[0] = fresh
        oe[0] = average_decay * e_ref[0] + (1.0 - average_decay) * fresh

    own = pl.BlockSpec((1, block, block), lambda i, places_ref: (places_ref[i], 0, 0))
    here = pl.BlockSpec((1, block, block), lambda i, places_ref: (i, 0, 0))
    extra = [] if before is None else list(before)
    shape = jax.ShapeDtypeStruct(weights.shape, F32)
    return pl.pallas_call(
        body,
        out_shape=[shape] * 5,
        grid_spec=pltpu.PrefetchScalarGridSpec(
            num_scalar_prefetch=1,
            grid=(count,),
            in_specs=[here] + [own] * 6 + [ANY] * len(extra),
            out_specs=[own] * 5,
        ),
        input_output_aliases={8 + i: i for i in range(len(extra))},
        compiler_params=pltpu.CompilerParams(dimension_semantics=("arbitrary",)),
        cost_estimate=pl.CostEstimate(
            flops=8 * count * block**3,
            bytes_accessed=46 * count * block * block,
            transcendentals=0,
        ),
        name="shampoo",
    )(places, sums, weights, ema, left, right, left_roots, right_roots, *extra)


def doc_positions(doc_ids):
    length = doc_ids.shape[-1]
    offsets = jnp.arange(length, dtype=jnp.int32)
    starts = jnp.concatenate(
        [jnp.ones(doc_ids.shape[:-1] + (1,), jnp.bool_), doc_ids[..., 1:] != doc_ids[..., :-1]],
        axis=-1,
    )
    first_index = lax.cummax(jnp.where(starts, offsets, 0), axis=doc_ids.ndim - 1)
    return offsets - first_index


def rope_tables(positions, head_size):
    half_size = head_size // 2
    exponent = jnp.arange(half_size, dtype=F32) * (2.0 / head_size)
    inverse = jnp.power(F32(10000.0), -exponent)
    angles = positions.astype(F32)[..., None] * inverse
    return (jnp.cos(angles), jnp.sin(angles))


def rotate(values, cosine_table, sine_table):
    half_size = values.shape[-1] // 2
    first_half = values[..., :half_size]
    second_half = values[..., half_size:]
    return jnp.concatenate(
        [
            first_half * cosine_table - second_half * sine_table,
            second_half * cosine_table + first_half * sine_table,
        ],
        axis=-1,
    )


def rotate_back(grads, cosine_table, sine_table):
    return rotate(grads, cosine_table, -sine_table)


def block_scores(query_part, keys, doc_ids, offset, scale):
    row_count = query_part.shape[0]
    query_index = offset + jnp.arange(row_count)
    key_index = jnp.arange(keys.shape[0])
    allowed = (key_index[None, :] <= query_index[:, None]) & (
        doc_ids[None, :] == doc_ids[offset : offset + row_count][:, None]
    )
    scores = jnp.einsum("qgjd,kgd->gjqk", query_part, keys, preferred_element_type=F32) * scale
    return jnp.where(allowed, scores, -1e30)


def attend_forward(queries, keys, values, doc_ids, query_block):
    length = queries.shape[0]
    scale = float(queries.shape[-1]) ** (-0.5)
    outputs = []
    totals = []
    for offset in range(0, length, query_block):
        scores = block_scores(queries[offset : offset + query_block], keys, doc_ids, offset, scale)
        maximum = jnp.max(scores, axis=-1, keepdims=True)
        expo_values = jnp.exp(scores - maximum)
        denominator = jnp.sum(expo_values, axis=-1, keepdims=True)
        probs = (expo_values / denominator).astype(LOW)
        outputs.append(jnp.einsum("gjqk,kgd->qgjd", probs, values, preferred_element_type=F32))
        totals.append(maximum + jnp.log(denominator))
    return (jnp.concatenate(outputs, axis=0), jnp.concatenate(totals, axis=2))


def attend_backward(queries, keys, values, doc_ids, log_totals, out_grads, query_block):
    length = queries.shape[0]
    scale = float(queries.shape[-1]) ** (-0.5)
    key_grads = jnp.zeros(keys.shape, F32)
    value_grads = jnp.zeros(values.shape, F32)
    query_grads = []
    for offset in range(0, length, query_block):
        query_part = queries[offset : offset + query_block]
        scores = block_scores(query_part, keys, doc_ids, offset, scale)
        probs = jnp.exp(scores - log_totals[:, :, offset : offset + query_block])
        grad_part = out_grads[offset : offset + query_block]
        value_grads = value_grads + jnp.einsum(
            "gjqk,qgjd->kgd", probs.astype(LOW), grad_part, preferred_element_type=F32
        )
        prob_grads = jnp.einsum("qgjd,kgd->gjqk", grad_part, values, preferred_element_type=F32)
        inner = jnp.sum(probs * prob_grads, axis=-1, keepdims=True)
        score_grads = (probs * (prob_grads - inner)).astype(LOW)
        query_grads.append(
            jnp.einsum("gjqk,kgd->qgjd", score_grads, keys, preferred_element_type=F32) * scale
        )
        key_grads = (
            key_grads
            + jnp.einsum("gjqk,qgjd->kgd", score_grads, query_part, preferred_element_type=F32)
            * scale
        )
    return (jnp.concatenate(query_grads, axis=0), key_grads, value_grads)


def dot(left, right):
    return jnp.dot(left, right, preferred_element_type=F32)


def dot_turned(left, right):
    return lax.dot_general(left, right, (((1,), (1,)), ((), ())), preferred_element_type=F32)


EXCHANGE = (0, 2, 1, 3)


def on_device(
    tokens_in,
    cotangent,
    select_mask,
    doc_ids,
    norm_gains,
    weight_blocks,
    ema_blocks,
    left_stats,
    right_stats,
    left_roots,
    right_roots,
):
    mp_count = lax.axis_size("mp")
    dp_count = lax.axis_size("dp")
    sequences, length, model_width = tokens_in.shape
    assert sequences == 1 and mp_count == 4 and dp_count & (dp_count - 1) == 0
    rows = sequences * length
    own, block, _ = weight_blocks.shape
    query_cols = HEADS * HD // mp_count
    key_cols = KV_HEADS * HD // mp_count
    hidden_cols = FF // mp_count
    kv_local = KV_HEADS // mp_count
    group_size = HEADS // KV_HEADS
    row_blocks = model_width // block
    attn_blocks = (query_cols + 2 * key_cols) // block
    hidden_blocks = hidden_cols // block
    in_blocks = attn_blocks + 2 * hidden_blocks
    out_attn_blocks = query_cols // block
    query_block = min(512, length)
    share = rows // mp_count
    m_index = lax.axis_index("mp")
    d_index = lax.axis_index("dp")

    plan = Layout(dp_count, own, row_blocks, attn_blocks, in_blocks, out_attn_blocks)
    order = lax.dynamic_slice_in_dim(jnp.asarray(plan.order), d_index, 1, 0).reshape(-1)
    shapes = [
        (model_width, attn_blocks * block),
        (query_cols, model_width),
        (model_width, 2 * hidden_cols),
        (hidden_cols, model_width),
    ]

    def partner(values, bit):
        return lax.ppermute(values, "mp", [(i, i ^ bit) for i in range(mp_count)])

    def true_share(values, group):
        return lax.dynamic_slice_in_dim(values, (m_index ^ group) * share, share, 0)

    def to_exchange(values):
        return jnp.concatenate([true_share(values, g) for g in EXCHANGE], axis=0)

    def to_true(parts):
        by_group = [parts[EXCHANGE.index(g)] for g in range(4)]
        low, high = m_index & 1, m_index & 2
        pairs = []
        for a, b in ((0, 1), (2, 3)):
            pairs.append(
                (
                    jnp.where(low == 0, by_group[a], by_group[b]),
                    jnp.where(low == 0, by_group[b], by_group[a]),
                )
            )
        flat = []
        for first, second in ((0, 1), (1, 0)):
            for i in range(2):
                flat.append(jnp.where(high == 0, pairs[first][i], pairs[second][i]))
        return jnp.concatenate(flat, axis=0)

    def sum_shares(sent, kept):
        got = partner(sent, 1).astype(F32)
        kept = kept.astype(F32) + got
        return kept[:share] + partner(kept[share:].astype(LOW), 2).astype(F32)

    def spread_share(mine):
        near = partner(mine, 1)
        far = partner(mine, 2)
        return [mine, far, near, partner(far, 1)]

    sorted_low = sort_blocks(weight_blocks, order, plan.chunks)
    matrices = [None] * 4
    for x, chunk in enumerate(sorted_low):
        gathered = lax.all_gather(chunk, "dp", axis=0, tiled=True, axis_index_groups=[plan.ring])
        matrices = place_blocks(
            gathered, [plan.of_chunk(x, i) for i in range(4)], shapes, matrices
        )
        if x == 0:
            w_qkv = matrices[0]
    w_attn_out, w_gateup, w_down = matrices[1:]

    positions = doc_positions(doc_ids)
    cosine_table, sine_table = rope_tables(positions, HD)
    query_cos = cosine_table[:, :, None, None, :]
    query_sin = sine_table[:, :, None, None, :]
    key_cos = cosine_table[:, :, None, :]
    key_sin = sine_table[:, :, None, :]

    tokens_low = tokens_in.reshape(rows, model_width)
    tokens = tokens_low.astype(F32)
    first_scale = lax.rsqrt(jnp.mean(tokens * tokens, axis=-1, keepdims=True) + 1e-05)
    first_in = (tokens * first_scale * norm_gains[0]).astype(LOW)
    out_grad = cotangent.reshape(rows, model_width).astype(F32) * select_mask.astype(F32).reshape(
        rows, 1
    )
    mlp_grad = to_exchange(out_grad.astype(LOW))
    own_tokens = true_share(tokens_low, 0).astype(F32)
    own_scale = lax.rsqrt(jnp.mean(own_tokens * own_tokens, axis=-1, keepdims=True) + 1e-05)
    own_unit = own_tokens * own_scale

    qkv = dot(first_in, w_qkv)
    queries_raw = qkv[:, :query_cols].reshape(sequences, length, kv_local, group_size, HD)
    keys_raw = qkv[:, query_cols : query_cols + key_cols].reshape(sequences, length, kv_local, HD)
    values_raw = qkv[:, query_cols + key_cols :].reshape(sequences, length, kv_local, HD)
    query_use = rotate(queries_raw, query_cos, query_sin).astype(LOW)
    key_use = rotate(keys_raw, key_cos, key_sin).astype(LOW)
    value_use = values_raw.astype(LOW)
    mixed, log_totals = attend_forward(
        query_use[0], key_use[0], value_use[0], doc_ids[0], query_block
    )
    mixed_use = to_exchange(mixed.reshape(rows, query_cols).astype(LOW))
    half = rows // 2
    attended_part = sum_shares(
        dot(mixed_use[half:], w_attn_out).astype(LOW), dot(mixed_use[:half], w_attn_out).astype(LOW)
    )
    middle = own_tokens + attended_part
    second_scale = lax.rsqrt(jnp.mean(middle * middle, axis=-1, keepdims=True) + 1e-05)
    second_unit = middle * second_scale
    second_in = jnp.concatenate(
        spread_share((second_unit * norm_gains[1]).astype(LOW)), axis=0
    )
    hidden_grad = dot_turned(mlp_grad, w_down)
    gateup = dot(second_in, w_gateup)
    gate = gateup[:, :hidden_cols]
    up_part = gateup[:, hidden_cols:]
    sigmoid_gate = jax.nn.sigmoid(gate)
    hidden = (gate * sigmoid_gate * up_part).astype(LOW)
    gate_grad = hidden_grad * up_part * sigmoid_gate * (1.0 + gate * (1.0 - sigmoid_gate))
    up_grad = hidden_grad * gate * sigmoid_gate
    gateup_grad = jnp.concatenate([gate_grad.astype(LOW), up_grad.astype(LOW)], axis=1)

    second_grad = sum_shares(
        dot_turned(gateup_grad[half:], w_gateup).astype(LOW),
        dot_turned(gateup_grad[:half], w_gateup).astype(LOW),
    )
    scaled = second_grad * norm_gains[1]
    middle_grad = true_share(out_grad, 0) + second_scale * (
        scaled - second_unit * jnp.mean(scaled * second_unit, axis=-1, keepdims=True)
    )
    second_gain = jnp.sum(second_grad * second_unit, axis=0)

    sizes = [dp_count * n for _, n in plan.chunks]
    sums = [None] * len(sizes)
    sums = grad_blocks(
        hidden, mlp_grad, plan.of_matrix(3, hidden_blocks, row_blocks), 2, sums, sizes, block
    )
    sums = grad_blocks(
        second_in, gateup_grad, plan.of_matrix(2, row_blocks, 2 * hidden_blocks), 2, sums, sizes, block
    )
    reduced = [None] * len(sizes)

    def scatter(x):
        reduced[x] = lax.psum_scatter(
            sums[x], "dp", scatter_dimension=0, tiled=True, axis_index_groups=[plan.ring]
        )

    if len(sizes) > 2:
        scatter(2)

    feed_part = sum_shares(
        dot(hidden[half:], w_down).astype(LOW), dot(hidden[:half], w_down).astype(LOW)
    )
    out_parts = spread_share((middle + feed_part).astype(LOW))
    block_out = to_true(out_parts).reshape(sequences, length, model_width)

    attn_grad = jnp.concatenate(spread_share(middle_grad.astype(LOW)), axis=0)
    sums = grad_blocks(
        mixed_use, attn_grad, plan.of_matrix(1, out_attn_blocks, row_blocks), 4, sums, sizes, block
    )
    scatter(1)
    mixed_grad_parts = dot_turned(attn_grad, w_attn_out).astype(LOW)
    mixed_grad = to_true([mixed_grad_parts[i * share : (i + 1) * share] for i in range(4)]).reshape(
        sequences, length, kv_local, group_size, HD
    )
    query_grad, key_grad, value_grad = attend_backward(
        query_use[0], key_use[0], value_use[0], doc_ids[0], log_totals, mixed_grad[0], query_block
    )
    query_grad = rotate_back(query_grad[None], query_cos, query_sin).reshape(rows, query_cols)
    key_grad = rotate_back(key_grad[None], key_cos, key_sin).reshape(rows, key_cols)
    qkv_grad = jnp.concatenate(
        [query_grad, key_grad, value_grad.reshape(rows, key_cols)], axis=1
    ).astype(LOW)
    sums = grad_blocks(
        first_in,
        qkv_grad,
        plan.of_matrix(0, row_blocks, attn_blocks),
        attn_blocks,
        sums,
        sizes,
        block,
    )
    scatter(0)
    qkv_local = to_exchange(qkv_grad)
    first_grad = sum_shares(
        dot_turned(qkv_local[half:], w_qkv).astype(LOW),
        dot_turned(qkv_local[:half], w_qkv).astype(LOW),
    )
    scaled = first_grad * norm_gains[0]
    input_part = middle_grad + own_scale * (
        scaled - own_unit * jnp.mean(scaled * own_unit, axis=-1, keepdims=True)
    )
    input_parts = spread_share(input_part.astype(LOW))
    input_grad = to_true(input_parts).astype(F32).reshape(sequences, length, model_width)

    factor = float(rows * dp_count) ** (-0.5)
    gain_sums = jnp.stack([jnp.sum(first_grad * own_unit, axis=0), second_gain], axis=0)
    for bit in (1, 2):
        gain_sums = gain_sums + partner(gain_sums, bit)
    bit = 1
    while bit < dp_count:
        gain_sums = gain_sums + lax.ppermute(
            gain_sums, "dp", [(i, i ^ bit) for i in range(dp_count)]
        )
        bit *= 2
    gain_share = model_width // dp_count
    gain_grads = factor * lax.dynamic_slice_in_dim(gain_sums, d_index * gain_share, gain_share, 1)
    old_gains = lax.dynamic_slice_in_dim(norm_gains, d_index * gain_share, gain_share, 1)
    new_gains = old_gains - gain_rate * gain_grads

    state = None
    for x in reversed(range(len(sizes))):
        start, count = plan.chunks[x]
        state = shampoo(
            reduced[x],
            lax.slice_in_dim(order, start, start + count),
            factor,
            weight_blocks,
            ema_blocks,
            left_stats,
            right_stats,
            left_roots,
            right_roots,
            state,
        )
    grads, new_weights, new_ema, new_left, new_right = state
    return (
        block_out,
        input_grad,
        grads,
        new_weights,
        new_ema,
        new_left,
        new_right,
        gain_grads,
        new_gains,
    )


def solution(mesh):
    in_specs = (
        P("dp", None, None),
        P("dp", None, None),
        P("dp", None),
        P("dp", None),
        P(),
        P(("dp", "mp"), None, None),
        P(("dp", "mp"), None, None),
        P(("dp", "mp"), None, None),
        P(("dp", "mp"), None, None),
        P(("dp", "mp"), None, None),
        P(("dp", "mp"), None, None),
    )
    out_specs = (
        P("dp", None, None),
        P("dp", None, None),
        P(("dp", "mp"), None, None),
        P(("dp", "mp"), None, None),
        P(("dp", "mp"), None, None),
        P(("dp", "mp"), None, None),
        P(("dp", "mp"), None, None),
        P(None, "dp"),
        P(None, "dp"),
    )
    return jax.shard_map(
        on_device, mesh=mesh, in_specs=in_specs, out_specs=out_specs, check_vma=False
    )
```

```python
import functools

import jax
import jax.numpy as jnp
import numpy as np
from jax import lax
from jax.experimental import pallas as pl
from jax.experimental.pallas import tpu as pltpu
from jax.sharding import PartitionSpec as P

HEADS = 32
KV_HEADS = 4
HD = 64
FF = 5632
LOW = jnp.bfloat16
F32 = jnp.float32

weight_rate = 1.0
gain_rate = 0.2
average_decay = 0.9
VMEM_LIMIT = 60 * 1024 * 1024


def ring_order(count):
    return list(range(0, count, 2)) + list(range(1, count, 2))[::-1]


class Layout:
    def __init__(self, dp, own, rows, attn_cols, in_cols, out_attn_rows):
        self.dp, self.own = dp, own
        self.ring = ring_order(dp)
        n_in = rows * in_cols
        kinds, spots = [], []
        for k in range(dp * own):
            if k < n_in:
                r, c = divmod(k, in_cols)
                if c < attn_cols:
                    kinds.append(0), spots.append((0, r, c))
                else:
                    kinds.append(2), spots.append((2, r, c - attn_cols))
            else:
                r, c = divmod(k - n_in, rows)
                if r < out_attn_rows:
                    kinds.append(1), spots.append((1, r, c))
                else:
                    kinds.append(2), spots.append((3, r - out_attn_rows, c))
        self.order = np.zeros((dp, own), np.int32)
        for d in range(dp):
            mine = kinds[d * own : (d + 1) * own]
            self.order[d] = sorted(range(own), key=lambda l: (mine[l], l))
        count = np.array(kinds).reshape(dp, own)
        first = int((count == 0).sum(1).max())
        second = int((count <= 1).sum(1).max())
        bounds = [0, first, max(first, second), own]
        self.chunks = [(a, b - a) for a, b in zip(bounds[:-1], bounds[1:]) if b > a]
        self.table = []
        for p, d in enumerate(self.ring):
            for j, l in enumerate(self.order[d]):
                (x,) = [i for i, (a, n) in enumerate(self.chunks) if a <= j < a + n]
                a, n = self.chunks[x]
                self.table.append(spots[d * own + int(l)] + (x, p * n + j - a))

    def of_chunk(self, x, matrix):
        rows = [(s, r, c) for m, r, c, y, s in self.table if y == x and m == matrix]
        return np.array(sorted(rows), np.int32).reshape(-1, 3)

    def of_matrix(self, matrix, rows, cols):
        out = np.zeros((cols, rows, 2), np.int32)
        for m, r, c, x, s in self.table:
            if m == matrix:
                out[c, r] = (x, s)
        return out


ANY = pl.BlockSpec(memory_space=pl.ANY)
SMEM = pl.BlockSpec(memory_space=pltpu.SMEM)
VMEM = pl.BlockSpec(memory_space=pltpu.VMEM)


def sort_blocks(weights, order, chunks):
    block = weights.shape[1:]

    def body(order_ref, w_ref, *outs):
        for (start, count), out in zip(chunks, outs):

            def one(j, carry, start=start, out=out):
                out[j] = w_ref[order_ref[start + j]].astype(LOW)
                return carry

            lax.fori_loop(0, count, one, 0)

    return pl.pallas_call(
        body,
        out_shape=[jax.ShapeDtypeStruct((n,) + block, LOW) for _, n in chunks],
        in_specs=[SMEM, VMEM],
        out_specs=[VMEM] * len(chunks),
        compiler_params=pltpu.CompilerParams(vmem_limit_bytes=VMEM_LIMIT),
        name="sort_blocks",
    )(order, weights)


def place_blocks(gathered, tables, shapes, partial):
    block = gathered.shape[-1]
    used = [i for i, t in enumerate(tables) if len(t)]
    if not used:
        return partial
    count = sum(len(tables[i]) for i in used)
    known = [i for i in used if partial[i] is not None]

    def body(*refs):
        table_refs = refs[: len(used)]
        src = refs[len(used)]
        outs = refs[len(used) + 1 + len(known) : -3]
        stage, sem_in, sem_out = refs[-3:]
        at = 0
        for i, table_ref in zip(used, table_refs):

            def load(j, carry, table_ref=table_ref, at=at):
                pltpu.make_async_copy(src.at[table_ref[3 * j]], stage.at[at + j], sem_in).start()
                return carry

            lax.fori_loop(0, len(tables[i]), load, 0)
            at += len(tables[i])
        pltpu.make_async_copy(stage, stage, sem_in).wait()
        at = 0
        for i, table_ref, out in zip(used, table_refs, outs):

            def put(j, carry, table_ref=table_ref, out=out, at=at):
                row = pl.multiple_of(table_ref[3 * j + 1] * block, block)
                col = pl.multiple_of(table_ref[3 * j + 2] * block, block)
                pltpu.make_async_copy(
                    stage.at[at + j], out.at[pl.ds(row, block), pl.ds(col, block)], sem_out
                ).start()
                return carry

            lax.fori_loop(0, len(tables[i]), put, 0)
            at += len(tables[i])
        pltpu.make_async_copy(stage, stage, sem_out).wait()

    results = pl.pallas_call(
        body,
        out_shape=[jax.ShapeDtypeStruct(shapes[i], LOW) for i in used],
        in_specs=[SMEM] * len(used) + [ANY] * (1 + len(known)),
        out_specs=[ANY] * len(used),
        input_output_aliases={len(used) + 1 + j: used.index(i) for j, i in enumerate(known)},
        scratch_shapes=[
            pltpu.VMEM((count, block, block), LOW),
            pltpu.SemaphoreType.DMA,
            pltpu.SemaphoreType.DMA,
        ],
        compiler_params=pltpu.CompilerParams(vmem_limit_bytes=VMEM_LIMIT),
        cost_estimate=pl.CostEstimate(
            flops=0, bytes_accessed=4 * count * block * block, transcendentals=0
        ),
        name="place_blocks",
    )(
        *[jnp.asarray(tables[i].reshape(-1)) for i in used],
        gathered,
        *[partial[i] for i in known],
    )
    merged = list(partial)
    for i, value in zip(used, results):
        merged[i] = value
    return merged


def fill(scratch, pieces, order_ref):
    count = pieces[0].shape[0]
    for i, piece in enumerate(pieces):
        if order_ref is None:
            scratch[i * count : (i + 1) * count] = piece[...]
        else:
            scratch[pl.ds(pl.multiple_of(order_ref[i] * count, count), count)] = piece[...]


def grad_blocks(left, rights, order, pairs, table, wide, buffers, sizes, block):
    tokens, height = left.shape
    by_column = len(rights) > 1 and rights[0].shape[0] == tokens
    width = rights[0].shape[-1] * (2 if pairs else len(rights) if by_column else 1)
    rows, cols = height // block, width // block
    if pairs:
        table = np.stack([table[: cols // 2], table[cols // 2 :]], 1).reshape(table.shape)
        wide = 2
    steps = cols // wide
    assert not by_column or steps == 1
    per_step = rows * wide
    targets = table.reshape(steps, per_step, 2).tolist()
    used = sorted(set(table[:, :, 0].reshape(-1).tolist()))
    known = [x for x in used if buffers[x] is not None]
    n_order = 0 if order is None else 1
    joined = len(rights) > 1
    first_known = n_order + 1 + len(rights)
    first_out = first_known + len(known)

    def body(*refs):
        left_ref = refs[n_order]
        right_refs = refs[n_order + 1 : first_known]
        outs = refs[first_out : first_out + len(used)]
        stage, sems = refs[first_out + len(used) : first_out + len(used) + 2]
        t = pl.program_id(0)
        slot = lax.rem(t, 2)
        if joined:
            right_ref = refs[-1]
            if by_column:
                for i, piece in enumerate(right_refs):
                    right_ref[:, i * block : (i + 1) * block] = piece[...]
            else:
                fill(right_ref, right_refs, refs[0] if n_order else None)
            taken = right_ref[...]
        elif pairs:
            taken = jnp.concatenate([right_refs[0][0], right_refs[0][1]], axis=1)
        else:
            taken = right_refs[0][...]

        def finish(slot):
            pltpu.make_async_copy(stage.at[slot], stage.at[slot], sems.at[slot]).wait()

        @pl.when(t >= 2)
        def _():
            finish(slot)

        part = lax.dot_general(
            left_ref[...], taken, (((0,), (0,)), ((), ())), preferred_element_type=F32
        ).astype(LOW)
        for r in range(rows):
            for c in range(wide):
                stage[slot, c * rows + r] = part[
                    r * block : (r + 1) * block, c * block : (c + 1) * block
                ]
        for step in range(steps):

            @pl.when(t == step)
            def _(step=step):
                for j, (x, spot) in enumerate(targets[step]):
                    pltpu.make_async_copy(
                        stage.at[step % 2, j], outs[used.index(x)].at[spot], sems.at[step % 2]
                    ).start()

        @pl.when(t == steps - 1)
        def _():
            for step in range(max(0, steps - 2), steps):
                finish(step % 2)

    span = wide * block
    if pairs:
        right_specs = [pl.BlockSpec((2, tokens, block), lambda j: (0, 0, j))]
    elif by_column:
        right_specs = [pl.BlockSpec((tokens, block), lambda j: (0, 0))] * len(rights)
    else:
        right_specs = [pl.BlockSpec((x.shape[0], span), lambda j: (0, j)) for x in rights]
    results = pl.pallas_call(
        body,
        grid=(steps,),
        out_shape=[jax.ShapeDtypeStruct((sizes[x], block, block), LOW) for x in used],
        in_specs=[SMEM] * n_order
        + [pl.BlockSpec((tokens, height), lambda j: (0, 0))]
        + right_specs
        + [ANY] * len(known),
        out_specs=[ANY] * len(used),
        input_output_aliases={first_known + j: used.index(x) for j, x in enumerate(known)},
        scratch_shapes=[
            pltpu.VMEM((2, per_step, block, block), LOW),
            pltpu.SemaphoreType.DMA((2,)),
        ]
        + ([pltpu.VMEM((tokens, span), LOW)] if joined else []),
        compiler_params=pltpu.CompilerParams(vmem_limit_bytes=VMEM_LIMIT),
        cost_estimate=pl.CostEstimate(
            flops=4 * tokens * height * width,
            bytes_accessed=2 * (tokens * (height + width) + height * width),
            transcendentals=0,
        ),
        name="grad_blocks",
    )(*([] if order is None else [order]), left, *rights, *[buffers[x] for x in known])
    merged = list(buffers)
    for x, value in zip(used, results):
        merged[x] = value
    return merged


def feed_forward(pieces, weights, hidden_grad, block):
    share, width = pieces[0].shape
    rows = share * len(pieces)
    hidden = weights.shape[1] // 2
    steps = hidden // block

    def body(*refs):
        gate_w, up_w, grad_ref, hid_ref, out_ref, joined = refs[len(pieces) :]

        @pl.when(pl.program_id(0) == 0)
        def _():
            fill(joined, refs[: len(pieces)], None)

        both = jnp.dot(
            joined[...],
            jnp.concatenate([gate_w[...], up_w[...]], axis=1),
            preferred_element_type=F32,
        )
        gate, up = both[:, :block], both[:, block:]
        grad = grad_ref[...]
        sig = jax.nn.sigmoid(gate)
        act = gate * sig
        hid_ref[...] = (act * up).astype(LOW)
        out_ref[0] = (grad * up * sig * (1.0 + gate * (1.0 - sig))).astype(LOW)
        out_ref[1] = (grad * act).astype(LOW)

    return pl.pallas_call(
        body,
        grid=(steps,),
        in_specs=[pl.BlockSpec((share, width), lambda j: (0, 0))] * len(pieces)
        + [
            pl.BlockSpec((width, block), lambda j: (0, j)),
            pl.BlockSpec((width, block), lambda j: (0, steps + j)),
            pl.BlockSpec((rows, block), lambda j: (0, j)),
        ],
        out_specs=[
            pl.BlockSpec((rows, block), lambda j: (0, j)),
            pl.BlockSpec((2, rows, block), lambda j: (0, 0, j)),
            pl.BlockSpec((rows, width), lambda j: (0, 0)),
        ],
        out_shape=[
            jax.ShapeDtypeStruct((rows, hidden), LOW),
            jax.ShapeDtypeStruct((2, rows, hidden), LOW),
            jax.ShapeDtypeStruct((rows, width), LOW),
        ],
        compiler_params=pltpu.CompilerParams(vmem_limit_bytes=VMEM_LIMIT),
        cost_estimate=pl.CostEstimate(
            flops=4 * rows * width * hidden,
            bytes_accessed=2 * rows * width + 4 * width * hidden + 10 * rows * hidden,
            transcendentals=rows * hidden,
        ),
        name="feed_forward",
    )(*pieces, weights, weights, hidden_grad)


def project_rows(parts, weights, order, turned, tile):
    stacked = parts[0].ndim == 3
    rows = parts[0].shape[-2]
    half = rows // 2
    widths = [parts[0].shape[2]] * parts[0].shape[0] if stacked else [x.shape[1] for x in parts]
    starts = [sum(widths[:i]) for i in range(len(widths))]
    width = weights.shape[0] if turned else weights.shape[1]
    depth = sum(widths)
    share = rows // 4
    n_order = 0 if order is None else 1

    def body(*refs):
        part_refs = refs[n_order : n_order + len(parts)]
        w_ref, kept_ref, sent_ref = refs[n_order + len(parts) : n_order + len(parts) + 3]
        if n_order:
            joined = refs[-1]

            @pl.when(pl.program_id(0) == 0)
            def _():
                for i in range(4):
                    take = pl.ds(pl.multiple_of(refs[0][i] * share, share), share)
                    for part, at, size in zip(part_refs, starts, widths):
                        joined[i * share : (i + 1) * share, at : at + size] = part[take]

            pieces = [(joined[...], 0, depth)]
        elif stacked:
            pieces = [(part_refs[0][i], at, widths[i]) for i, at in enumerate(starts)]
        else:
            pieces = [(p[...], at, size) for p, at, size in zip(part_refs, starts, widths)]
        total = None
        for value, at, size in pieces:
            if turned:
                one = dot_turned(value, w_ref[:, at : at + size])
            else:
                one = dot(value, w_ref[at : at + size])
            total = one if total is None else total + one
        total = total.astype(LOW)
        kept_ref[...] = total[:half]
        sent_ref[...] = total[half:]

    whole = [pl.BlockSpec(x.shape, lambda j, n=x.ndim: (0,) * n) for x in parts]
    if turned:
        weight_spec = pl.BlockSpec((tile, depth), lambda j: (j, 0))
    else:
        weight_spec = pl.BlockSpec((depth, tile), lambda j: (0, j))
    kept, sent = pl.pallas_call(
        body,
        grid=(width // tile,),
        in_specs=[SMEM] * n_order + whole + [weight_spec],
        out_specs=[pl.BlockSpec((half, tile), lambda j: (0, j))] * 2,
        out_shape=[jax.ShapeDtypeStruct((half, width), LOW)] * 2,
        scratch_shapes=[pltpu.VMEM((rows, depth), LOW)] * n_order,
        compiler_params=pltpu.CompilerParams(vmem_limit_bytes=VMEM_LIMIT),
        cost_estimate=pl.CostEstimate(
            flops=2 * rows * depth * width,
            bytes_accessed=2 * (rows * depth + depth * width + rows * width),
            transcendentals=0,
        ),
        name="project_rows",
    )(*([order] if n_order else []), *parts, weights)
    return sent, kept


def to_heads(pieces, weights, order):
    share = pieces[0].shape[0]
    width = weights.shape[0]

    def body(order_ref, *refs):
        w_ref, out_ref = refs[-2:]
        for i, piece in enumerate(refs[:-2]):
            put = pl.ds(pl.multiple_of(order_ref[i] * share, share), share)
            out_ref[put] = dot_turned(piece[...], w_ref[...]).astype(LOW)

    rows = share * len(pieces)
    return pl.pallas_call(
        body,
        in_specs=[SMEM] + [VMEM] * (len(pieces) + 1),
        out_specs=VMEM,
        out_shape=jax.ShapeDtypeStruct((rows, width), LOW),
        compiler_params=pltpu.CompilerParams(vmem_limit_bytes=VMEM_LIMIT),
        cost_estimate=pl.CostEstimate(
            flops=2 * rows * width * weights.shape[1],
            bytes_accessed=2 * (rows + width) * weights.shape[1],
            transcendentals=0,
        ),
        name="to_heads",
    )(order, *pieces, weights)


LANES = 128
QUERIES = 256
LONGEST = 512


def turn(values, cos, sin):
    lane = lax.broadcasted_iota(jnp.int32, values.shape, 1)
    other = jnp.where(
        lane % HD < HD // 2,
        pltpu.roll(values, LANES - HD // 2, 1),
        pltpu.roll(values, HD // 2, 1),
    )
    return values * cos + other * sin


def key_tables(cos, sin):
    lane = lax.broadcasted_iota(jnp.int32, cos.shape, 1)
    return jnp.where(lane < HD, cos, 1.0), jnp.where(lane < HD, sin, 0.0)


def project_heads(inputs, weights, cos, sin):
    rows, depth = inputs.shape
    width = weights.shape[1]
    assert width % LANES == 0 and HD == 64

    def body(x_ref, w_ref, cos_ref, sin_ref, q_ref, kv_ref):
        for at in range(0, width, LANES):
            raw = dot(x_ref[...], w_ref[:, at : at + LANES])
            if at < width - LANES:
                q_ref[:, at : at + LANES] = (
                    turn(raw, cos_ref[...], sin_ref[...]).astype(LOW) * LOW(HD**-0.5)
                )
            else:
                kv_ref[...] = turn(raw, *key_tables(cos_ref[...], sin_ref[...])).astype(LOW)

    return pl.pallas_call(
        body,
        in_specs=[VMEM] * 4,
        out_specs=[VMEM] * 2,
        out_shape=[
            jax.ShapeDtypeStruct((rows, width - LANES), LOW),
            jax.ShapeDtypeStruct((rows, LANES), LOW),
        ],
        compiler_params=pltpu.CompilerParams(vmem_limit_bytes=VMEM_LIMIT),
        cost_estimate=pl.CostEstimate(
            flops=2 * rows * depth * width,
            bytes_accessed=2 * (rows * depth + depth * width + rows * width),
            transcendentals=0,
        ),
        name="project_heads",
    )(inputs, weights, cos, sin)


def key_range(at):
    low = max(0, (at - LONGEST + 1) // QUERIES * QUERIES)
    return low, at + QUERIES


def visible(start_ref, at, low, high):
    shape = (high - low, QUERIES)
    key = low + lax.broadcasted_iota(jnp.int32, shape, 0)
    query = at + lax.broadcasted_iota(jnp.int32, shape, 1)
    return (key >= start_ref[:, at : at + QUERIES]) & (key <= query)


def attend(queries, kv, starts):
    rows, width = queries.shape
    groups = width // LANES

    def body(start_ref, q_ref, kv_ref, o_ref, log_ref):
        for at in range(0, rows, QUERIES):
            low, high = key_range(at)
            seen = visible(start_ref, at, low, high)
            keys = kv_ref[low:high, :HD]
            values = kv_ref[low:high, HD:]
            for h in range(LANES // HD):
                query = q_ref[at : at + QUERIES, h * HD : (h + 1) * HD]
                scores = jnp.where(seen, dot_turned(keys, query), -1e30)
                top = jnp.max(scores, axis=0, keepdims=True)
                expo = jnp.exp(scores - top)
                total = jnp.sum(expo, axis=0, keepdims=True)
                probs = (expo * (1.0 / total)).astype(LOW)
                o_ref[at : at + QUERIES, h * HD : (h + 1) * HD] = lax.dot_general(
                    probs, values, (((0,), (0,)), ((), ())), preferred_element_type=F32
                ).astype(LOW)
                log_ref[0, h : h + 1, at : at + QUERIES] = top + jnp.log(total)

    column = pl.BlockSpec((rows, LANES), lambda j: (0, j))
    return pl.pallas_call(
        body,
        grid=(groups,),
        in_specs=[
            pl.BlockSpec((1, rows), lambda j: (0, 0)),
            column,
            pl.BlockSpec((rows, LANES), lambda j: (0, 0)),
        ],
        out_specs=[column, pl.BlockSpec((1, LANES // HD, rows), lambda j: (j, 0, 0))],
        out_shape=[
            jax.ShapeDtypeStruct((rows, width), LOW),
            jax.ShapeDtypeStruct((groups, LANES // HD, rows), F32),
        ],
        compiler_params=pltpu.CompilerParams(vmem_limit_bytes=VMEM_LIMIT),
        cost_estimate=pl.CostEstimate(
            flops=30 * rows * rows * width,
            bytes_accessed=4 * rows * width,
            transcendentals=rows * rows * width // HD,
        ),
        name="attend",
    )(starts, queries, kv)


def attend_back(group, queries, kv, starts, logs, grads, cos, sin, before, last):
    rows, _ = queries.shape
    first = before is None

    def body(start_ref, q_ref, kv_ref, log_ref, g_ref, cos_ref, sin_ref, *rest):
        before_ref = None if first else rest[0]
        dq_ref, sum_ref, acc = rest[-3:]
        acc[...] = jnp.zeros_like(acc) if first else before_ref[...]
        for at in range(0, rows, QUERIES):
            low, high = key_range(at)
            seen = visible(start_ref, at, low, high)
            keys = kv_ref[low:high, :HD]
            values = kv_ref[low:high, HD:]
            parts = []
            key_part, value_part = 0.0, 0.0
            for h in range(LANES // HD):
                query = q_ref[at : at + QUERIES, h * HD : (h + 1) * HD]
                grad = g_ref[at : at + QUERIES, h * HD : (h + 1) * HD]
                scores = jnp.where(seen, dot_turned(keys, query), -1e30)
                probs = jnp.exp(scores - log_ref[0, h : h + 1, at : at + QUERIES])
                value_part += dot(probs.astype(LOW), grad)
                prob_grads = dot_turned(values, grad)
                inner = jnp.sum(probs * prob_grads, axis=0, keepdims=True)
                score_grads = (probs * (prob_grads - inner)).astype(LOW)
                key_part += dot(score_grads, query)
                parts.append(
                    lax.dot_general(
                        score_grads, keys, (((0,), (0,)), ((), ())), preferred_element_type=F32
                    )
                )
            acc[low:high] += jnp.concatenate([key_part, value_part], axis=1)
            span = slice(at, at + QUERIES)
            dq_ref[span] = turn(
                jnp.concatenate(parts, axis=1) * HD**-0.5, cos_ref[span], -sin_ref[span]
            ).astype(LOW)
        if last:
            key_cos, key_sin = key_tables(cos_ref[...], sin_ref[...])
            sum_ref[...] = turn(acc[...], key_cos, -key_sin).astype(LOW)
        else:
            sum_ref[...] = acc[...]

    column = pl.BlockSpec((rows, LANES), lambda j: (0, group))
    whole = pl.BlockSpec((rows, LANES), lambda j: (0, 0))
    return pl.pallas_call(
        body,
        grid=(1,),
        in_specs=[
            pl.BlockSpec((1, rows), lambda j: (0, 0)),
            column,
            whole,
            pl.BlockSpec((1, LANES // HD, rows), lambda j: (group, 0, 0)),
            column,
            whole,
            whole,
        ]
        + ([] if first else [whole]),
        out_specs=[whole] * 2,
        out_shape=[
            jax.ShapeDtypeStruct((rows, LANES), LOW),
            jax.ShapeDtypeStruct((rows, LANES), LOW if last else F32),
        ],
        scratch_shapes=[pltpu.VMEM((rows, LANES), F32)],
        compiler_params=pltpu.CompilerParams(vmem_limit_bytes=VMEM_LIMIT),
        cost_estimate=pl.CostEstimate(
            flops=80 * rows * rows * LANES,
            bytes_accessed=16 * rows * LANES,
            transcendentals=rows * rows * LANES // HD,
        ),
        name="attend_back",
    )(starts, queries, kv, logs, grads, cos, sin, *([] if first else [before]))


def shampoo(sums, places, factor, weights, ema, left, right, left_roots, right_roots, before):
    count, block, _ = sums.shape
    group = 2 if count % 2 == 0 else 1
    steps = count // group
    depth = min(4, steps)
    extra = [] if before is None else list(before)

    def mm(a, b, dims):
        return lax.dot_general(
            a.astype(LOW), b.astype(LOW), (dims, ((), ())), preferred_element_type=F32
        )

    def body(places_ref, g_ref, *refs):
        ins, outs = refs[:6], refs[6 + len(extra) : 11 + len(extra)]
        given, made, sem_in, sem_out = refs[11 + len(extra) :]

        def load(t, slot):
            for u in range(group):
                place = places_ref[t * group + u]
                for i, ref in enumerate(ins):
                    pltpu.make_async_copy(
                        ref.at[place], given.at[slot, u, i], sem_in.at[slot]
                    ).start()

        def wait(buffer, slot, sems):
            pltpu.make_async_copy(buffer.at[slot], buffer.at[slot], sems.at[slot]).wait()

        for t in range(depth):
            load(t, t)

        def step(t, carry):
            slot = lax.rem(t, depth)
            wait(given, slot, sem_in)

            @pl.when(t >= depth)
            def _():
                wait(made, slot, sem_out)

            both = 0.5 * factor * factor
            for u in range(group):
                low = g_ref[t * group + u]
                made[slot, u, 0] = low.astype(F32) * factor
                made[slot, u, 3] = 0.5 * given[slot, u, 2] + both * mm(low, low, ((1,), (1,)))
                made[slot, u, 4] = 0.5 * given[slot, u, 3] + both * mm(low, low, ((0,), (0,)))
                part = mm(low, given[slot, u, 5], ((1,), (0,))) * factor
                fresh = given[slot, u, 0] - weight_rate * mm(given[slot, u, 4], part, ((1,), (0,)))
                made[slot, u, 1] = fresh
                made[slot, u, 2] = (
                    average_decay * given[slot, u, 1] + (1.0 - average_decay) * fresh
                )
            for u in range(group):
                place = places_ref[t * group + u]
                for i, ref in enumerate(outs):
                    pltpu.make_async_copy(
                        made.at[slot, u, i], ref.at[place], sem_out.at[slot]
                    ).start()

            @pl.when(t + depth < steps)
            def _():
                load(t + depth, slot)

            return carry

        lax.fori_loop(0, steps, step, 0)
        for t in range(steps - depth, steps):
            wait(made, t % depth, sem_out)

    return pl.pallas_call(
        body,
        out_shape=[jax.ShapeDtypeStruct(weights.shape, F32)] * 5,
        in_specs=[SMEM, VMEM] + [ANY] * (6 + len(extra)),
        out_specs=[ANY] * 5,
        input_output_aliases={8 + i: i for i in range(len(extra))},
        scratch_shapes=[
            pltpu.VMEM((depth, group, 6, block, block), F32),
            pltpu.VMEM((depth, group, 5, block, block), F32),
            pltpu.SemaphoreType.DMA((depth,)),
            pltpu.SemaphoreType.DMA((depth,)),
        ],
        compiler_params=pltpu.CompilerParams(vmem_limit_bytes=VMEM_LIMIT),
        cost_estimate=pl.CostEstimate(
            flops=8 * count * block**3,
            bytes_accessed=46 * count * block * block,
            transcendentals=0,
        ),
        name="shampoo",
    )(places, sums, weights, ema, left, right, left_roots, right_roots, *extra)


def rows_call(body, ins, outs, name, step=64):
    rows = max(x.shape[0] for x in ins)

    def spec(x):
        if x.shape[0] == rows:
            return pl.BlockSpec((step, x.shape[1]), lambda j: (j, 0))
        return pl.BlockSpec(x.shape, lambda j: (0, 0))

    return pl.pallas_call(
        body,
        grid=(rows // step,),
        in_specs=[spec(x) for x in ins],
        out_specs=[spec(x) for x in outs],
        out_shape=outs,
        compiler_params=pltpu.CompilerParams(vmem_limit_bytes=VMEM_LIMIT),
        cost_estimate=pl.CostEstimate(
            flops=10 * rows * ins[0].shape[1],
            bytes_accessed=sum(x.size * x.dtype.itemsize for x in list(ins) + list(outs)),
            transcendentals=0,
        ),
        name=name,
    )(*ins)


def add_near(kept, got):
    share = kept.shape[0] // 2
    width = kept.shape[1]
    step = 64

    def body(a_ref, c_ref, b_ref, d_ref, mine_ref, other_ref):
        mine_ref[...] = a_ref[...].astype(F32) + b_ref[...].astype(F32)
        other_ref[...] = (c_ref[...].astype(F32) + d_ref[...].astype(F32)).astype(LOW)

    first = pl.BlockSpec((step, width), lambda j: (j, 0))
    second = pl.BlockSpec((step, width), lambda j: (share // step + j, 0))
    return pl.pallas_call(
        body,
        grid=(share // step,),
        in_specs=[first, second, first, second],
        out_specs=[first] * 2,
        out_shape=[
            jax.ShapeDtypeStruct((share, width), F32),
            jax.ShapeDtypeStruct((share, width), LOW),
        ],
        compiler_params=pltpu.CompilerParams(vmem_limit_bytes=VMEM_LIMIT),
        cost_estimate=pl.CostEstimate(
            flops=2 * share * width, bytes_accessed=14 * share * width, transcendentals=0
        ),
        name="add_near",
    )(kept, kept, got, got)


def second_norm(tokens, mine, got, gain):
    def body(x_ref, a_ref, b_ref, gain_ref, middle_ref, low_ref):
        middle = x_ref[...].astype(F32) + (a_ref[...] + b_ref[...].astype(F32))
        middle_ref[...] = middle
        scale = lax.rsqrt(jnp.mean(middle * middle, axis=-1, keepdims=True) + 1e-05)
        low_ref[...] = (middle * scale * gain_ref[...]).astype(LOW)

    return rows_call(
        body,
        [tokens, mine, got, gain],
        [jax.ShapeDtypeStruct(tokens.shape, F32), jax.ShapeDtypeStruct(tokens.shape, LOW)],
        "second_norm",
    )


def norm_back(values, mine, got, gain, residual):
    def body(x_ref, a_ref, b_ref, gain_ref, r_ref, out_ref, low_ref, sum_ref):
        x = x_ref[...].astype(F32)
        grad = a_ref[...] + b_ref[...].astype(F32)
        scale = lax.rsqrt(jnp.mean(x * x, axis=-1, keepdims=True) + 1e-05)
        unit = x * scale
        scaled = grad * gain_ref[...]
        out = r_ref[...].astype(F32) + scale * (
            scaled - unit * jnp.mean(scaled * unit, axis=-1, keepdims=True)
        )
        out_ref[...] = out
        low_ref[...] = out.astype(LOW)

        @pl.when(pl.program_id(0) == 0)
        def _():
            sum_ref[...] = jnp.zeros_like(sum_ref)

        sum_ref[...] += jnp.sum(grad * unit, axis=0, keepdims=True)

    shape = values.shape
    return rows_call(
        body,
        [values, mine, got, gain, residual],
        [
            jax.ShapeDtypeStruct(shape, F32),
            jax.ShapeDtypeStruct(shape, LOW),
            jax.ShapeDtypeStruct((1, shape[1]), F32),
        ],
        "norm_back",
    )


def doc_positions(doc_ids):
    length = doc_ids.shape[-1]
    offsets = jnp.arange(length, dtype=jnp.int32)
    starts = jnp.concatenate(
        [jnp.ones(doc_ids.shape[:-1] + (1,), jnp.bool_), doc_ids[..., 1:] != doc_ids[..., :-1]],
        axis=-1,
    )
    first_index = lax.cummax(jnp.where(starts, offsets, 0), axis=doc_ids.ndim - 1)
    return offsets - first_index


def rope_tables(positions, head_size):
    half_size = head_size // 2
    exponent = jnp.arange(half_size, dtype=F32) * (2.0 / head_size)
    inverse = jnp.power(F32(10000.0), -exponent)
    angles = positions.astype(F32)[..., None] * inverse
    cos, sin = jnp.cos(angles), jnp.sin(angles)
    repeats = LANES // head_size
    return (
        jnp.concatenate([cos, cos] * repeats, axis=-1),
        jnp.concatenate([-sin, sin] * repeats, axis=-1),
    )


def after(value, *others):
    return lax.optimization_barrier((value,) + others)[0]


def dot(left, right):
    return jnp.dot(left, right, preferred_element_type=F32)


def dot_turned(left, right):
    return lax.dot_general(left, right, (((1,), (1,)), ((), ())), preferred_element_type=F32)


EXCHANGE = (0, 2, 1, 3)


def on_device(
    tokens_in,
    cotangent,
    select_mask,
    doc_ids,
    norm_gains,
    weight_blocks,
    ema_blocks,
    left_stats,
    right_stats,
    left_roots,
    right_roots,
):
    mp_count = lax.axis_size("mp")
    dp_count = lax.axis_size("dp")
    sequences, length, model_width = tokens_in.shape
    assert sequences == 1 and mp_count == 4 and dp_count & (dp_count - 1) == 0
    rows = sequences * length
    own, block, _ = weight_blocks.shape
    query_cols = HEADS * HD // mp_count
    key_cols = KV_HEADS * HD // mp_count
    hidden_cols = FF // mp_count
    assert KV_HEADS == mp_count and length % QUERIES == 0
    row_blocks = model_width // block
    attn_blocks = (query_cols + 2 * key_cols) // block
    hidden_blocks = hidden_cols // block
    in_blocks = attn_blocks + 2 * hidden_blocks
    out_attn_blocks = query_cols // block
    share = rows // mp_count
    m_index = lax.axis_index("mp")
    d_index = lax.axis_index("dp")

    plan = Layout(dp_count, own, row_blocks, attn_blocks, in_blocks, out_attn_blocks)
    order = lax.dynamic_slice_in_dim(jnp.asarray(plan.order), d_index, 1, 0).reshape(-1)
    shapes = [
        (model_width, attn_blocks * block),
        (query_cols, model_width),
        (model_width, 2 * hidden_cols),
        (hidden_cols, model_width),
    ]

    def partner(values, bit):
        return lax.ppermute(values, "mp", [(i, i ^ bit) for i in range(mp_count)])

    def true_share(values, group):
        return lax.dynamic_slice_in_dim(values, (m_index ^ group) * share, share, 0)

    def to_exchange(values):
        return jnp.concatenate([true_share(values, g) for g in EXCHANGE], axis=0)

    def to_true(parts):
        by_group = [parts[EXCHANGE.index(g)] for g in range(4)]
        low, high = m_index & 1, m_index & 2
        pairs = []
        for a, b in ((0, 1), (2, 3)):
            pairs.append(
                (
                    jnp.where(low == 0, by_group[a], by_group[b]),
                    jnp.where(low == 0, by_group[b], by_group[a]),
                )
            )
        flat = []
        for first, second in ((0, 1), (1, 0)):
            for i in range(2):
                flat.append(jnp.where(high == 0, pairs[first][i], pairs[second][i]))
        return jnp.concatenate(flat, axis=0)

    def near_sum(sent, kept):
        return add_near(kept, partner(sent, 1))

    def spread_share(mine, *cover):
        far = partner(mine, 2)
        near = partner(mine, 1)
        if cover:
            far = after(far, *cover)
        return [mine, far, near, partner(far, 1)]

    sorted_low = sort_blocks(weight_blocks, order, plan.chunks)
    gathered = [
        lax.all_gather(chunk, "dp", axis=0, tiled=True, axis_index_groups=[plan.ring])
        for chunk in sorted_low
    ]
    none = np.zeros((0, 3), np.int32)
    last = len(gathered) - 1

    def place(x, source, which, matrices):
        tables = [plan.of_chunk(x, i) if i in which else none for i in range(4)]
        return place_blocks(source, tables, shapes, matrices)

    matrices = place(0, gathered[0], (0, 1, 2, 3), [None] * 4)
    w_qkv = matrices[0]
    if last >= 1:
        matrices = place(1, gathered[1], (1,), matrices)
    w_attn_out = matrices[1]

    positions = doc_positions(doc_ids)
    starts = jnp.arange(length, dtype=jnp.int32)[None] - positions
    cos, sin = rope_tables(positions[0], HD)

    tokens_low = tokens_in.reshape(rows, model_width)
    tokens = tokens_low.astype(F32)
    first_scale = lax.rsqrt(jnp.mean(tokens * tokens, axis=-1, keepdims=True) + 1e-05)
    first_in = (tokens * first_scale * norm_gains[0]).astype(LOW)
    out_grad = cotangent.reshape(rows, model_width) * select_mask.astype(LOW).reshape(rows, 1)
    own_tokens = true_share(tokens_low, 0)
    own_grad = true_share(out_grad, 0)
    mlp_grad = to_exchange(out_grad)

    shares = (m_index ^ jnp.array(EXCHANGE, jnp.int32)).astype(jnp.int32)
    queries, kv = project_heads(first_in, w_qkv, cos, sin)
    kv, mlp_grad, own_tokens, own_grad = lax.optimization_barrier(
        (kv, mlp_grad, own_tokens, own_grad)
    )
    mixed, logs = attend(queries, kv, starts)
    attended_sent, attended_kept = project_rows([mixed], w_attn_out, shares, False, 512)
    mine, other = near_sum(attended_sent, attended_kept)
    if last >= 1:
        matrices = place(1, after(gathered[1], other), (2, 3), matrices)
        mine, *matrices[2:] = lax.optimization_barrier((mine, *matrices[2:]))
    middle, second_low = second_norm(own_tokens, mine, partner(other, 2), norm_gains[1:])
    if last >= 2:
        matrices = place(2, after(gathered[2], second_low), (2, 3), matrices)
    w_gateup, w_down = matrices[2:]
    hidden_grad = dot_turned(mlp_grad, w_down)
    second_pieces = spread_share(second_low, hidden_grad)
    hidden, gateup_grad, second_in = feed_forward(second_pieces, w_gateup, hidden_grad, block)

    second_sent, second_kept = project_rows([gateup_grad], w_gateup, None, True, 256)
    sizes = [dp_count * n for _, n in plan.chunks]
    sums = [None] * len(sizes)
    sums = grad_blocks(
        after(hidden, second_sent),
        [mlp_grad],
        None,
        False,
        plan.of_matrix(3, hidden_blocks, row_blocks),
        2,
        sums,
        sizes,
        block,
    )
    mine, other = near_sum(second_sent, after(second_kept, *[x for x in sums if x is not None]))
    second_in = after(second_in, other)
    got = partner(other, 2)
    sums = grad_blocks(
        second_in,
        [gateup_grad],
        None,
        True,
        plan.of_matrix(2, row_blocks, 2 * hidden_blocks),
        2,
        sums,
        sizes,
        block,
    )
    reduced = [None] * len(sizes)

    def scatter(x):
        reduced[x] = lax.psum_scatter(
            sums[x], "dp", scatter_dimension=0, tiled=True, axis_index_groups=[plan.ring]
        )

    if last >= 2:
        scatter(2)

    mine = after(mine, *[x for x in sums if x is not None])
    middle_grad, attn_low, second_gain = norm_back(
        middle, mine, got, norm_gains[1:], own_grad
    )
    feed_sent, feed_kept = project_rows([after(hidden, attn_low)], w_down, None, False, 512)
    attn_grad = spread_share(attn_low, feed_kept)
    sums = grad_blocks(
        mixed,
        attn_grad,
        shares,
        False,
        plan.of_matrix(1, out_attn_blocks, row_blocks),
        4,
        sums,
        sizes,
        block,
    )
    if last >= 1:
        scatter(1)

    mixed_grad = to_heads(attn_grad, after(w_attn_out, *[x for x in sums if x is not None]), shares)

    feed_mine, feed_other = near_sum(feed_sent, after(feed_kept, mixed_grad))
    groups = query_cols // LANES
    query_grads, kv_grad = [], None
    feed_step = feed_other
    for group in range(groups):
        pair_grad, kv_grad = attend_back(
            group,
            queries,
            kv,
            starts,
            logs,
            after(mixed_grad, feed_step),
            cos,
            sin,
            kv_grad,
            group == groups - 1,
        )
        query_grads.append(pair_grad)
        if group == groups - 3:
            feed_part = after(feed_mine, pair_grad) + partner(feed_other, 2).astype(F32)
            feed_step = out_low = (middle + feed_part).astype(LOW)
    out_parts = spread_share(out_low)
    qkv_grads = query_grads + [kv_grad]
    sums = grad_blocks(
        first_in,
        qkv_grads,
        None,
        False,
        plan.of_matrix(0, row_blocks, attn_blocks),
        attn_blocks,
        sums,
        sizes,
        block,
    )
    scatter(0)
    first_sent, first_kept = project_rows(
        [after(qkv_grads[0], sums[0])] + qkv_grads[1:], w_qkv, shares, True, 512
    )
    mine, other = near_sum(first_sent, first_kept)
    factor = float(rows * dp_count) ** (-0.5)

    def update(x, state, *others):
        start, count = plan.chunks[x]
        return shampoo(
            reduced[x],
            after(lax.slice_in_dim(order, start, start + count), *others),
            factor,
            weight_blocks,
            ema_blocks,
            left_stats,
            right_stats,
            left_roots,
            right_roots,
            state,
        )

    state = None
    if last >= 2:
        state = update(2, state, other)
        mine = after(mine, *state)
    _, input_low, first_gain = norm_back(
        own_tokens, mine, partner(other, 2), norm_gains[:1], middle_grad
    )
    gain_sums = jnp.concatenate([first_gain, second_gain], axis=0)
    gain_sums = gain_sums + partner(gain_sums, 2)
    input_low = after(input_low, gain_sums)
    if last >= 1:
        state = update(1, state, other)
        input_low = after(input_low, *state)
    input_parts = spread_share(input_low)
    gain_sums = gain_sums + partner(gain_sums, 1)
    bit = 1
    while bit < dp_count:
        gain_sums = gain_sums + lax.ppermute(
            gain_sums, "dp", [(i, i ^ bit) for i in range(dp_count)]
        )
        bit *= 2
    gain_share = model_width // dp_count
    gain_grads = factor * lax.dynamic_slice_in_dim(gain_sums, d_index * gain_share, gain_share, 1)
    old_gains = lax.dynamic_slice_in_dim(norm_gains, d_index * gain_share, gain_share, 1)
    new_gains = old_gains - gain_rate * gain_grads
    block_out = to_true(out_parts).reshape(sequences, length, model_width)
    input_grad = to_true(input_parts).astype(F32).reshape(sequences, length, model_width)
    grads, new_weights, new_ema, new_left, new_right = update(
        0, state, block_out, input_grad, new_gains
    )
    return (
        block_out,
        input_grad,
        grads,
        new_weights,
        new_ema,
        new_left,
        new_right,
        gain_grads,
        new_gains,
    )


def solution(mesh):
    in_specs = (
        P("dp", None, None),
        P("dp", None, None),
        P("dp", None),
        P("dp", None),
        P(),
        P(("dp", "mp"), None, None),
        P(("dp", "mp"), None, None),
        P(("dp", "mp"), None, None),
        P(("dp", "mp"), None, None),
        P(("dp", "mp"), None, None),
        P(("dp", "mp"), None, None),
    )
    out_specs = (
        P("dp", None, None),
        P("dp", None, None),
        P(("dp", "mp"), None, None),
        P(("dp", "mp"), None, None),
        P(("dp", "mp"), None, None),
        P(("dp", "mp"), None, None),
        P(("dp", "mp"), None, None),
        P(None, "dp"),
        P(None, "dp"),
    )
    return jax.shard_map(
        on_device, mesh=mesh, in_specs=in_specs, out_specs=out_specs, check_vma=False
    )
```

```python
import functools

import jax
import jax.numpy as jnp
import numpy as np
from jax import lax
from jax.experimental import pallas as pl
from jax.experimental.pallas import tpu as pltpu
from jax.sharding import PartitionSpec as P

HEADS = 32
KV_HEADS = 4
HD = 64
FF = 5632
LOW = jnp.bfloat16
F32 = jnp.float32

weight_rate = 1.0
gain_rate = 0.2
average_decay = 0.9
VMEM_LIMIT = 60 * 1024 * 1024


def ring_order(count):
    return list(range(0, count, 2)) + list(range(1, count, 2))[::-1]


class Layout:
    def __init__(self, dp, own, rows, attn_cols, in_cols, out_attn_rows):
        self.dp, self.own = dp, own
        self.ring = ring_order(dp)
        n_in = rows * in_cols
        units = (in_cols - attn_cols) // 2
        kinds, spots, keys = [], [], []
        for k in range(dp * own):
            if k < n_in:
                r, c = divmod(k, in_cols)
                if c < attn_cols:
                    kinds.append(0), spots.append((0, r, c)), keys.append((0, k))
                else:
                    c -= attn_cols
                    kinds.append(2), spots.append((2, r, c)), keys.append((2, c % units / units, k))
            else:
                r, c = divmod(k - n_in, rows)
                if r < out_attn_rows:
                    kinds.append(1), spots.append((1, r, c)), keys.append((1, k))
                else:
                    kinds.append(2), spots.append((3, r - out_attn_rows, c))
                    keys.append((2, c / rows, k))
        self.order = np.zeros((dp, own), np.int32)
        for d in range(dp):
            self.order[d] = sorted(range(own), key=lambda l: keys[d * own + l])
        count = np.array(kinds).reshape(dp, own)
        first = int((count == 0).sum(1).max())
        second = int((count <= 1).sum(1).max())
        bounds = [0, first, max(first, second), own]
        self.chunks = [(a, b - a) for a, b in zip(bounds[:-1], bounds[1:]) if b > a]
        self.table = []
        for p, d in enumerate(self.ring):
            for j, l in enumerate(self.order[d]):
                (x,) = [i for i, (a, n) in enumerate(self.chunks) if a <= j < a + n]
                a, n = self.chunks[x]
                self.table.append(spots[d * own + int(l)] + (x, p * n + j - a))
        mixed = [p for p, d in enumerate(self.ring) if (count[d] == 1).any()]
        last, size = len(self.chunks) - 1, self.chunks[-1][1]
        late = [t for t in self.table if t[3] == last]
        self.first_late = {}
        for m, cols in ((2, units), (3, rows)):
            own_late = [c % cols for i, r, c, x, s in late if i == m and s // size not in mixed]
            self.first_late[m] = min(own_late, default=cols)
        self.strips = sorted(
            (m, r, c, s)
            for m, r, c, x, s in late
            if m >= 2 and s // size in mixed and c % (units if m == 2 else rows) < self.first_late[m]
        )

    def of_chunk(self, x, matrix):
        rows = [(s, r, c) for m, r, c, y, s in self.table if y == x and m == matrix]
        return np.array(sorted(rows), np.int32).reshape(-1, 3)

    def of_matrix(self, matrix, rows, cols):
        out = np.zeros((cols, rows, 2), np.int32)
        for m, r, c, x, s in self.table:
            if m == matrix:
                out[c, r] = (x, s)
        return out


ANY = pl.BlockSpec(memory_space=pl.ANY)
SMEM = pl.BlockSpec(memory_space=pltpu.SMEM)
VMEM = pl.BlockSpec(memory_space=pltpu.VMEM)


def sort_blocks(weights, order, chunks):
    block = weights.shape[1:]

    def body(order_ref, w_ref, *outs):
        for (start, count), out in zip(chunks, outs):

            def one(j, carry, start=start, out=out):
                out[j] = w_ref[order_ref[start + j]].astype(LOW)
                return carry

            lax.fori_loop(0, count, one, 0)

    return pl.pallas_call(
        body,
        out_shape=[jax.ShapeDtypeStruct((n,) + block, LOW) for _, n in chunks],
        in_specs=[SMEM, VMEM],
        out_specs=[VMEM] * len(chunks),
        compiler_params=pltpu.CompilerParams(vmem_limit_bytes=VMEM_LIMIT),
        name="sort_blocks",
    )(order, weights)


def place_blocks(gathered, tables, shapes, partial):
    block = gathered.shape[-1]
    used = [i for i, t in enumerate(tables) if len(t)]
    if not used:
        return partial
    count = sum(len(tables[i]) for i in used)
    known = [i for i in used if partial[i] is not None]

    def body(*refs):
        table_refs = refs[: len(used)]
        src = refs[len(used)]
        outs = refs[len(used) + 1 + len(known) : -3]
        stage, sem_in, sem_out = refs[-3:]
        at = 0
        for i, table_ref in zip(used, table_refs):

            def load(j, carry, table_ref=table_ref, at=at):
                pltpu.make_async_copy(src.at[table_ref[3 * j]], stage.at[at + j], sem_in).start()
                return carry

            lax.fori_loop(0, len(tables[i]), load, 0)
            at += len(tables[i])
        pltpu.make_async_copy(stage, stage, sem_in).wait()
        at = 0
        for i, table_ref, out in zip(used, table_refs, outs):

            def put(j, carry, table_ref=table_ref, out=out, at=at):
                row = pl.multiple_of(table_ref[3 * j + 1] * block, block)
                col = pl.multiple_of(table_ref[3 * j + 2] * block, block)
                pltpu.make_async_copy(
                    stage.at[at + j], out.at[pl.ds(row, block), pl.ds(col, block)], sem_out
                ).start()
                return carry

            lax.fori_loop(0, len(tables[i]), put, 0)
            at += len(tables[i])
        pltpu.make_async_copy(stage, stage, sem_out).wait()

    results = pl.pallas_call(
        body,
        out_shape=[jax.ShapeDtypeStruct(shapes[i], LOW) for i in used],
        in_specs=[SMEM] * len(used) + [ANY] * (1 + len(known)),
        out_specs=[ANY] * len(used),
        input_output_aliases={len(used) + 1 + j: used.index(i) for j, i in enumerate(known)},
        scratch_shapes=[
            pltpu.VMEM((count, block, block), LOW),
            pltpu.SemaphoreType.DMA,
            pltpu.SemaphoreType.DMA,
        ],
        compiler_params=pltpu.CompilerParams(vmem_limit_bytes=VMEM_LIMIT),
        cost_estimate=pl.CostEstimate(
            flops=0, bytes_accessed=4 * count * block * block, transcendentals=0
        ),
        name="place_blocks",
    )(
        *[jnp.asarray(tables[i].reshape(-1)) for i in used],
        gathered,
        *[partial[i] for i in known],
    )
    merged = list(partial)
    for i, value in zip(used, results):
        merged[i] = value
    return merged


def fill(scratch, pieces, order_ref):
    count = pieces[0].shape[0]
    for i, piece in enumerate(pieces):
        if order_ref is None:
            scratch[i * count : (i + 1) * count] = piece[...]
        else:
            scratch[pl.ds(pl.multiple_of(order_ref[i] * count, count), count)] = piece[...]


def grad_blocks(
    left, rights, order, pairs, table, wide, buffers, sizes, block, span=None, done=()
):
    tokens, height = left.shape
    by_column = len(rights) > 1 and rights[0].shape[0] == tokens
    width = sum(x.shape[-1] for x in rights) if by_column else rights[0].shape[-1]
    if pairs:
        width *= 2
    rows, cols = height // block, width // block
    if pairs:
        table = np.stack([table[: cols // 2], table[cols // 2 :]], 1).reshape(table.shape)
        wide = 2
    first, end = (0, cols // wide) if span is None else span
    steps = end - first
    if steps <= 0:
        return buffers
    assert not by_column or wide == 1
    per_step = rows * wide
    targets = [
        [(j, x, spot) for j, (x, spot) in enumerate(step) if (x, spot) not in done]
        for step in table.reshape(cols // wide, per_step, 2).tolist()[first:end]
    ]
    assert all(targets)
    used = sorted({x for step in targets for _, x, _ in step})
    known = [x for x in used if buffers[x] is not None]
    n_order = 0 if order is None else 1
    joined = len(rights) > 1
    first_known = n_order + 1 + len(rights)
    first_out = first_known + len(known)

    def body(*refs):
        left_ref = refs[n_order]
        right_refs = refs[n_order + 1 : first_known]
        outs = refs[first_out : first_out + len(used)]
        stage, sems = refs[first_out + len(used) : first_out + len(used) + 2]
        t = pl.program_id(0)
        slot = lax.rem(t, 2)
        if joined:
            right_ref = refs[-1]
            if by_column:
                step = 0
                for piece in right_refs:
                    for at in range(0, piece.shape[1], block):

                        @pl.when(t + first == step)
                        def _(piece=piece, at=at):
                            right_ref[...] = piece[:, at : at + block]

                        step += 1
            else:
                fill(right_ref, right_refs, refs[0] if n_order else None)
            taken = right_ref[...]
        elif pairs:
            taken = jnp.concatenate([right_refs[0][0], right_refs[0][1]], axis=1)
        else:
            taken = right_refs[0][...]

        def finish(step):
            sent = stage.at[step % 2, : len(targets[step])]
            pltpu.make_async_copy(sent, sent, sems.at[step % 2]).wait()

        for step in range(2, steps):

            @pl.when(t == step)
            def _(step=step):
                finish(step - 2)

        def some(i, carry):
            at = pl.multiple_of(i * (few * block), block)
            part = lax.dot_general(
                left_ref[:, pl.ds(at, few * block)],
                taken,
                (((0,), (0,)), ((), ())),
                preferred_element_type=F32,
            ).astype(LOW)
            for r in range(few):
                for c in range(wide):
                    stage[slot, c * rows + i * few + r] = part[
                        r * block : (r + 1) * block, c * block : (c + 1) * block
                    ]
            return carry

        few = rows // 2 if rows % 2 == 0 else rows
        lax.fori_loop(0, rows // few, some, 0)
        for step in range(steps):

            @pl.when(t == step)
            def _(step=step):
                for j, x, spot in targets[step]:
                    pltpu.make_async_copy(
                        stage.at[step % 2, j], outs[used.index(x)].at[spot], sems.at[step % 2]
                    ).start()

        @pl.when(t == steps - 1)
        def _():
            for step in range(max(0, steps - 2), steps):
                finish(step)

    taken_width = wide * block
    if pairs:
        right_specs = [pl.BlockSpec((2, tokens, block), lambda j: (0, 0, first + j))]
    elif by_column:
        right_specs = [pl.BlockSpec(x.shape, lambda j: (0, 0)) for x in rights]
    else:
        right_specs = [
            pl.BlockSpec((x.shape[0], taken_width), lambda j: (0, first + j)) for x in rights
        ]
    results = pl.pallas_call(
        body,
        grid=(steps,),
        out_shape=[jax.ShapeDtypeStruct((sizes[x], block, block), LOW) for x in used],
        in_specs=[SMEM] * n_order
        + [pl.BlockSpec((tokens, height), lambda j: (0, 0))]
        + right_specs
        + [ANY] * len(known),
        out_specs=[ANY] * len(used),
        input_output_aliases={first_known + j: used.index(x) for j, x in enumerate(known)},
        scratch_shapes=[
            pltpu.VMEM((2, per_step, block, block), LOW),
            pltpu.SemaphoreType.DMA((2,)),
        ]
        + ([pltpu.VMEM((tokens, taken_width), LOW)] if joined else []),
        compiler_params=pltpu.CompilerParams(vmem_limit_bytes=VMEM_LIMIT),
        cost_estimate=pl.CostEstimate(
            flops=4 * tokens * height * wide * block * steps,
            bytes_accessed=2 * (tokens * (height + width) + height * width),
            transcendentals=0,
        ),
        name="grad_blocks",
    )(*([] if order is None else [order]), left, *rights, *[buffers[x] for x in known])
    merged = list(buffers)
    for x, value in zip(used, results):
        merged[x] = value
    return merged


def grad_strips(strips, buffer_size, block):
    def body(*refs):
        out, stage, sem = refs[-3:]
        at = 0
        for i, (_, _, _, half, blocks) in enumerate(strips):
            right = refs[2 * i + 1]
            part = lax.dot_general(
                refs[2 * i][...],
                right[...] if half is None else right[0],
                (((0,), (0,)), ((), ())),
                preferred_element_type=F32,
            ).astype(LOW)
            for c, spot in blocks:
                stage[at] = part[:, c * block : (c + 1) * block]
                pltpu.make_async_copy(stage.at[at], out.at[spot], sem).start()
                at += 1
        pltpu.make_async_copy(stage, stage, sem).wait()

    specs, values = [], []
    for left, row, right, half, blocks in strips:
        tokens = left.shape[0]
        wide = (max(c for c, _ in blocks) + 1) * block
        specs.append(pl.BlockSpec((tokens, block), lambda j, row=row: (0, row)))
        if half is None:
            specs.append(pl.BlockSpec((tokens, wide), lambda j: (0, 0)))
        else:
            specs.append(pl.BlockSpec((1, tokens, wide), lambda j, half=half: (half, 0, 0)))
        values += [left, right]
    count = sum(len(blocks) for *_, blocks in strips)
    return pl.pallas_call(
        body,
        grid=(1,),
        in_specs=specs,
        out_specs=ANY,
        out_shape=jax.ShapeDtypeStruct((buffer_size, block, block), LOW),
        scratch_shapes=[pltpu.VMEM((count, block, block), LOW), pltpu.SemaphoreType.DMA],
        compiler_params=pltpu.CompilerParams(vmem_limit_bytes=VMEM_LIMIT),
        cost_estimate=pl.CostEstimate(
            flops=4 * count * values[0].shape[0] * block**2,
            bytes_accessed=4 * count * block * values[0].shape[0],
            transcendentals=0,
        ),
        name="grad_strips",
    )(*values)


def feed_forward(pieces, weights, hidden_grad, block):
    share, width = pieces[0].shape
    rows = share * len(pieces)
    hidden = weights.shape[1] // 2
    steps = hidden // block

    def body(*refs):
        gate_w, up_w, grad_ref, hid_ref, out_ref, joined = refs[len(pieces) :]

        @pl.when(pl.program_id(0) == 0)
        def _():
            fill(joined, refs[: len(pieces)], None)

        both = jnp.dot(
            joined[...],
            jnp.concatenate([gate_w[...], up_w[...]], axis=1),
            preferred_element_type=F32,
        )
        gate, up = both[:, :block], both[:, block:]
        grad = grad_ref[...]
        sig = jax.nn.sigmoid(gate)
        act = gate * sig
        hid_ref[...] = (act * up).astype(LOW)
        out_ref[0] = (grad * up * sig * (1.0 + gate * (1.0 - sig))).astype(LOW)
        out_ref[1] = (grad * act).astype(LOW)

    return pl.pallas_call(
        body,
        grid=(steps,),
        in_specs=[pl.BlockSpec((share, width), lambda j: (0, 0))] * len(pieces)
        + [
            pl.BlockSpec((width, block), lambda j: (0, j)),
            pl.BlockSpec((width, block), lambda j: (0, steps + j)),
            pl.BlockSpec((rows, block), lambda j: (0, j)),
        ],
        out_specs=[
            pl.BlockSpec((rows, block), lambda j: (0, j)),
            pl.BlockSpec((2, rows, block), lambda j: (0, 0, j)),
            pl.BlockSpec((rows, width), lambda j: (0, 0)),
        ],
        out_shape=[
            jax.ShapeDtypeStruct((rows, hidden), LOW),
            jax.ShapeDtypeStruct((2, rows, hidden), LOW),
            jax.ShapeDtypeStruct((rows, width), LOW),
        ],
        compiler_params=pltpu.CompilerParams(vmem_limit_bytes=VMEM_LIMIT),
        cost_estimate=pl.CostEstimate(
            flops=4 * rows * width * hidden,
            bytes_accessed=2 * rows * width + 4 * width * hidden + 10 * rows * hidden,
            transcendentals=rows * hidden,
        ),
        name="feed_forward",
    )(*pieces, weights, weights, hidden_grad)


def project_rows(parts, weights, order, turned, tile):
    stacked = parts[0].ndim == 3
    rows = parts[0].shape[-2]
    half = rows // 2
    widths = [parts[0].shape[2]] * parts[0].shape[0] if stacked else [x.shape[1] for x in parts]
    starts = [sum(widths[:i]) for i in range(len(widths))]
    width = weights.shape[0] if turned else weights.shape[1]
    depth = sum(widths)
    share = rows // 4
    n_order = 0 if order is None else 1

    def body(*refs):
        part_refs = refs[n_order : n_order + len(parts)]
        w_ref, kept_ref, sent_ref = refs[n_order + len(parts) : n_order + len(parts) + 3]
        if n_order:
            joined = refs[-1]

            @pl.when(pl.program_id(0) == 0)
            def _():
                for i in range(4):
                    take = pl.ds(pl.multiple_of(refs[0][i] * share, share), share)
                    for part, at, size in zip(part_refs, starts, widths):
                        joined[i * share : (i + 1) * share, at : at + size] = part[take]

            pieces = [(joined[...], 0, depth)]
        elif stacked:
            pieces = [(part_refs[0][i], at, widths[i]) for i, at in enumerate(starts)]
        else:
            pieces = [(p[...], at, size) for p, at, size in zip(part_refs, starts, widths)]
        total = None
        for value, at, size in pieces:
            if turned:
                one = dot_turned(value, w_ref[:, at : at + size])
            else:
                one = dot(value, w_ref[at : at + size])
            total = one if total is None else total + one
        total = total.astype(LOW)
        kept_ref[...] = total[:half]
        sent_ref[...] = total[half:]

    whole = [pl.BlockSpec(x.shape, lambda j, n=x.ndim: (0,) * n) for x in parts]
    if turned:
        weight_spec = pl.BlockSpec((tile, depth), lambda j: (j, 0))
    else:
        weight_spec = pl.BlockSpec((depth, tile), lambda j: (0, j))
    kept, sent = pl.pallas_call(
        body,
        grid=(width // tile,),
        in_specs=[SMEM] * n_order + whole + [weight_spec],
        out_specs=[pl.BlockSpec((half, tile), lambda j: (0, j))] * 2,
        out_shape=[jax.ShapeDtypeStruct((half, width), LOW)] * 2,
        scratch_shapes=[pltpu.VMEM((rows, depth), LOW)] * n_order,
        compiler_params=pltpu.CompilerParams(vmem_limit_bytes=VMEM_LIMIT),
        cost_estimate=pl.CostEstimate(
            flops=2 * rows * depth * width,
            bytes_accessed=2 * (rows * depth + depth * width + rows * width),
            transcendentals=0,
        ),
        name="project_rows",
    )(*([order] if n_order else []), *parts, weights)
    return sent, kept


def down_back(grads, weights):
    rows, depth = grads.shape
    hidden = weights.shape[0]
    tile = 2 * LANES
    full, rest = divmod(hidden, tile)

    def body(g_ref, w_ref, o_ref):
        t = pl.program_id(0)

        @pl.when(t < full)
        def _():
            here = pl.ds(pl.multiple_of(t * tile, tile), tile)
            o_ref[...] = dot_turned(g_ref[...], w_ref[here])

        if rest:

            @pl.when(t == full)
            def _():
                o_ref[:, :rest] = dot_turned(g_ref[...], w_ref[full * tile :])

    return pl.pallas_call(
        body,
        grid=(full + (rest > 0),),
        in_specs=[
            pl.BlockSpec((rows, depth), lambda j: (0, 0)),
            pl.BlockSpec((hidden, depth), lambda j: (0, 0)),
        ],
        out_specs=pl.BlockSpec((rows, tile), lambda j: (0, j)),
        out_shape=jax.ShapeDtypeStruct((rows, hidden), F32),
        compiler_params=pltpu.CompilerParams(vmem_limit_bytes=VMEM_LIMIT),
        cost_estimate=pl.CostEstimate(
            flops=2 * rows * depth * hidden,
            bytes_accessed=2 * depth * (rows + hidden) + 4 * rows * hidden,
            transcendentals=0,
        ),
        name="down_back",
    )(grads, weights)


def to_heads(pieces, weights, order):
    share = pieces[0].shape[0]
    width = weights.shape[0]

    rows = share * len(pieces)

    def body(order_ref, *refs):
        w_ref, out_ref = refs[-2:]
        for i, piece in enumerate(refs[:-2]):
            put = pl.ds(pl.multiple_of(order_ref[i] * share, share), share)
            out_ref[put] = dot_turned(piece[...], w_ref[...]).astype(LOW)

    return pl.pallas_call(
        body,
        in_specs=[SMEM] + [VMEM] * (len(pieces) + 1),
        out_specs=VMEM,
        out_shape=jax.ShapeDtypeStruct((rows, width), LOW),
        compiler_params=pltpu.CompilerParams(vmem_limit_bytes=VMEM_LIMIT),
        cost_estimate=pl.CostEstimate(
            flops=2 * rows * width * weights.shape[1],
            bytes_accessed=2 * (rows + width) * weights.shape[1],
            transcendentals=0,
        ),
        name="to_heads",
    )(order, *pieces, weights)


LANES = 128
QUERIES = 256
LONGEST = 512


def turn(values, cos, sin):
    lane = lax.broadcasted_iota(jnp.int32, values.shape, 1)
    other = jnp.where(
        lane % HD < HD // 2,
        pltpu.roll(values, LANES - HD // 2, 1),
        pltpu.roll(values, HD // 2, 1),
    )
    return values * cos + other * sin


def key_tables(cos, sin):
    lane = lax.broadcasted_iota(jnp.int32, cos.shape, 1)
    return jnp.where(lane < HD, cos, 1.0), jnp.where(lane < HD, sin, 0.0)


def project_heads(inputs, weights, cos, sin):
    rows, depth = inputs.shape
    width = weights.shape[1]
    assert width % LANES == 0 and HD == 64

    def body(x_ref, w_ref, cos_ref, sin_ref, q_ref, kv_ref):
        t = pl.program_id(0)
        raw = dot(x_ref[...], w_ref[...])

        @pl.when(t < steps - 1)
        def _():
            q_ref[...] = turn(raw, cos_ref[...], sin_ref[...]).astype(LOW) * LOW(HD**-0.5)

        @pl.when(t == steps - 1)
        def _():
            kv_ref[...] = turn(raw, *key_tables(cos_ref[...], sin_ref[...])).astype(LOW)

    steps = width // LANES
    whole = pl.BlockSpec((rows, LANES), lambda j: (0, 0))
    return pl.pallas_call(
        body,
        grid=(steps,),
        in_specs=[
            pl.BlockSpec((rows, depth), lambda j: (0, 0)),
            pl.BlockSpec((depth, LANES), lambda j: (0, j)),
            whole,
            whole,
        ],
        out_specs=[pl.BlockSpec((rows, LANES), lambda j: (0, jnp.minimum(j, steps - 2))), whole],
        out_shape=[
            jax.ShapeDtypeStruct((rows, width - LANES), LOW),
            jax.ShapeDtypeStruct((rows, LANES), LOW),
        ],
        compiler_params=pltpu.CompilerParams(vmem_limit_bytes=VMEM_LIMIT),
        cost_estimate=pl.CostEstimate(
            flops=2 * rows * depth * width,
            bytes_accessed=2 * (rows * depth + depth * width + rows * width),
            transcendentals=0,
        ),
        name="project_heads",
    )(inputs, weights, cos, sin)


def keep_keys(padded, kv_ref):
    padded[:LONGEST] = jnp.zeros((LONGEST, LANES), LOW)
    padded[LONGEST:] = kv_ref[...]


def visible(start_ref, at):
    shape = (LONGEST + QUERIES, QUERIES)
    key = at - LONGEST + lax.broadcasted_iota(jnp.int32, shape, 0)
    query = at + lax.broadcasted_iota(jnp.int32, shape, 1)
    return (key >= start_ref[:, pl.ds(at, QUERIES)]) & (key <= query)


def attend(queries, kv, starts):
    rows, width = queries.shape
    groups = width // LANES

    def body(start_ref, q_ref, kv_ref, o_ref, log_ref, padded):
        @pl.when(pl.program_id(0) == 0)
        def _():
            keep_keys(padded, kv_ref)

        def one(i, carry):
            at = pl.multiple_of(i * QUERIES, QUERIES)
            here = pl.ds(at, QUERIES)
            seen = visible(start_ref, at)
            window = padded[pl.ds(at, LONGEST + QUERIES)]
            keys, values = window[:, :HD], window[:, HD:]
            for h in range(LANES // HD):
                query = q_ref[here, h * HD : (h + 1) * HD]
                scores = jnp.where(seen, dot_turned(keys, query), -1e30)
                top = jnp.max(scores, axis=0, keepdims=True)
                expo = jnp.exp(scores - top)
                total = jnp.sum(expo, axis=0, keepdims=True)
                probs = (expo * (1.0 / total)).astype(LOW)
                o_ref[here, h * HD : (h + 1) * HD] = lax.dot_general(
                    probs, values, (((0,), (0,)), ((), ())), preferred_element_type=F32
                ).astype(LOW)
                log_ref[0, h : h + 1, here] = top + jnp.log(total)
            return carry

        lax.fori_loop(0, rows // QUERIES, one, 0)

    column = pl.BlockSpec((rows, LANES), lambda j: (0, j))
    return pl.pallas_call(
        body,
        grid=(groups,),
        in_specs=[
            pl.BlockSpec((1, rows), lambda j: (0, 0)),
            column,
            pl.BlockSpec((rows, LANES), lambda j: (0, 0)),
        ],
        out_specs=[column, pl.BlockSpec((1, LANES // HD, rows), lambda j: (j, 0, 0))],
        out_shape=[
            jax.ShapeDtypeStruct((rows, width), LOW),
            jax.ShapeDtypeStruct((groups, LANES // HD, rows), F32),
        ],
        scratch_shapes=[pltpu.VMEM((LONGEST + rows, LANES), LOW)],
        compiler_params=pltpu.CompilerParams(vmem_limit_bytes=VMEM_LIMIT),
        cost_estimate=pl.CostEstimate(
            flops=30 * rows * rows * width,
            bytes_accessed=4 * rows * width,
            transcendentals=rows * rows * width // HD,
        ),
        name="attend",
    )(starts, queries, kv)


def attend_back(queries, kv, starts, logs, grads, cos, sin):
    rows, width = queries.shape
    groups = width // LANES

    def body(
        start_ref, q_ref, kv_ref, log_ref, g_ref, cos_ref, sin_ref, dq_ref, sum_ref, acc, padded
    ):
        @pl.when(pl.program_id(0) == 0)
        def _():
            keep_keys(padded, kv_ref)
            acc[...] = jnp.zeros_like(acc)

        def one(i, carry):
            at = pl.multiple_of(i * QUERIES, QUERIES)
            here = pl.ds(at, QUERIES)
            there = pl.ds(at, LONGEST + QUERIES)
            seen = visible(start_ref, at)
            window = padded[there]
            keys, values = window[:, :HD], window[:, HD:]
            parts = []
            key_part, value_part = 0.0, 0.0
            for h in range(LANES // HD):
                query = q_ref[here, h * HD : (h + 1) * HD]
                grad = g_ref[here, h * HD : (h + 1) * HD]
                scores = jnp.where(seen, dot_turned(keys, query), -1e30)
                probs = jnp.exp(scores - log_ref[0, h : h + 1, here])
                value_part += dot(probs.astype(LOW), grad)
                prob_grads = dot_turned(values, grad)
                inner = jnp.sum(probs * prob_grads, axis=0, keepdims=True)
                score_grads = (probs * (prob_grads - inner)).astype(LOW)
                key_part += dot(score_grads, query)
                parts.append(
                    lax.dot_general(
                        score_grads, keys, (((0,), (0,)), ((), ())), preferred_element_type=F32
                    )
                )
            acc[there] += jnp.concatenate([key_part, value_part], axis=1)
            dq_ref[here] = turn(
                jnp.concatenate(parts, axis=1) * HD**-0.5, cos_ref[here], -sin_ref[here]
            ).astype(LOW)
            return carry

        lax.fori_loop(0, rows // QUERIES, one, 0)

        @pl.when(pl.program_id(0) == groups - 1)
        def _():
            key_cos, key_sin = key_tables(cos_ref[...], sin_ref[...])
            sum_ref[...] = turn(acc[LONGEST:], key_cos, -key_sin).astype(LOW)

    column = pl.BlockSpec((rows, LANES), lambda j: (0, j))
    whole = pl.BlockSpec((rows, LANES), lambda j: (0, 0))
    return pl.pallas_call(
        body,
        grid=(groups,),
        in_specs=[
            pl.BlockSpec((1, rows), lambda j: (0, 0)),
            column,
            whole,
            pl.BlockSpec((1, LANES // HD, rows), lambda j: (j, 0, 0)),
            column,
            whole,
            whole,
        ],
        out_specs=[column, whole],
        out_shape=[
            jax.ShapeDtypeStruct((rows, width), LOW),
            jax.ShapeDtypeStruct((rows, LANES), LOW),
        ],
        scratch_shapes=[
            pltpu.VMEM((LONGEST + rows, LANES), F32),
            pltpu.VMEM((LONGEST + rows, LANES), LOW),
        ],
        compiler_params=pltpu.CompilerParams(vmem_limit_bytes=VMEM_LIMIT),
        cost_estimate=pl.CostEstimate(
            flops=400 * rows * rows * width,
            bytes_accessed=16 * rows * width,
            transcendentals=rows * rows * width // HD,
        ),
        name="attend_back",
    )(starts, queries, kv, logs, grads, cos, sin)


def shampoo(sums, places, factor, weights, ema, left, right, left_roots, right_roots, before):
    count, block, _ = sums.shape
    group = 2 if count % 2 == 0 else 1
    steps = count // group
    depth = min(4, steps)
    extra = [] if before is None else list(before)

    def mm(a, b, dims):
        return lax.dot_general(
            a.astype(LOW), b.astype(LOW), (dims, ((), ())), preferred_element_type=F32
        )

    def body(places_ref, g_ref, *refs):
        ins, outs = refs[:6], refs[6 + len(extra) : 11 + len(extra)]
        given, made, sem_in, sem_out = refs[11 + len(extra) :]

        def load(t, slot):
            for u in range(group):
                place = places_ref[t * group + u]
                for i, ref in enumerate(ins):
                    pltpu.make_async_copy(
                        ref.at[place], given.at[slot, u, i], sem_in.at[slot]
                    ).start()

        def wait(buffer, slot, sems):
            pltpu.make_async_copy(buffer.at[slot], buffer.at[slot], sems.at[slot]).wait()

        for t in range(depth):
            load(t, t)

        def step(t, carry):
            slot = lax.rem(t, depth)
            wait(given, slot, sem_in)

            @pl.when(t >= depth)
            def _():
                wait(made, slot, sem_out)

            both = 0.5 * factor * factor
            for u in range(group):
                low = g_ref[t * group + u]
                made[slot, u, 0] = low.astype(F32) * factor
                made[slot, u, 3] = 0.5 * given[slot, u, 2] + both * mm(low, low, ((1,), (1,)))
                made[slot, u, 4] = 0.5 * given[slot, u, 3] + both * mm(low, low, ((0,), (0,)))
                part = mm(low, given[slot, u, 5], ((1,), (0,))) * factor
                fresh = given[slot, u, 0] - weight_rate * mm(given[slot, u, 4], part, ((1,), (0,)))
                made[slot, u, 1] = fresh
                made[slot, u, 2] = (
                    average_decay * given[slot, u, 1] + (1.0 - average_decay) * fresh
                )
            for u in range(group):
                place = places_ref[t * group + u]
                for i, ref in enumerate(outs):
                    pltpu.make_async_copy(
                        made.at[slot, u, i], ref.at[place], sem_out.at[slot]
                    ).start()

            @pl.when(t + depth < steps)
            def _():
                load(t + depth, slot)

            return carry

        lax.fori_loop(0, steps, step, 0)
        for t in range(steps - depth, steps):
            wait(made, t % depth, sem_out)

    return pl.pallas_call(
        body,
        out_shape=[jax.ShapeDtypeStruct(weights.shape, F32)] * 5,
        in_specs=[SMEM, VMEM] + [ANY] * (6 + len(extra)),
        out_specs=[ANY] * 5,
        input_output_aliases={8 + i: i for i in range(len(extra))},
        scratch_shapes=[
            pltpu.VMEM((depth, group, 6, block, block), F32),
            pltpu.VMEM((depth, group, 5, block, block), F32),
            pltpu.SemaphoreType.DMA((depth,)),
            pltpu.SemaphoreType.DMA((depth,)),
        ],
        compiler_params=pltpu.CompilerParams(vmem_limit_bytes=VMEM_LIMIT),
        cost_estimate=pl.CostEstimate(
            flops=8 * count * block**3,
            bytes_accessed=46 * count * block * block,
            transcendentals=0,
        ),
        name="shampoo",
    )(places, sums, weights, ema, left, right, left_roots, right_roots, *extra)


def rows_call(body, ins, outs, name, step=64):
    rows = max(x.shape[0] for x in ins)

    def spec(x):
        if x.shape[0] == rows:
            return pl.BlockSpec((step, x.shape[1]), lambda j: (j, 0))
        return pl.BlockSpec(x.shape, lambda j: (0, 0))

    return pl.pallas_call(
        body,
        grid=(rows // step,),
        in_specs=[spec(x) for x in ins],
        out_specs=[spec(x) for x in outs],
        out_shape=outs,
        compiler_params=pltpu.CompilerParams(vmem_limit_bytes=VMEM_LIMIT),
        cost_estimate=pl.CostEstimate(
            flops=10 * rows * ins[0].shape[1],
            bytes_accessed=sum(x.size * x.dtype.itemsize for x in list(ins) + list(outs)),
            transcendentals=0,
        ),
        name=name,
    )(*ins)


def add_near(kept, got):
    share = kept.shape[0] // 2
    width = kept.shape[1]
    step = 64

    def body(a_ref, c_ref, b_ref, d_ref, mine_ref, other_ref):
        mine_ref[...] = a_ref[...].astype(F32) + b_ref[...].astype(F32)
        other_ref[...] = (c_ref[...].astype(F32) + d_ref[...].astype(F32)).astype(LOW)

    first = pl.BlockSpec((step, width), lambda j: (j, 0))
    second = pl.BlockSpec((step, width), lambda j: (share // step + j, 0))
    return pl.pallas_call(
        body,
        grid=(share // step,),
        in_specs=[first, second, first, second],
        out_specs=[first] * 2,
        out_shape=[
            jax.ShapeDtypeStruct((share, width), F32),
            jax.ShapeDtypeStruct((share, width), LOW),
        ],
        compiler_params=pltpu.CompilerParams(vmem_limit_bytes=VMEM_LIMIT),
        cost_estimate=pl.CostEstimate(
            flops=2 * share * width, bytes_accessed=14 * share * width, transcendentals=0
        ),
        name="add_near",
    )(kept, kept, got, got)


def second_norm(tokens, mine, got, gain):
    def body(x_ref, a_ref, b_ref, gain_ref, middle_ref, low_ref):
        middle = x_ref[...].astype(F32) + (a_ref[...] + b_ref[...].astype(F32))
        middle_ref[...] = middle
        scale = lax.rsqrt(jnp.mean(middle * middle, axis=-1, keepdims=True) + 1e-05)
        low_ref[...] = (middle * scale * gain_ref[...]).astype(LOW)

    return rows_call(
        body,
        [tokens, mine, got, gain],
        [jax.ShapeDtypeStruct(tokens.shape, F32), jax.ShapeDtypeStruct(tokens.shape, LOW)],
        "second_norm",
    )


def first_norm(tokens, gain):
    def body(x_ref, gain_ref, low_ref):
        x = x_ref[...].astype(F32)
        scale = lax.rsqrt(jnp.mean(x * x, axis=-1, keepdims=True) + 1e-05)
        low_ref[...] = (x * scale * gain_ref[...]).astype(LOW)

    return rows_call(
        body,
        [tokens, gain],
        [jax.ShapeDtypeStruct(tokens.shape, LOW)],
        "first_norm",
    )[0]


def norm_back(values, mine, got, gain, residual):
    def body(x_ref, a_ref, b_ref, gain_ref, r_ref, out_ref, low_ref, sum_ref):
        x = x_ref[...].astype(F32)
        grad = a_ref[...] + b_ref[...].astype(F32)
        scale = lax.rsqrt(jnp.mean(x * x, axis=-1, keepdims=True) + 1e-05)
        unit = x * scale
        scaled = grad * gain_ref[...]
        out = r_ref[...].astype(F32) + scale * (
            scaled - unit * jnp.mean(scaled * unit, axis=-1, keepdims=True)
        )
        out_ref[...] = out
        low_ref[...] = out.astype(LOW)

        @pl.when(pl.program_id(0) == 0)
        def _():
            sum_ref[...] = jnp.zeros_like(sum_ref)

        sum_ref[...] += jnp.sum(grad * unit, axis=0, keepdims=True)

    shape = values.shape
    return rows_call(
        body,
        [values, mine, got, gain, residual],
        [
            jax.ShapeDtypeStruct(shape, F32),
            jax.ShapeDtypeStruct(shape, LOW),
            jax.ShapeDtypeStruct((1, shape[1]), F32),
        ],
        "norm_back",
    )


def doc_positions(doc_ids):
    length = doc_ids.shape[-1]
    offsets = jnp.arange(length, dtype=jnp.int32)
    starts = jnp.concatenate(
        [jnp.ones(doc_ids.shape[:-1] + (1,), jnp.bool_), doc_ids[..., 1:] != doc_ids[..., :-1]],
        axis=-1,
    )
    first_index = lax.cummax(jnp.where(starts, offsets, 0), axis=doc_ids.ndim - 1)
    return offsets - first_index


def rope_tables(positions, head_size):
    half_size = head_size // 2
    exponent = jnp.arange(half_size, dtype=F32) * (2.0 / head_size)
    inverse = jnp.power(F32(10000.0), -exponent)
    angles = positions.astype(F32)[..., None] * inverse
    cos, sin = jnp.cos(angles), jnp.sin(angles)
    repeats = LANES // head_size
    return (
        jnp.concatenate([cos, cos] * repeats, axis=-1),
        jnp.concatenate([-sin, sin] * repeats, axis=-1),
    )


def after(value, *others):
    return lax.optimization_barrier((value,) + others)[0]


def dot(left, right):
    return jnp.dot(left, right, preferred_element_type=F32)


def dot_turned(left, right):
    return lax.dot_general(left, right, (((1,), (1,)), ((), ())), preferred_element_type=F32)


EXCHANGE = (0, 2, 1, 3)


def on_device(
    tokens_in,
    cotangent,
    select_mask,
    doc_ids,
    norm_gains,
    weight_blocks,
    ema_blocks,
    left_stats,
    right_stats,
    left_roots,
    right_roots,
):
    mp_count = lax.axis_size("mp")
    dp_count = lax.axis_size("dp")
    sequences, length, model_width = tokens_in.shape
    assert sequences == 1 and mp_count == 4 and dp_count & (dp_count - 1) == 0
    rows = sequences * length
    own, block, _ = weight_blocks.shape
    query_cols = HEADS * HD // mp_count
    key_cols = KV_HEADS * HD // mp_count
    hidden_cols = FF // mp_count
    assert KV_HEADS == mp_count and length % QUERIES == 0
    row_blocks = model_width // block
    attn_blocks = (query_cols + 2 * key_cols) // block
    hidden_blocks = hidden_cols // block
    in_blocks = attn_blocks + 2 * hidden_blocks
    out_attn_blocks = query_cols // block
    share = rows // mp_count
    m_index = lax.axis_index("mp")
    d_index = lax.axis_index("dp")

    plan = Layout(dp_count, own, row_blocks, attn_blocks, in_blocks, out_attn_blocks)
    order = lax.dynamic_slice_in_dim(jnp.asarray(plan.order), d_index, 1, 0).reshape(-1)
    shapes = [
        (model_width, attn_blocks * block),
        (query_cols, model_width),
        (model_width, 2 * hidden_cols),
        (hidden_cols, model_width),
    ]

    def partner(values, bit):
        return lax.ppermute(values, "mp", [(i, i ^ bit) for i in range(mp_count)])

    def true_share(values, group):
        return lax.dynamic_slice_in_dim(values, (m_index ^ group) * share, share, 0)

    def to_exchange(values):
        return jnp.concatenate([true_share(values, g) for g in EXCHANGE], axis=0)

    def to_true(parts):
        by_group = [parts[EXCHANGE.index(g)] for g in range(4)]
        low, high = m_index & 1, m_index & 2
        pairs = []
        for a, b in ((0, 1), (2, 3)):
            pairs.append(
                (
                    jnp.where(low == 0, by_group[a], by_group[b]),
                    jnp.where(low == 0, by_group[b], by_group[a]),
                )
            )
        flat = []
        for first, second in ((0, 1), (1, 0)):
            for i in range(2):
                flat.append(jnp.where(high == 0, pairs[first][i], pairs[second][i]))
        return jnp.concatenate(flat, axis=0)

    def near_sum(sent, kept):
        return add_near(kept, partner(sent, 1))

    def spread_share(mine, *cover):
        far = partner(mine, 2)
        near = partner(mine, 1)
        if cover:
            far = after(far, *cover)
        return [mine, far, near, partner(far, 1)]

    sorted_low = sort_blocks(weight_blocks, order, plan.chunks)
    gathered = [
        lax.all_gather(chunk, "dp", axis=0, tiled=True, axis_index_groups=[plan.ring])
        for chunk in sorted_low
    ]
    none = np.zeros((0, 3), np.int32)
    last = len(gathered) - 1

    def place(x, source, which, matrices):
        tables = [plan.of_chunk(x, i) if i in which else none for i in range(4)]
        return place_blocks(source, tables, shapes, matrices)

    matrices = place(0, gathered[0], (0, 1, 2, 3), [None] * 4)
    w_qkv = matrices[0]
    if last >= 1:
        matrices = place(1, gathered[1], (1,), matrices)
    w_attn_out = matrices[1]

    positions = doc_positions(doc_ids)
    starts = jnp.arange(length, dtype=jnp.int32)[None] - positions
    cos, sin = rope_tables(positions[0], HD)

    tokens_low = tokens_in.reshape(rows, model_width)
    first_in = first_norm(tokens_low, norm_gains[:1])
    out_grad = cotangent.reshape(rows, model_width) * select_mask.astype(LOW).reshape(rows, 1)
    own_tokens = true_share(tokens_low, 0)
    own_grad = true_share(out_grad, 0)
    mlp_grad = to_exchange(out_grad)
    tokens_local = to_exchange(tokens_low)
    unit_scale = lax.rsqrt(
        jnp.mean(jnp.square(tokens_local.astype(F32)), axis=-1, keepdims=True) + 1e-05
    )

    shares = (m_index ^ jnp.array(EXCHANGE, jnp.int32)).astype(jnp.int32)
    queries, kv = project_heads(first_in, w_qkv, cos, sin)
    kv, mlp_grad, own_tokens, own_grad, tokens_local, unit_scale = lax.optimization_barrier(
        (kv, mlp_grad, own_tokens, own_grad, tokens_local, unit_scale)
    )
    mixed, logs = attend(queries, kv, starts)
    attended_sent, attended_kept = project_rows([mixed], w_attn_out, shares, False, 512)
    mine, other = near_sum(attended_sent, attended_kept)
    if last >= 1:
        matrices = place(1, after(gathered[1], other), (2, 3), matrices)
        mine, *matrices[2:] = lax.optimization_barrier((mine, *matrices[2:]))
    middle, second_low = second_norm(own_tokens, mine, partner(other, 2), norm_gains[1:])
    if last >= 2:
        matrices = place(2, after(gathered[2], second_low), (2, 3), matrices)
    w_gateup, w_down = matrices[2:]
    hidden_grad = down_back(mlp_grad, w_down)
    second_pieces = spread_share(second_low, hidden_grad)
    hidden, gateup_grad, second_in = feed_forward(second_pieces, w_gateup, hidden_grad, block)

    second_sent, second_kept = project_rows([gateup_grad], w_gateup, None, True, 256)
    sizes = [dp_count * n for _, n in plan.chunks]
    sums = [None] * len(sizes)
    reduced = [None] * len(sizes)

    def scatter(x):
        reduced[x] = lax.psum_scatter(
            sums[x], "dp", scatter_dimension=0, tiled=True, axis_index_groups=[plan.ring]
        )

    def known(values):
        return [x for x in values if x is not None]

    cuts = {2: 0, 3: 0}
    sent = set()
    if last >= 2:
        cuts = {2: plan.first_late[2], 3: plan.first_late[3] // 2}
        sent = {(last, spot) for *_, spot in plan.strips}
    if sent:
        strips = {}
        for matrix, r, c, spot in plan.strips:
            half = c // hidden_blocks if matrix == 2 else None
            at = c if half is None else c % hidden_blocks
            strips.setdefault((matrix, r, half), []).append((at, spot))
        sums[last] = grad_strips(
            [
                (
                    after(second_in, second_sent) if matrix == 2 else after(hidden, second_sent),
                    r,
                    gateup_grad if matrix == 2 else mlp_grad,
                    half,
                    blocks,
                )
                for (matrix, r, half), blocks in strips.items()
            ],
            sizes[last],
            block,
        )

    def down_grads(sums, hidden, span):
        table = plan.of_matrix(3, hidden_blocks, row_blocks)
        return grad_blocks(
            hidden, [mlp_grad], None, False, table, 2, sums, sizes, block, span, sent
        )

    def gateup_grads(sums, second_in, span):
        table = plan.of_matrix(2, row_blocks, 2 * hidden_blocks)
        return grad_blocks(
            second_in, [gateup_grad], None, True, table, 2, sums, sizes, block, span, sent
        )

    sums = down_grads(sums, after(hidden, second_sent), (cuts[3], row_blocks // 2))
    mine, other = near_sum(second_sent, after(second_kept, *known(sums)))
    sums = gateup_grads(sums, after(second_in, other), (cuts[2], hidden_blocks))
    if last >= 2:
        scatter(2)
    got = partner(other, 2)
    sums = gateup_grads(sums, second_in, (0, cuts[2]))
    mine = after(mine, *known(sums[:2]))
    middle_grad, attn_low, second_gain = norm_back(
        middle, mine, got, norm_gains[1:], own_grad
    )
    sums = down_grads(sums, after(hidden, attn_low), (0, cuts[3]))
    feed_sent, feed_kept = project_rows(
        [after(hidden, *known(sums[:2]))], w_down, None, False, 512
    )
    attn_grad = spread_share(attn_low, feed_kept)
    sums = grad_blocks(
        mixed,
        attn_grad,
        shares,
        False,
        plan.of_matrix(1, out_attn_blocks, row_blocks),
        4,
        sums,
        sizes,
        block,
    )
    if last >= 1:
        scatter(1)

    feed_mine, feed_other = near_sum(feed_sent, after(feed_kept, *known(sums[:2])))
    mixed_grad = to_heads(attn_grad, after(w_attn_out, feed_other), shares)
    query_grad, kv_grad = attend_back(queries, kv, starts, logs, mixed_grad, cos, sin)
    feed_part = after(feed_mine, query_grad) + partner(feed_other, 2).astype(F32)
    out_low = (middle + feed_part).astype(LOW)
    qkv_grads = [query_grad, kv_grad]
    first_sent, first_kept = project_rows(
        [after(query_grad, out_low), kv_grad], w_qkv, shares, True, 512
    )
    mine, other = near_sum(first_sent, first_kept)

    half = rows // 2
    first_gain = sum(
        jnp.sum(part.astype(F32) * (x.astype(F32) * scale), axis=0, keepdims=True)
        for part, x, scale in (
            (first_kept, tokens_local[:half], unit_scale[:half]),
            (first_sent, tokens_local[half:], unit_scale[half:]),
        )
    )
    gain_sums = jnp.concatenate([first_gain, second_gain], axis=0)
    gain_sums = gain_sums + partner(gain_sums, 2)
    other = after(other, gain_sums)
    sums = grad_blocks(
        after(first_in, other),
        qkv_grads,
        None,
        False,
        plan.of_matrix(0, row_blocks, attn_blocks),
        1,
        sums,
        sizes,
        block,
    )
    scatter(0)
    factor = float(rows * dp_count) ** (-0.5)

    def update(x, state, *others):
        start, count = plan.chunks[x]
        return shampoo(
            reduced[x],
            after(lax.slice_in_dim(order, start, start + count), *others),
            factor,
            weight_blocks,
            ema_blocks,
            left_stats,
            right_stats,
            left_roots,
            right_roots,
            state,
        )

    _, input_low, _ = norm_back(
        own_tokens,
        after(mine, sums[0]),
        partner(other, 2),
        norm_gains[:1],
        middle_grad,
    )
    state = None
    if last >= 2:
        state = update(2, state, input_low)
    if last >= 1:
        state = update(1, state, input_low)
    gain_sums = after(gain_sums, input_low, *(state or ()))
    gain_sums = gain_sums + partner(gain_sums, 1)
    bit = 1
    while bit < dp_count:
        gain_sums = gain_sums + lax.ppermute(
            gain_sums, "dp", [(i, i ^ bit) for i in range(dp_count)]
        )
        bit *= 2
    input_parts = spread_share(input_low, *(state or ()))
    gain_share = model_width // dp_count
    gain_grads = factor * lax.dynamic_slice_in_dim(gain_sums, d_index * gain_share, gain_share, 1)
    old_gains = lax.dynamic_slice_in_dim(norm_gains, d_index * gain_share, gain_share, 1)
    new_gains = old_gains - gain_rate * gain_grads
    out_parts = spread_share(after(out_low, input_low), *(state or ()))
    block_out = to_true(out_parts).reshape(sequences, length, model_width)
    input_grad = to_true(input_parts).astype(F32).reshape(sequences, length, model_width)
    grads, new_weights, new_ema, new_left, new_right = update(
        0, state, input_grad, block_out, new_gains
    )
    return (
        block_out,
        input_grad,
        grads,
        new_weights,
        new_ema,
        new_left,
        new_right,
        gain_grads,
        new_gains,
    )


def solution(mesh):
    in_specs = (
        P("dp", None, None),
        P("dp", None, None),
        P("dp", None),
        P("dp", None),
        P(),
        P(("dp", "mp"), None, None),
        P(("dp", "mp"), None, None),
        P(("dp", "mp"), None, None),
        P(("dp", "mp"), None, None),
        P(("dp", "mp"), None, None),
        P(("dp", "mp"), None, None),
    )
    out_specs = (
        P("dp", None, None),
        P("dp", None, None),
        P(("dp", "mp"), None, None),
        P(("dp", "mp"), None, None),
        P(("dp", "mp"), None, None),
        P(("dp", "mp"), None, None),
        P(("dp", "mp"), None, None),
        P(None, "dp"),
        P(None, "dp"),
    )
    return jax.shard_map(
        on_device, mesh=mesh, in_specs=in_specs, out_specs=out_specs, check_vma=False
    )
```

```python
import functools

import jax
import jax.numpy as jnp
import numpy as np
from jax import lax
from jax.experimental import pallas as pl
from jax.experimental.pallas import tpu as pltpu
from jax.sharding import PartitionSpec as P

HEADS = 32
KV_HEADS = 4
HD = 64
FF = 5632
LOW = jnp.bfloat16
F32 = jnp.float32

weight_rate = 1.0
gain_rate = 0.2
average_decay = 0.9
VMEM_LIMIT = 60 * 1024 * 1024


def ring_order(count):
    return list(range(0, count, 2)) + list(range(1, count, 2))[::-1]


class Layout:
    def __init__(self, dp, own, rows, attn_cols, in_cols, out_attn_rows):
        self.dp, self.own = dp, own
        self.ring = ring_order(dp)
        n_in = rows * in_cols
        units = (in_cols - attn_cols) // 2
        kinds, spots, keys = [], [], []
        for k in range(dp * own):
            if k < n_in:
                r, c = divmod(k, in_cols)
                if c < attn_cols:
                    kinds.append(0), spots.append((0, r, c)), keys.append((0, k))
                else:
                    c -= attn_cols
                    kinds.append(2), spots.append((2, r, c)), keys.append((2, c % units / units, k))
            else:
                r, c = divmod(k - n_in, rows)
                if r < out_attn_rows:
                    kinds.append(1), spots.append((1, r, c)), keys.append((1, k))
                else:
                    kinds.append(2), spots.append((3, r - out_attn_rows, c))
                    keys.append((2, c / rows, k))
        self.order = np.zeros((dp, own), np.int32)
        for d in range(dp):
            self.order[d] = sorted(range(own), key=lambda l: keys[d * own + l])
        count = np.array(kinds).reshape(dp, own)
        first = int((count == 0).sum(1).max())
        second = int((count <= 1).sum(1).max())
        bounds = [0, first, max(first, second), own]
        self.chunks = [(a, b - a) for a, b in zip(bounds[:-1], bounds[1:]) if b > a]
        self.table = []
        for p, d in enumerate(self.ring):
            for j, l in enumerate(self.order[d]):
                (x,) = [i for i, (a, n) in enumerate(self.chunks) if a <= j < a + n]
                a, n = self.chunks[x]
                self.table.append(spots[d * own + int(l)] + (x, p * n + j - a))
        mixed = [p for p, d in enumerate(self.ring) if (count[d] == 1).any()]
        last, size = len(self.chunks) - 1, self.chunks[-1][1]
        late = [t for t in self.table if t[3] == last]
        self.first_late = {}
        for m, cols in ((2, units), (3, rows)):
            own_late = [c % cols for i, r, c, x, s in late if i == m and s // size not in mixed]
            self.first_late[m] = min(own_late, default=cols)
        self.strips = sorted(
            (m, r, c, s)
            for m, r, c, x, s in late
            if m >= 2 and s // size in mixed and c % (units if m == 2 else rows) < self.first_late[m]
        )

    def of_chunk(self, x, matrix):
        rows = [(s, r, c) for m, r, c, y, s in self.table if y == x and m == matrix]
        return np.array(sorted(rows), np.int32).reshape(-1, 3)

    def of_matrix(self, matrix, rows, cols):
        out = np.zeros((cols, rows, 2), np.int32)
        for m, r, c, x, s in self.table:
            if m == matrix:
                out[c, r] = (x, s)
        return out


ANY = pl.BlockSpec(memory_space=pl.ANY)
SMEM = pl.BlockSpec(memory_space=pltpu.SMEM)
VMEM = pl.BlockSpec(memory_space=pltpu.VMEM)


def sort_blocks(weights, order, chunks):
    block = weights.shape[1:]

    def body(order_ref, w_ref, *outs):
        for (start, count), out in zip(chunks, outs):

            def one(j, carry, start=start, out=out):
                out[j] = w_ref[order_ref[start + j]].astype(LOW)
                return carry

            lax.fori_loop(0, count, one, 0)

    return pl.pallas_call(
        body,
        out_shape=[jax.ShapeDtypeStruct((n,) + block, LOW) for _, n in chunks],
        in_specs=[SMEM, VMEM],
        out_specs=[VMEM] * len(chunks),
        compiler_params=pltpu.CompilerParams(vmem_limit_bytes=VMEM_LIMIT),
        name="sort_blocks",
    )(order, weights)


def place_blocks(gathered, tables, shapes, partial):
    block = gathered.shape[-1]
    used = [i for i, t in enumerate(tables) if len(t)]
    if not used:
        return partial
    count = sum(len(tables[i]) for i in used)
    known = [i for i in used if partial[i] is not None]

    def body(*refs):
        table_refs = refs[: len(used)]
        src = refs[len(used)]
        outs = refs[len(used) + 1 + len(known) : -3]
        stage, sem_in, sem_out = refs[-3:]
        at = 0
        for i, table_ref in zip(used, table_refs):

            def load(j, carry, table_ref=table_ref, at=at):
                pltpu.make_async_copy(src.at[table_ref[3 * j]], stage.at[at + j], sem_in).start()
                return carry

            lax.fori_loop(0, len(tables[i]), load, 0)
            at += len(tables[i])
        pltpu.make_async_copy(stage, stage, sem_in).wait()
        at = 0
        for i, table_ref, out in zip(used, table_refs, outs):

            def put(j, carry, table_ref=table_ref, out=out, at=at):
                row = pl.multiple_of(table_ref[3 * j + 1] * block, block)
                col = pl.multiple_of(table_ref[3 * j + 2] * block, block)
                pltpu.make_async_copy(
                    stage.at[at + j], out.at[pl.ds(row, block), pl.ds(col, block)], sem_out
                ).start()
                return carry

            lax.fori_loop(0, len(tables[i]), put, 0)
            at += len(tables[i])
        pltpu.make_async_copy(stage, stage, sem_out).wait()

    results = pl.pallas_call(
        body,
        out_shape=[jax.ShapeDtypeStruct(shapes[i], LOW) for i in used],
        in_specs=[SMEM] * len(used) + [ANY] * (1 + len(known)),
        out_specs=[ANY] * len(used),
        input_output_aliases={len(used) + 1 + j: used.index(i) for j, i in enumerate(known)},
        scratch_shapes=[
            pltpu.VMEM((count, block, block), LOW),
            pltpu.SemaphoreType.DMA,
            pltpu.SemaphoreType.DMA,
        ],
        compiler_params=pltpu.CompilerParams(vmem_limit_bytes=VMEM_LIMIT),
        cost_estimate=pl.CostEstimate(
            flops=0, bytes_accessed=4 * count * block * block, transcendentals=0
        ),
        name="place_blocks",
    )(
        *[jnp.asarray(tables[i].reshape(-1)) for i in used],
        gathered,
        *[partial[i] for i in known],
    )
    merged = list(partial)
    for i, value in zip(used, results):
        merged[i] = value
    return merged


def fill(scratch, pieces, order_ref):
    count = pieces[0].shape[0]
    for i, piece in enumerate(pieces):
        if order_ref is None:
            scratch[i * count : (i + 1) * count] = piece[...]
        else:
            scratch[pl.ds(pl.multiple_of(order_ref[i] * count, count), count)] = piece[...]


def grad_blocks(
    left, rights, order, pairs, table, wide, buffers, sizes, block, span=None, done=()
):
    tokens, height = left.shape
    by_column = len(rights) > 1 and rights[0].shape[0] == tokens
    width = sum(x.shape[-1] for x in rights) if by_column else rights[0].shape[-1]
    if pairs:
        width *= 2
    rows, cols = height // block, width // block
    if pairs:
        table = np.stack([table[: cols // 2], table[cols // 2 :]], 1).reshape(table.shape)
        wide = 2
    first, end = (0, cols // wide) if span is None else span
    steps = end - first
    if steps <= 0:
        return buffers
    assert not by_column or wide == 1
    per_step = rows * wide
    targets = [
        [(j, x, spot) for j, (x, spot) in enumerate(step) if (x, spot) not in done]
        for step in table.reshape(cols // wide, per_step, 2).tolist()[first:end]
    ]
    assert all(targets)
    used = sorted({x for step in targets for _, x, _ in step})
    known = [x for x in used if buffers[x] is not None]
    n_order = 0 if order is None else 1
    joined = len(rights) > 1
    first_known = n_order + 1 + len(rights)
    first_out = first_known + len(known)

    def body(*refs):
        left_ref = refs[n_order]
        right_refs = refs[n_order + 1 : first_known]
        outs = refs[first_out : first_out + len(used)]
        stage, sems = refs[first_out + len(used) : first_out + len(used) + 2]
        t = pl.program_id(0)
        slot = lax.rem(t, 2)
        if joined:
            right_ref = refs[-1]
            if by_column:
                step = 0
                for piece in right_refs:
                    for at in range(0, piece.shape[1], block):

                        @pl.when(t + first == step)
                        def _(piece=piece, at=at):
                            right_ref[...] = piece[:, at : at + block]

                        step += 1
            else:
                fill(right_ref, right_refs, refs[0] if n_order else None)
            taken = right_ref[...]
        elif pairs:
            taken = jnp.concatenate([right_refs[0][0], right_refs[0][1]], axis=1)
        else:
            taken = right_refs[0][...]

        def finish(step):
            sent = stage.at[step % 2, : len(targets[step])]
            pltpu.make_async_copy(sent, sent, sems.at[step % 2]).wait()

        for step in range(2, steps):

            @pl.when(t == step)
            def _(step=step):
                finish(step - 2)

        def some(i, carry):
            at = pl.multiple_of(i * (few * block), block)
            part = lax.dot_general(
                left_ref[:, pl.ds(at, few * block)],
                taken,
                (((0,), (0,)), ((), ())),
                preferred_element_type=F32,
            ).astype(LOW)
            for r in range(few):
                for c in range(wide):
                    stage[slot, c * rows + i * few + r] = part[
                        r * block : (r + 1) * block, c * block : (c + 1) * block
                    ]
            return carry

        few = rows // 2 if rows % 2 == 0 else rows
        lax.fori_loop(0, rows // few, some, 0)
        for step in range(steps):

            @pl.when(t == step)
            def _(step=step):
                for j, x, spot in targets[step]:
                    pltpu.make_async_copy(
                        stage.at[step % 2, j], outs[used.index(x)].at[spot], sems.at[step % 2]
                    ).start()

        @pl.when(t == steps - 1)
        def _():
            for step in range(max(0, steps - 2), steps):
                finish(step)

    taken_width = wide * block
    if pairs:
        right_specs = [pl.BlockSpec((2, tokens, block), lambda j: (0, 0, first + j))]
    elif by_column:
        right_specs = [pl.BlockSpec(x.shape, lambda j: (0, 0)) for x in rights]
    else:
        right_specs = [
            pl.BlockSpec((x.shape[0], taken_width), lambda j: (0, first + j)) for x in rights
        ]
    results = pl.pallas_call(
        body,
        grid=(steps,),
        out_shape=[jax.ShapeDtypeStruct((sizes[x], block, block), LOW) for x in used],
        in_specs=[SMEM] * n_order
        + [pl.BlockSpec((tokens, height), lambda j: (0, 0))]
        + right_specs
        + [ANY] * len(known),
        out_specs=[ANY] * len(used),
        input_output_aliases={first_known + j: used.index(x) for j, x in enumerate(known)},
        scratch_shapes=[
            pltpu.VMEM((2, per_step, block, block), LOW),
            pltpu.SemaphoreType.DMA((2,)),
        ]
        + ([pltpu.VMEM((tokens, taken_width), LOW)] if joined else []),
        compiler_params=pltpu.CompilerParams(vmem_limit_bytes=VMEM_LIMIT),
        cost_estimate=pl.CostEstimate(
            flops=4 * tokens * height * wide * block * steps,
            bytes_accessed=2 * (tokens * (height + width) + height * width),
            transcendentals=0,
        ),
        name="grad_blocks",
    )(*([] if order is None else [order]), left, *rights, *[buffers[x] for x in known])
    merged = list(buffers)
    for x, value in zip(used, results):
        merged[x] = value
    return merged


def grad_strips(strips, buffer_size, block):
    def body(*refs):
        out, stage, sem = refs[-3:]
        at = 0
        for i, (_, _, _, half, blocks) in enumerate(strips):
            right = refs[2 * i + 1]
            part = lax.dot_general(
                refs[2 * i][...],
                right[...] if half is None else right[0],
                (((0,), (0,)), ((), ())),
                preferred_element_type=F32,
            ).astype(LOW)
            for c, spot in blocks:
                stage[at] = part[:, c * block : (c + 1) * block]
                pltpu.make_async_copy(stage.at[at], out.at[spot], sem).start()
                at += 1
        pltpu.make_async_copy(stage, stage, sem).wait()

    specs, values = [], []
    for left, row, right, half, blocks in strips:
        tokens = left.shape[0]
        wide = (max(c for c, _ in blocks) + 1) * block
        specs.append(pl.BlockSpec((tokens, block), lambda j, row=row: (0, row)))
        if half is None:
            specs.append(pl.BlockSpec((tokens, wide), lambda j: (0, 0)))
        else:
            specs.append(pl.BlockSpec((1, tokens, wide), lambda j, half=half: (half, 0, 0)))
        values += [left, right]
    count = sum(len(blocks) for *_, blocks in strips)
    return pl.pallas_call(
        body,
        grid=(1,),
        in_specs=specs,
        out_specs=ANY,
        out_shape=jax.ShapeDtypeStruct((buffer_size, block, block), LOW),
        scratch_shapes=[pltpu.VMEM((count, block, block), LOW), pltpu.SemaphoreType.DMA],
        compiler_params=pltpu.CompilerParams(vmem_limit_bytes=VMEM_LIMIT),
        cost_estimate=pl.CostEstimate(
            flops=4 * count * values[0].shape[0] * block**2,
            bytes_accessed=4 * count * block * values[0].shape[0],
            transcendentals=0,
        ),
        name="grad_strips",
    )(*values)


def feed_forward(pieces, weights, hidden_grad, block):
    share, width = pieces[0].shape
    rows = share * len(pieces)
    hidden = weights.shape[1] // 2
    steps = hidden // block

    def body(*refs):
        gate_w, up_w, grad_ref, hid_ref, out_ref, joined = refs[len(pieces) :]

        @pl.when(pl.program_id(0) == 0)
        def _():
            fill(joined, refs[: len(pieces)], None)

        both = jnp.dot(
            joined[...],
            jnp.concatenate([gate_w[...], up_w[...]], axis=1),
            preferred_element_type=F32,
        )
        gate, up = both[:, :block], both[:, block:]
        grad = grad_ref[...]
        sig = jax.nn.sigmoid(gate)
        act = gate * sig
        hid_ref[...] = (act * up).astype(LOW)
        out_ref[0] = (grad * up * sig * (1.0 + gate * (1.0 - sig))).astype(LOW)
        out_ref[1] = (grad * act).astype(LOW)

    return pl.pallas_call(
        body,
        grid=(steps,),
        in_specs=[pl.BlockSpec((share, width), lambda j: (0, 0))] * len(pieces)
        + [
            pl.BlockSpec((width, block), lambda j: (0, j)),
            pl.BlockSpec((width, block), lambda j: (0, steps + j)),
            pl.BlockSpec((rows, block), lambda j: (0, j)),
        ],
        out_specs=[
            pl.BlockSpec((rows, block), lambda j: (0, j)),
            pl.BlockSpec((2, rows, block), lambda j: (0, 0, j)),
            pl.BlockSpec((rows, width), lambda j: (0, 0)),
        ],
        out_shape=[
            jax.ShapeDtypeStruct((rows, hidden), LOW),
            jax.ShapeDtypeStruct((2, rows, hidden), LOW),
            jax.ShapeDtypeStruct((rows, width), LOW),
        ],
        compiler_params=pltpu.CompilerParams(vmem_limit_bytes=VMEM_LIMIT),
        cost_estimate=pl.CostEstimate(
            flops=4 * rows * width * hidden,
            bytes_accessed=2 * rows * width + 4 * width * hidden + 10 * rows * hidden,
            transcendentals=rows * hidden,
        ),
        name="feed_forward",
    )(*pieces, weights, weights, hidden_grad)


def project_rows(parts, weights, order, turned, tile):
    stacked = parts[0].ndim == 3
    rows = parts[0].shape[-2]
    half = rows // 2
    widths = [parts[0].shape[2]] * parts[0].shape[0] if stacked else [x.shape[1] for x in parts]
    starts = [sum(widths[:i]) for i in range(len(widths))]
    width = weights.shape[0] if turned else weights.shape[1]
    depth = sum(widths)
    share = rows // 4
    n_order = 0 if order is None else 1

    def body(*refs):
        part_refs = refs[n_order : n_order + len(parts)]
        w_ref, kept_ref, sent_ref = refs[n_order + len(parts) : n_order + len(parts) + 3]
        if n_order:
            joined = refs[-1]

            @pl.when(pl.program_id(0) == 0)
            def _():
                for i in range(4):
                    take = pl.ds(pl.multiple_of(refs[0][i] * share, share), share)
                    for part, at, size in zip(part_refs, starts, widths):
                        joined[i * share : (i + 1) * share, at : at + size] = part[take]

            pieces = [(joined[...], 0, depth)]
        elif stacked:
            pieces = [(part_refs[0][i], at, widths[i]) for i, at in enumerate(starts)]
        else:
            pieces = [(p[...], at, size) for p, at, size in zip(part_refs, starts, widths)]
        total = None
        for value, at, size in pieces:
            if turned:
                one = dot_turned(value, w_ref[:, at : at + size])
            else:
                one = dot(value, w_ref[at : at + size])
            total = one if total is None else total + one
        total = total.astype(LOW)
        kept_ref[...] = total[:half]
        sent_ref[...] = total[half:]

    whole = [pl.BlockSpec(x.shape, lambda j, n=x.ndim: (0,) * n) for x in parts]
    if turned:
        weight_spec = pl.BlockSpec((tile, depth), lambda j: (j, 0))
    else:
        weight_spec = pl.BlockSpec((depth, tile), lambda j: (0, j))
    kept, sent = pl.pallas_call(
        body,
        grid=(width // tile,),
        in_specs=[SMEM] * n_order + whole + [weight_spec],
        out_specs=[pl.BlockSpec((half, tile), lambda j: (0, j))] * 2,
        out_shape=[jax.ShapeDtypeStruct((half, width), LOW)] * 2,
        scratch_shapes=[pltpu.VMEM((rows, depth), LOW)] * n_order,
        compiler_params=pltpu.CompilerParams(vmem_limit_bytes=VMEM_LIMIT),
        cost_estimate=pl.CostEstimate(
            flops=2 * rows * depth * width,
            bytes_accessed=2 * (rows * depth + depth * width + rows * width),
            transcendentals=0,
        ),
        name="project_rows",
    )(*([order] if n_order else []), *parts, weights)
    return sent, kept


def down_back(grads, weights):
    rows, depth = grads.shape
    hidden = weights.shape[0]
    tile = 2 * LANES
    full, rest = divmod(hidden, tile)

    def body(g_ref, w_ref, o_ref):
        t = pl.program_id(0)

        @pl.when(t < full)
        def _():
            here = pl.ds(pl.multiple_of(t * tile, tile), tile)
            o_ref[...] = dot_turned(g_ref[...], w_ref[here])

        if rest:

            @pl.when(t == full)
            def _():
                o_ref[:, :rest] = dot_turned(g_ref[...], w_ref[full * tile :])

    return pl.pallas_call(
        body,
        grid=(full + (rest > 0),),
        in_specs=[
            pl.BlockSpec((rows, depth), lambda j: (0, 0)),
            pl.BlockSpec((hidden, depth), lambda j: (0, 0)),
        ],
        out_specs=pl.BlockSpec((rows, tile), lambda j: (0, j)),
        out_shape=jax.ShapeDtypeStruct((rows, hidden), F32),
        compiler_params=pltpu.CompilerParams(vmem_limit_bytes=VMEM_LIMIT),
        cost_estimate=pl.CostEstimate(
            flops=2 * rows * depth * hidden,
            bytes_accessed=2 * depth * (rows + hidden) + 4 * rows * hidden,
            transcendentals=0,
        ),
        name="down_back",
    )(grads, weights)


def to_heads(pieces, weights, order):
    share = pieces[0].shape[0]
    width = weights.shape[0]

    rows = share * len(pieces)

    def body(order_ref, *refs):
        w_ref, out_ref = refs[-2:]
        for i, piece in enumerate(refs[:-2]):
            put = pl.ds(pl.multiple_of(order_ref[i] * share, share), share)
            out_ref[put] = dot_turned(piece[...], w_ref[...]).astype(LOW)

    return pl.pallas_call(
        body,
        in_specs=[SMEM] + [VMEM] * (len(pieces) + 1),
        out_specs=VMEM,
        out_shape=jax.ShapeDtypeStruct((rows, width), LOW),
        compiler_params=pltpu.CompilerParams(vmem_limit_bytes=VMEM_LIMIT),
        cost_estimate=pl.CostEstimate(
            flops=2 * rows * width * weights.shape[1],
            bytes_accessed=2 * (rows + width) * weights.shape[1],
            transcendentals=0,
        ),
        name="to_heads",
    )(order, *pieces, weights)


LANES = 128
QUERIES = 256
LONGEST = 512


def turn(values, cos, sin):
    lane = lax.broadcasted_iota(jnp.int32, values.shape, 1)
    other = jnp.where(
        lane % HD < HD // 2,
        pltpu.roll(values, LANES - HD // 2, 1),
        pltpu.roll(values, HD // 2, 1),
    )
    return values * cos + other * sin


def key_tables(cos, sin):
    lane = lax.broadcasted_iota(jnp.int32, cos.shape, 1)
    return jnp.where(lane < HD, cos, 1.0), jnp.where(lane < HD, sin, 0.0)


def project_heads(inputs, weights, cos, sin):
    rows, depth = inputs.shape
    width = weights.shape[1]
    assert width % LANES == 0 and HD == 64

    def body(x_ref, w_ref, cos_ref, sin_ref, q_ref, kv_ref):
        t = pl.program_id(0)
        raw = dot(x_ref[...], w_ref[...])

        @pl.when(t < steps - 1)
        def _():
            q_ref[...] = turn(raw, cos_ref[...], sin_ref[...]).astype(LOW) * LOW(HD**-0.5)

        @pl.when(t == steps - 1)
        def _():
            kv_ref[...] = turn(raw, *key_tables(cos_ref[...], sin_ref[...])).astype(LOW)

    steps = width // LANES
    whole = pl.BlockSpec((rows, LANES), lambda j: (0, 0))
    return pl.pallas_call(
        body,
        grid=(steps,),
        in_specs=[
            pl.BlockSpec((rows, depth), lambda j: (0, 0)),
            pl.BlockSpec((depth, LANES), lambda j: (0, j)),
            whole,
            whole,
        ],
        out_specs=[pl.BlockSpec((rows, LANES), lambda j: (0, jnp.minimum(j, steps - 2))), whole],
        out_shape=[
            jax.ShapeDtypeStruct((rows, width - LANES), LOW),
            jax.ShapeDtypeStruct((rows, LANES), LOW),
        ],
        compiler_params=pltpu.CompilerParams(vmem_limit_bytes=VMEM_LIMIT),
        cost_estimate=pl.CostEstimate(
            flops=2 * rows * depth * width,
            bytes_accessed=2 * (rows * depth + depth * width + rows * width),
            transcendentals=0,
        ),
        name="project_heads",
    )(inputs, weights, cos, sin)


def keep_keys(padded, kv_ref):
    padded[:LONGEST] = jnp.zeros((LONGEST, LANES), LOW)
    padded[LONGEST:] = kv_ref[...]


def visible(start_ref, at):
    shape = (LONGEST + QUERIES, QUERIES)
    key = at - LONGEST + lax.broadcasted_iota(jnp.int32, shape, 0)
    query = at + lax.broadcasted_iota(jnp.int32, shape, 1)
    return (key >= start_ref[:, pl.ds(at, QUERIES)]) & (key <= query)


def attend(queries, kv, starts):
    rows, width = queries.shape
    groups = width // LANES

    def body(start_ref, q_ref, kv_ref, o_ref, log_ref, padded):
        @pl.when(pl.program_id(0) == 0)
        def _():
            keep_keys(padded, kv_ref)

        def one(i, carry):
            at = pl.multiple_of(i * QUERIES, QUERIES)
            here = pl.ds(at, QUERIES)
            seen = visible(start_ref, at)
            window = padded[pl.ds(at, LONGEST + QUERIES)]
            keys, values = window[:, :HD], window[:, HD:]
            for h in range(LANES // HD):
                query = q_ref[here, h * HD : (h + 1) * HD]
                scores = jnp.where(seen, dot_turned(keys, query), -1e30)
                top = jnp.max(scores, axis=0, keepdims=True)
                expo = jnp.exp(scores - top)
                total = jnp.sum(expo, axis=0, keepdims=True)
                probs = (expo * (1.0 / total)).astype(LOW)
                o_ref[here, h * HD : (h + 1) * HD] = lax.dot_general(
                    probs, values, (((0,), (0,)), ((), ())), preferred_element_type=F32
                ).astype(LOW)
                log_ref[0, h : h + 1, here] = top + jnp.log(total)
            return carry

        lax.fori_loop(0, rows // QUERIES, one, 0)

    column = pl.BlockSpec((rows, LANES), lambda j: (0, j))
    return pl.pallas_call(
        body,
        grid=(groups,),
        in_specs=[
            pl.BlockSpec((1, rows), lambda j: (0, 0)),
            column,
            pl.BlockSpec((rows, LANES), lambda j: (0, 0)),
        ],
        out_specs=[column, pl.BlockSpec((1, LANES // HD, rows), lambda j: (j, 0, 0))],
        out_shape=[
            jax.ShapeDtypeStruct((rows, width), LOW),
            jax.ShapeDtypeStruct((groups, LANES // HD, rows), F32),
        ],
        scratch_shapes=[pltpu.VMEM((LONGEST + rows, LANES), LOW)],
        compiler_params=pltpu.CompilerParams(vmem_limit_bytes=VMEM_LIMIT),
        cost_estimate=pl.CostEstimate(
            flops=30 * rows * rows * width,
            bytes_accessed=4 * rows * width,
            transcendentals=rows * rows * width // HD,
        ),
        name="attend",
    )(starts, queries, kv)


def attend_back(queries, kv, starts, logs, grads, cos, sin):
    rows, width = queries.shape
    groups = width // LANES

    def body(
        start_ref, q_ref, kv_ref, log_ref, g_ref, cos_ref, sin_ref, dq_ref, sum_ref, acc, padded
    ):
        @pl.when(pl.program_id(0) == 0)
        def _():
            keep_keys(padded, kv_ref)
            acc[...] = jnp.zeros_like(acc)

        def one(i, carry):
            at = pl.multiple_of(i * QUERIES, QUERIES)
            here = pl.ds(at, QUERIES)
            there = pl.ds(at, LONGEST + QUERIES)
            seen = visible(start_ref, at)
            window = padded[there]
            keys, values = window[:, :HD], window[:, HD:]
            parts = []
            key_part, value_part = 0.0, 0.0
            for h in range(LANES // HD):
                query = q_ref[here, h * HD : (h + 1) * HD]
                grad = g_ref[here, h * HD : (h + 1) * HD]
                scores = jnp.where(seen, dot_turned(keys, query), -1e30)
                probs = jnp.exp(scores - log_ref[0, h : h + 1, here])
                value_part += dot(probs.astype(LOW), grad)
                prob_grads = dot_turned(values, grad)
                inner = jnp.sum(probs * prob_grads, axis=0, keepdims=True)
                score_grads = (probs * (prob_grads - inner)).astype(LOW)
                key_part += dot(score_grads, query)
                parts.append(
                    lax.dot_general(
                        score_grads, keys, (((0,), (0,)), ((), ())), preferred_element_type=F32
                    )
                )
            acc[there] += jnp.concatenate([key_part, value_part], axis=1)
            dq_ref[here] = turn(
                jnp.concatenate(parts, axis=1) * HD**-0.5, cos_ref[here], -sin_ref[here]
            ).astype(LOW)
            return carry

        lax.fori_loop(0, rows // QUERIES, one, 0)

        @pl.when(pl.program_id(0) == groups - 1)
        def _():
            key_cos, key_sin = key_tables(cos_ref[...], sin_ref[...])
            sum_ref[...] = turn(acc[LONGEST:], key_cos, -key_sin).astype(LOW)

    column = pl.BlockSpec((rows, LANES), lambda j: (0, j))
    whole = pl.BlockSpec((rows, LANES), lambda j: (0, 0))
    return pl.pallas_call(
        body,
        grid=(groups,),
        in_specs=[
            pl.BlockSpec((1, rows), lambda j: (0, 0)),
            column,
            whole,
            pl.BlockSpec((1, LANES // HD, rows), lambda j: (j, 0, 0)),
            column,
            whole,
            whole,
        ],
        out_specs=[column, whole],
        out_shape=[
            jax.ShapeDtypeStruct((rows, width), LOW),
            jax.ShapeDtypeStruct((rows, LANES), LOW),
        ],
        scratch_shapes=[
            pltpu.VMEM((LONGEST + rows, LANES), F32),
            pltpu.VMEM((LONGEST + rows, LANES), LOW),
        ],
        compiler_params=pltpu.CompilerParams(vmem_limit_bytes=VMEM_LIMIT),
        cost_estimate=pl.CostEstimate(
            flops=80 * rows * rows * width,
            bytes_accessed=16 * rows * width,
            transcendentals=rows * rows * width // HD,
        ),
        name="attend_back",
    )(starts, queries, kv, logs, grads, cos, sin)


def shampoo(sums, places, factor, weights, ema, left, right, left_roots, right_roots, before):
    count, block, _ = sums.shape
    group = 2 if count % 2 == 0 else 1
    steps = count // group
    depth = min(4, steps)
    extra = [] if before is None else list(before)

    def mm(a, b, dims):
        return lax.dot_general(
            a.astype(LOW), b.astype(LOW), (dims, ((), ())), preferred_element_type=F32
        )

    def body(places_ref, g_ref, *refs):
        ins, outs = refs[:6], refs[6 + len(extra) : 11 + len(extra)]
        given, made, sem_in, sem_out = refs[11 + len(extra) :]

        def load(t, slot):
            for u in range(group):
                place = places_ref[t * group + u]
                for i, ref in enumerate(ins):
                    pltpu.make_async_copy(
                        ref.at[place], given.at[slot, u, i], sem_in.at[slot]
                    ).start()

        def wait(buffer, slot, sems):
            pltpu.make_async_copy(buffer.at[slot], buffer.at[slot], sems.at[slot]).wait()

        for t in range(depth):
            load(t, t)

        def step(t, carry):
            slot = lax.rem(t, depth)
            wait(given, slot, sem_in)

            @pl.when(t >= depth)
            def _():
                wait(made, slot, sem_out)

            both = 0.5 * factor * factor
            for u in range(group):
                low = g_ref[t * group + u]
                made[slot, u, 0] = low.astype(F32) * factor
                made[slot, u, 3] = 0.5 * given[slot, u, 2] + both * mm(low, low, ((1,), (1,)))
                made[slot, u, 4] = 0.5 * given[slot, u, 3] + both * mm(low, low, ((0,), (0,)))
                part = mm(low, given[slot, u, 5], ((1,), (0,))) * factor
                fresh = given[slot, u, 0] - weight_rate * mm(given[slot, u, 4], part, ((1,), (0,)))
                made[slot, u, 1] = fresh
                made[slot, u, 2] = (
                    average_decay * given[slot, u, 1] + (1.0 - average_decay) * fresh
                )
            for u in range(group):
                place = places_ref[t * group + u]
                for i, ref in enumerate(outs):
                    pltpu.make_async_copy(
                        made.at[slot, u, i], ref.at[place], sem_out.at[slot]
                    ).start()

            @pl.when(t + depth < steps)
            def _():
                load(t + depth, slot)

            return carry

        lax.fori_loop(0, steps, step, 0)
        for t in range(steps - depth, steps):
            wait(made, t % depth, sem_out)

    return pl.pallas_call(
        body,
        out_shape=[jax.ShapeDtypeStruct(weights.shape, F32)] * 5,
        in_specs=[SMEM, VMEM] + [ANY] * (6 + len(extra)),
        out_specs=[ANY] * 5,
        input_output_aliases={8 + i: i for i in range(len(extra))},
        scratch_shapes=[
            pltpu.VMEM((depth, group, 6, block, block), F32),
            pltpu.VMEM((depth, group, 5, block, block), F32),
            pltpu.SemaphoreType.DMA((depth,)),
            pltpu.SemaphoreType.DMA((depth,)),
        ],
        compiler_params=pltpu.CompilerParams(vmem_limit_bytes=VMEM_LIMIT),
        cost_estimate=pl.CostEstimate(
            flops=8 * count * block**3,
            bytes_accessed=46 * count * block * block,
            transcendentals=0,
        ),
        name="shampoo",
    )(places, sums, weights, ema, left, right, left_roots, right_roots, *extra)


def rows_call(body, ins, outs, name, step=64, work=10):
    rows = max(x.shape[0] for x in ins)

    def spec(x):
        if x.shape[0] == rows:
            return pl.BlockSpec((step, x.shape[1]), lambda j: (j, 0))
        return pl.BlockSpec(x.shape, lambda j: (0, 0))

    return pl.pallas_call(
        body,
        grid=(rows // step,),
        in_specs=[spec(x) for x in ins],
        out_specs=[spec(x) for x in outs],
        out_shape=outs,
        compiler_params=pltpu.CompilerParams(vmem_limit_bytes=VMEM_LIMIT),
        cost_estimate=pl.CostEstimate(
            flops=work * rows * ins[0].shape[1],
            bytes_accessed=sum(x.size * x.dtype.itemsize for x in list(ins) + list(outs)),
            transcendentals=0,
        ),
        name=name,
    )(*ins)


def add_near(kept, got):
    share = kept.shape[0] // 2
    width = kept.shape[1]
    step = 64

    def body(a_ref, c_ref, b_ref, d_ref, mine_ref, other_ref):
        mine_ref[...] = a_ref[...].astype(F32) + b_ref[...].astype(F32)
        other_ref[...] = (c_ref[...].astype(F32) + d_ref[...].astype(F32)).astype(LOW)

    first = pl.BlockSpec((step, width), lambda j: (j, 0))
    second = pl.BlockSpec((step, width), lambda j: (share // step + j, 0))
    return pl.pallas_call(
        body,
        grid=(share // step,),
        in_specs=[first, second, first, second],
        out_specs=[first] * 2,
        out_shape=[
            jax.ShapeDtypeStruct((share, width), F32),
            jax.ShapeDtypeStruct((share, width), LOW),
        ],
        compiler_params=pltpu.CompilerParams(vmem_limit_bytes=VMEM_LIMIT),
        cost_estimate=pl.CostEstimate(
            flops=2 * share * width, bytes_accessed=14 * share * width, transcendentals=0
        ),
        name="add_near",
    )(kept, kept, got, got)


def second_norm(tokens, mine, got, gain):
    def body(x_ref, a_ref, b_ref, gain_ref, middle_ref, low_ref):
        middle = x_ref[...].astype(F32) + (a_ref[...] + b_ref[...].astype(F32))
        middle_ref[...] = middle
        scale = lax.rsqrt(jnp.mean(middle * middle, axis=-1, keepdims=True) + 1e-05)
        low_ref[...] = (middle * scale * gain_ref[...]).astype(LOW)

    return rows_call(
        body,
        [tokens, mine, got, gain],
        [jax.ShapeDtypeStruct(tokens.shape, F32), jax.ShapeDtypeStruct(tokens.shape, LOW)],
        "second_norm",
    )


def first_norm(tokens, gain):
    def body(x_ref, gain_ref, low_ref):
        x = x_ref[...].astype(F32)
        scale = lax.rsqrt(jnp.mean(x * x, axis=-1, keepdims=True) + 1e-05)
        low_ref[...] = (x * scale * gain_ref[...]).astype(LOW)

    return rows_call(
        body,
        [tokens, gain],
        [jax.ShapeDtypeStruct(tokens.shape, LOW)],
        "first_norm",
    )[0]


def norm_back(values, mine, got, gain, residual):
    def body(x_ref, a_ref, b_ref, gain_ref, r_ref, out_ref, low_ref, sum_ref):
        x = x_ref[...].astype(F32)
        grad = a_ref[...] + b_ref[...].astype(F32)
        scale = lax.rsqrt(jnp.mean(x * x, axis=-1, keepdims=True) + 1e-05)
        unit = x * scale
        scaled = grad * gain_ref[...]
        out = r_ref[...].astype(F32) + scale * (
            scaled - unit * jnp.mean(scaled * unit, axis=-1, keepdims=True)
        )
        out_ref[...] = out
        low_ref[...] = out.astype(LOW)

        @pl.when(pl.program_id(0) == 0)
        def _():
            sum_ref[...] = jnp.zeros_like(sum_ref)

        sum_ref[...] += jnp.sum(grad * unit, axis=0, keepdims=True)

    shape = values.shape
    return rows_call(
        body,
        [values, mine, got, gain, residual],
        [
            jax.ShapeDtypeStruct(shape, F32),
            jax.ShapeDtypeStruct(shape, LOW),
            jax.ShapeDtypeStruct((1, shape[1]), F32),
        ],
        "norm_back",
        work=1000000,
    )


def doc_positions(doc_ids):
    length = doc_ids.shape[-1]
    offsets = jnp.arange(length, dtype=jnp.int32)
    starts = jnp.concatenate(
        [jnp.ones(doc_ids.shape[:-1] + (1,), jnp.bool_), doc_ids[..., 1:] != doc_ids[..., :-1]],
        axis=-1,
    )
    first_index = lax.cummax(jnp.where(starts, offsets, 0), axis=doc_ids.ndim - 1)
    return offsets - first_index


def rope_tables(positions, head_size):
    half_size = head_size // 2
    exponent = jnp.arange(half_size, dtype=F32) * (2.0 / head_size)
    inverse = jnp.power(F32(10000.0), -exponent)
    angles = positions.astype(F32)[..., None] * inverse
    cos, sin = jnp.cos(angles), jnp.sin(angles)
    repeats = LANES // head_size
    return (
        jnp.concatenate([cos, cos] * repeats, axis=-1),
        jnp.concatenate([-sin, sin] * repeats, axis=-1),
    )


def after(value, *others):
    return lax.optimization_barrier((value,) + others)[0]


def dot(left, right):
    return jnp.dot(left, right, preferred_element_type=F32)


def dot_turned(left, right):
    return lax.dot_general(left, right, (((1,), (1,)), ((), ())), preferred_element_type=F32)


EXCHANGE = (0, 2, 1, 3)


def on_device(
    tokens_in,
    cotangent,
    select_mask,
    doc_ids,
    norm_gains,
    weight_blocks,
    ema_blocks,
    left_stats,
    right_stats,
    left_roots,
    right_roots,
):
    mp_count = lax.axis_size("mp")
    dp_count = lax.axis_size("dp")
    sequences, length, model_width = tokens_in.shape
    assert sequences == 1 and mp_count == 4 and dp_count & (dp_count - 1) == 0
    rows = sequences * length
    own, block, _ = weight_blocks.shape
    query_cols = HEADS * HD // mp_count
    key_cols = KV_HEADS * HD // mp_count
    hidden_cols = FF // mp_count
    assert KV_HEADS == mp_count and length % QUERIES == 0
    row_blocks = model_width // block
    attn_blocks = (query_cols + 2 * key_cols) // block
    hidden_blocks = hidden_cols // block
    in_blocks = attn_blocks + 2 * hidden_blocks
    out_attn_blocks = query_cols // block
    share = rows // mp_count
    m_index = lax.axis_index("mp")
    d_index = lax.axis_index("dp")

    plan = Layout(dp_count, own, row_blocks, attn_blocks, in_blocks, out_attn_blocks)
    order = lax.dynamic_slice_in_dim(jnp.asarray(plan.order), d_index, 1, 0).reshape(-1)
    shapes = [
        (model_width, attn_blocks * block),
        (query_cols, model_width),
        (model_width, 2 * hidden_cols),
        (hidden_cols, model_width),
    ]

    def partner(values, bit):
        return lax.ppermute(values, "mp", [(i, i ^ bit) for i in range(mp_count)])

    def true_share(values, group):
        return lax.dynamic_slice_in_dim(values, (m_index ^ group) * share, share, 0)

    def to_exchange(values):
        return jnp.concatenate([true_share(values, g) for g in EXCHANGE], axis=0)

    def to_true(parts):
        by_group = [parts[EXCHANGE.index(g)] for g in range(4)]
        low, high = m_index & 1, m_index & 2
        pairs = []
        for a, b in ((0, 1), (2, 3)):
            pairs.append(
                (
                    jnp.where(low == 0, by_group[a], by_group[b]),
                    jnp.where(low == 0, by_group[b], by_group[a]),
                )
            )
        flat = []
        for first, second in ((0, 1), (1, 0)):
            for i in range(2):
                flat.append(jnp.where(high == 0, pairs[first][i], pairs[second][i]))
        return jnp.concatenate(flat, axis=0)

    def near_sum(sent, kept):
        return add_near(kept, partner(sent, 1))

    def spread_share(mine, *cover):
        far = partner(mine, 2)
        near = partner(mine, 1)
        if cover:
            far = after(far, *cover)
        return [mine, far, near, partner(far, 1)]

    sorted_low = sort_blocks(weight_blocks, order, plan.chunks)
    gathered = [
        lax.all_gather(chunk, "dp", axis=0, tiled=True, axis_index_groups=[plan.ring])
        for chunk in sorted_low
    ]
    none = np.zeros((0, 3), np.int32)
    last = len(gathered) - 1

    def place(x, source, which, matrices):
        tables = [plan.of_chunk(x, i) if i in which else none for i in range(4)]
        return place_blocks(source, tables, shapes, matrices)

    matrices = place(0, gathered[0], (0, 1, 2, 3), [None] * 4)
    w_qkv = matrices[0]
    if last >= 1:
        matrices = place(1, gathered[1], (1,), matrices)
    w_attn_out = matrices[1]

    positions = doc_positions(doc_ids)
    starts = jnp.arange(length, dtype=jnp.int32)[None] - positions
    cos, sin = rope_tables(positions[0], HD)

    tokens_low = tokens_in.reshape(rows, model_width)
    first_in = first_norm(tokens_low, norm_gains[:1])
    out_grad = cotangent.reshape(rows, model_width) * select_mask.astype(LOW).reshape(rows, 1)
    own_tokens = true_share(tokens_low, 0)
    own_grad = true_share(out_grad, 0)
    mlp_grad = to_exchange(out_grad)
    tokens_local = to_exchange(tokens_low)
    unit_scale = lax.rsqrt(
        jnp.mean(jnp.square(tokens_local.astype(F32)), axis=-1, keepdims=True) + 1e-05
    )

    shares = (m_index ^ jnp.array(EXCHANGE, jnp.int32)).astype(jnp.int32)
    queries, kv = project_heads(first_in, w_qkv, cos, sin)
    kv, mlp_grad, own_tokens, own_grad, tokens_local, unit_scale = lax.optimization_barrier(
        (kv, mlp_grad, own_tokens, own_grad, tokens_local, unit_scale)
    )
    mixed, logs = attend(queries, kv, starts)
    attended_sent, attended_kept = project_rows([mixed], w_attn_out, shares, False, 512)
    mine, other = near_sum(attended_sent, attended_kept)
    if last >= 1:
        matrices = place(1, after(gathered[1], other), (2, 3), matrices)
        mine, *matrices[2:] = lax.optimization_barrier((mine, *matrices[2:]))
    middle, second_low = second_norm(own_tokens, mine, partner(other, 2), norm_gains[1:])
    if last >= 2:
        matrices = place(2, after(gathered[2], second_low), (2, 3), matrices)
    w_gateup, w_down = matrices[2:]
    hidden_grad = down_back(mlp_grad, w_down)
    second_pieces = spread_share(second_low, hidden_grad)
    hidden, gateup_grad, second_in = feed_forward(second_pieces, w_gateup, hidden_grad, block)

    second_sent, second_kept = project_rows([gateup_grad], w_gateup, None, True, 256)
    sizes = [dp_count * n for _, n in plan.chunks]
    sums = [None] * len(sizes)
    reduced = [None] * len(sizes)

    def scatter(x):
        reduced[x] = lax.psum_scatter(
            sums[x], "dp", scatter_dimension=0, tiled=True, axis_index_groups=[plan.ring]
        )

    def known(values):
        return [x for x in values if x is not None]

    cuts = {2: 0, 3: 0}
    sent = set()
    if last >= 2:
        cuts = {2: plan.first_late[2], 3: plan.first_late[3] // 2}
        sent = {(last, spot) for *_, spot in plan.strips}
    if sent:
        strips = {}
        for matrix, r, c, spot in plan.strips:
            half = c // hidden_blocks if matrix == 2 else None
            at = c if half is None else c % hidden_blocks
            strips.setdefault((matrix, r, half), []).append((at, spot))
        sums[last] = grad_strips(
            [
                (
                    after(second_in, second_sent) if matrix == 2 else after(hidden, second_sent),
                    r,
                    gateup_grad if matrix == 2 else mlp_grad,
                    half,
                    blocks,
                )
                for (matrix, r, half), blocks in strips.items()
            ],
            sizes[last],
            block,
        )

    def down_grads(sums, hidden, span):
        table = plan.of_matrix(3, hidden_blocks, row_blocks)
        return grad_blocks(
            hidden, [mlp_grad], None, False, table, 2, sums, sizes, block, span, sent
        )

    def gateup_grads(sums, second_in, span):
        table = plan.of_matrix(2, row_blocks, 2 * hidden_blocks)
        return grad_blocks(
            second_in, [gateup_grad], None, True, table, 2, sums, sizes, block, span, sent
        )

    sums = down_grads(sums, after(hidden, second_sent), (cuts[3], row_blocks // 2))
    mine, other = near_sum(second_sent, after(second_kept, *known(sums)))
    sums = gateup_grads(sums, after(second_in, other), (cuts[2], hidden_blocks))
    if last >= 2:
        scatter(2)
    got = partner(other, 2)
    mine = after(mine, *known(sums[:2]))
    middle_grad, attn_low, second_gain = norm_back(
        middle, mine, got, norm_gains[1:], own_grad
    )
    sums = gateup_grads(sums, after(second_in, attn_low), (0, cuts[2]))
    sums = down_grads(sums, after(hidden, attn_low), (0, cuts[3]))
    attn_grad = spread_share(attn_low, *known(sums[:2]))
    sums = grad_blocks(
        mixed,
        attn_grad,
        shares,
        False,
        plan.of_matrix(1, out_attn_blocks, row_blocks),
        4,
        sums,
        sizes,
        block,
    )
    if last >= 1:
        scatter(1)

    feed_sent, feed_kept = project_rows(
        [after(hidden, *known(sums[:2]))], w_down, None, False, 512
    )
    feed_mine, feed_other = near_sum(feed_sent, feed_kept)
    mixed_grad = to_heads(attn_grad, after(w_attn_out, feed_other), shares)
    query_grad, kv_grad = attend_back(queries, kv, starts, logs, mixed_grad, cos, sin)
    feed_part = after(feed_mine, query_grad) + partner(feed_other, 2).astype(F32)
    out_low = (middle + feed_part).astype(LOW)
    qkv_grads = [query_grad, kv_grad]
    first_sent, first_kept = project_rows(
        [after(query_grad, out_low), kv_grad], w_qkv, shares, True, 512
    )
    mine, other = near_sum(first_sent, first_kept)

    half = rows // 2
    first_gain = sum(
        jnp.sum(part.astype(F32) * (x.astype(F32) * scale), axis=0, keepdims=True)
        for part, x, scale in (
            (first_kept, tokens_local[:half], unit_scale[:half]),
            (first_sent, tokens_local[half:], unit_scale[half:]),
        )
    )
    gain_sums = jnp.concatenate([first_gain, second_gain], axis=0)
    gain_sums = gain_sums + partner(gain_sums, 2)
    other = after(other, gain_sums)
    sums = grad_blocks(
        after(first_in, other),
        qkv_grads,
        None,
        False,
        plan.of_matrix(0, row_blocks, attn_blocks),
        1,
        sums,
        sizes,
        block,
    )
    scatter(0)
    factor = float(rows * dp_count) ** (-0.5)

    def update(x, state, *others):
        start, count = plan.chunks[x]
        return shampoo(
            reduced[x],
            after(lax.slice_in_dim(order, start, start + count), *others),
            factor,
            weight_blocks,
            ema_blocks,
            left_stats,
            right_stats,
            left_roots,
            right_roots,
            state,
        )

    _, input_low, _ = norm_back(
        own_tokens,
        after(mine, sums[0]),
        partner(other, 2),
        norm_gains[:1],
        middle_grad,
    )
    state = None
    if last >= 2:
        state = update(2, state, input_low)
    if last >= 1:
        state = update(1, state, input_low)
    gain_sums = after(gain_sums, input_low, *(state or ()))
    gain_sums = gain_sums + partner(gain_sums, 1)
    bit = 1
    while bit < dp_count:
        gain_sums = gain_sums + lax.ppermute(
            gain_sums, "dp", [(i, i ^ bit) for i in range(dp_count)]
        )
        bit *= 2
    input_parts = spread_share(input_low, *(state or ()))
    gain_share = model_width // dp_count
    gain_grads = factor * lax.dynamic_slice_in_dim(gain_sums, d_index * gain_share, gain_share, 1)
    old_gains = lax.dynamic_slice_in_dim(norm_gains, d_index * gain_share, gain_share, 1)
    new_gains = old_gains - gain_rate * gain_grads
    out_parts = spread_share(after(out_low, input_low), *(state or ()))
    block_out = to_true(out_parts).reshape(sequences, length, model_width)
    input_grad = to_true(input_parts).astype(F32).reshape(sequences, length, model_width)
    grads, new_weights, new_ema, new_left, new_right = update(
        0, state, input_grad, block_out, new_gains
    )
    return (
        block_out,
        input_grad,
        grads,
        new_weights,
        new_ema,
        new_left,
        new_right,
        gain_grads,
        new_gains,
    )


def solution(mesh):
    in_specs = (
        P("dp", None, None),
        P("dp", None, None),
        P("dp", None),
        P("dp", None),
        P(),
        P(("dp", "mp"), None, None),
        P(("dp", "mp"), None, None),
        P(("dp", "mp"), None, None),
        P(("dp", "mp"), None, None),
        P(("dp", "mp"), None, None),
        P(("dp", "mp"), None, None),
    )
    out_specs = (
        P("dp", None, None),
        P("dp", None, None),
        P(("dp", "mp"), None, None),
        P(("dp", "mp"), None, None),
        P(("dp", "mp"), None, None),
        P(("dp", "mp"), None, None),
        P(("dp", "mp"), None, None),
        P(None, "dp"),
        P(None, "dp"),
    )
    return jax.shard_map(
        on_device, mesh=mesh, in_specs=in_specs, out_specs=out_specs, check_vma=False
    )
```

```python
import functools

import jax
import jax.numpy as jnp
import numpy as np
from jax import lax
from jax.experimental import pallas as pl
from jax.experimental.pallas import tpu as pltpu
from jax.sharding import PartitionSpec as P

HEADS = 32
KV_HEADS = 4
HD = 64
FF = 5632
LOW = jnp.bfloat16
F32 = jnp.float32

weight_rate = 1.0
gain_rate = 0.2
average_decay = 0.9
VMEM_LIMIT = 60 * 1024 * 1024


def ring_order(count):
    return list(range(0, count, 2)) + list(range(1, count, 2))[::-1]


class Layout:
    def __init__(self, dp, own, rows, attn_cols, in_cols, out_attn_rows):
        self.dp, self.own = dp, own
        self.ring = ring_order(dp)
        n_in = rows * in_cols
        units = (in_cols - attn_cols) // 2
        kinds, spots, keys = [], [], []
        for k in range(dp * own):
            if k < n_in:
                r, c = divmod(k, in_cols)
                if c < attn_cols:
                    kinds.append(0), spots.append((0, r, c)), keys.append((0, k))
                else:
                    c -= attn_cols
                    kinds.append(2), spots.append((2, r, c)), keys.append((2, c % units / units, k))
            else:
                r, c = divmod(k - n_in, rows)
                if r < out_attn_rows:
                    kinds.append(1), spots.append((1, r, c)), keys.append((1, k))
                else:
                    kinds.append(2), spots.append((3, r - out_attn_rows, c))
                    keys.append((2, c / rows, k))
        self.order = np.zeros((dp, own), np.int32)
        for d in range(dp):
            self.order[d] = sorted(range(own), key=lambda l: keys[d * own + l])
        count = np.array(kinds).reshape(dp, own)
        first = int((count == 0).sum(1).max())
        second = int((count <= 1).sum(1).max())
        bounds = [0, first, max(first, second), own]
        self.chunks = [(a, b - a) for a, b in zip(bounds[:-1], bounds[1:]) if b > a]
        self.table = []
        for p, d in enumerate(self.ring):
            for j, l in enumerate(self.order[d]):
                (x,) = [i for i, (a, n) in enumerate(self.chunks) if a <= j < a + n]
                a, n = self.chunks[x]
                self.table.append(spots[d * own + int(l)] + (x, p * n + j - a))
        mixed = [p for p, d in enumerate(self.ring) if (count[d] == 1).any()]
        last, size = len(self.chunks) - 1, self.chunks[-1][1]
        late = [t for t in self.table if t[3] == last]
        self.first_late = {}
        for m, cols in ((2, units), (3, rows)):
            own_late = [c % cols for i, r, c, x, s in late if i == m and s // size not in mixed]
            self.first_late[m] = min(own_late, default=cols)
        self.strips = sorted(
            (m, r, c, s)
            for m, r, c, x, s in late
            if m >= 2 and s // size in mixed and c % (units if m == 2 else rows) < self.first_late[m]
        )

    def of_chunk(self, x, matrix):
        rows = [(s, r, c) for m, r, c, y, s in self.table if y == x and m == matrix]
        return np.array(sorted(rows), np.int32).reshape(-1, 3)

    def of_matrix(self, matrix, rows, cols):
        out = np.zeros((cols, rows, 2), np.int32)
        for m, r, c, x, s in self.table:
            if m == matrix:
                out[c, r] = (x, s)
        return out


ANY = pl.BlockSpec(memory_space=pl.ANY)
SMEM = pl.BlockSpec(memory_space=pltpu.SMEM)
VMEM = pl.BlockSpec(memory_space=pltpu.VMEM)


def sort_blocks(weights, order, chunks):
    block = weights.shape[1:]
    total = sum(n for _, n in chunks)
    begin = chunks[0][0]

    def body(order_ref, w_ref, *refs):
        outs, (given, sem) = refs[: len(chunks)], refs[len(chunks) :]

        def load(j, carry):
            pltpu.make_async_copy(w_ref.at[order_ref[begin + j]], given.at[j], sem).start()
            return carry

        lax.fori_loop(0, total, load, 0)
        pltpu.make_async_copy(given, given, sem).wait()
        for (start, count), out in zip(chunks, outs):

            def one(j, carry, start=start, out=out):
                out[j] = given[start - begin + j].astype(LOW)
                return carry

            lax.fori_loop(0, count, one, 0)

    return pl.pallas_call(
        body,
        out_shape=[jax.ShapeDtypeStruct((n,) + block, LOW) for _, n in chunks],
        in_specs=[SMEM, ANY],
        out_specs=[VMEM] * len(chunks),
        scratch_shapes=[pltpu.VMEM((total,) + block, F32), pltpu.SemaphoreType.DMA],
        compiler_params=pltpu.CompilerParams(vmem_limit_bytes=VMEM_LIMIT),
        name="sort_blocks",
    )(order, weights)


def place_blocks(gathered, tables, shapes, partial):
    block = gathered.shape[-1]
    used = [i for i, t in enumerate(tables) if len(t)]
    if not used:
        return partial
    count = sum(len(tables[i]) for i in used)
    known = [i for i in used if partial[i] is not None]

    def body(*refs):
        table_refs = refs[: len(used)]
        src = refs[len(used)]
        outs = refs[len(used) + 1 + len(known) : -3]
        stage, sem_in, sem_out = refs[-3:]
        at = 0
        for i, table_ref in zip(used, table_refs):

            def load(j, carry, table_ref=table_ref, at=at):
                pltpu.make_async_copy(src.at[table_ref[3 * j]], stage.at[at + j], sem_in).start()
                return carry

            lax.fori_loop(0, len(tables[i]), load, 0)
            at += len(tables[i])
        pltpu.make_async_copy(stage, stage, sem_in).wait()
        at = 0
        for i, table_ref, out in zip(used, table_refs, outs):

            def put(j, carry, table_ref=table_ref, out=out, at=at):
                row = pl.multiple_of(table_ref[3 * j + 1] * block, block)
                col = pl.multiple_of(table_ref[3 * j + 2] * block, block)
                pltpu.make_async_copy(
                    stage.at[at + j], out.at[pl.ds(row, block), pl.ds(col, block)], sem_out
                ).start()
                return carry

            lax.fori_loop(0, len(tables[i]), put, 0)
            at += len(tables[i])
        pltpu.make_async_copy(stage, stage, sem_out).wait()

    results = pl.pallas_call(
        body,
        out_shape=[jax.ShapeDtypeStruct(shapes[i], LOW) for i in used],
        in_specs=[SMEM] * len(used) + [ANY] * (1 + len(known)),
        out_specs=[ANY] * len(used),
        input_output_aliases={len(used) + 1 + j: used.index(i) for j, i in enumerate(known)},
        scratch_shapes=[
            pltpu.VMEM((count, block, block), LOW),
            pltpu.SemaphoreType.DMA,
            pltpu.SemaphoreType.DMA,
        ],
        compiler_params=pltpu.CompilerParams(vmem_limit_bytes=VMEM_LIMIT),
        cost_estimate=pl.CostEstimate(
            flops=0, bytes_accessed=4 * count * block * block, transcendentals=0
        ),
        name="place_blocks",
    )(
        *[jnp.asarray(tables[i].reshape(-1)) for i in used],
        gathered,
        *[partial[i] for i in known],
    )
    merged = list(partial)
    for i, value in zip(used, results):
        merged[i] = value
    return merged


def fill(scratch, pieces, order_ref):
    count = pieces[0].shape[0]
    for i, piece in enumerate(pieces):
        if order_ref is None:
            scratch[i * count : (i + 1) * count] = piece[...]
        else:
            scratch[pl.ds(pl.multiple_of(order_ref[i] * count, count), count)] = piece[...]


def grad_blocks(
    left, rights, order, pairs, table, wide, buffers, sizes, block, span=None, done=()
):
    tokens, height = left.shape
    by_column = len(rights) > 1 and rights[0].shape[0] == tokens
    width = sum(x.shape[-1] for x in rights) if by_column else rights[0].shape[-1]
    if pairs:
        width *= 2
    rows, cols = height // block, width // block
    if pairs:
        table = np.stack([table[: cols // 2], table[cols // 2 :]], 1).reshape(table.shape)
        wide = 2
    first, end = (0, cols // wide) if span is None else span
    steps = end - first
    if steps <= 0:
        return buffers
    assert not by_column or wide == 1
    per_step = rows * wide
    targets = [
        [(j, x, spot) for j, (x, spot) in enumerate(step) if (x, spot) not in done]
        for step in table.reshape(cols // wide, per_step, 2).tolist()[first:end]
    ]
    assert all(targets)
    used = sorted({x for step in targets for _, x, _ in step})
    known = [x for x in used if buffers[x] is not None]
    n_order = 0 if order is None else 1
    joined = len(rights) > 1
    first_known = n_order + 1 + len(rights)
    first_out = first_known + len(known)

    def body(*refs):
        left_ref = refs[n_order]
        right_refs = refs[n_order + 1 : first_known]
        outs = refs[first_out : first_out + len(used)]
        stage, sems = refs[first_out + len(used) : first_out + len(used) + 2]
        t = pl.program_id(0)
        slot = lax.rem(t, 2)
        if joined:
            right_ref = refs[-1]
            if by_column:
                step = 0
                for piece in right_refs:
                    for at in range(0, piece.shape[1], block):

                        @pl.when(t + first == step)
                        def _(piece=piece, at=at):
                            right_ref[...] = piece[:, at : at + block]

                        step += 1
            else:
                fill(right_ref, right_refs, refs[0] if n_order else None)
            taken = right_ref[...]
        elif pairs:
            taken = jnp.concatenate([right_refs[0][0], right_refs[0][1]], axis=1)
        else:
            taken = right_refs[0][...]

        def finish(step):
            sent = stage.at[step % 2, : len(targets[step])]
            pltpu.make_async_copy(sent, sent, sems.at[step % 2]).wait()

        for step in range(2, steps):

            @pl.when(t == step)
            def _(step=step):
                finish(step - 2)

        def some(i, carry):
            at = pl.multiple_of(i * (few * block), block)
            part = lax.dot_general(
                left_ref[:, pl.ds(at, few * block)],
                taken,
                (((0,), (0,)), ((), ())),
                preferred_element_type=F32,
            ).astype(LOW)
            for r in range(few):
                for c in range(wide):
                    stage[slot, c * rows + i * few + r] = part[
                        r * block : (r + 1) * block, c * block : (c + 1) * block
                    ]
            return carry

        parts = 1 if first > 0 or rows < 8 else 2
        few = rows // parts if rows % parts == 0 else rows
        lax.fori_loop(0, rows // few, some, 0)
        for step in range(steps):

            @pl.when(t == step)
            def _(step=step):
                for j, x, spot in targets[step]:
                    pltpu.make_async_copy(
                        stage.at[step % 2, j], outs[used.index(x)].at[spot], sems.at[step % 2]
                    ).start()

        @pl.when(t == steps - 1)
        def _():
            for step in range(max(0, steps - 2), steps):
                finish(step)

    taken_width = wide * block
    if pairs:
        right_specs = [pl.BlockSpec((2, tokens, block), lambda j: (0, 0, first + j))]
    elif by_column:
        right_specs = [pl.BlockSpec(x.shape, lambda j: (0, 0)) for x in rights]
    else:
        right_specs = [
            pl.BlockSpec((x.shape[0], taken_width), lambda j: (0, first + j)) for x in rights
        ]
    results = pl.pallas_call(
        body,
        grid=(steps,),
        out_shape=[jax.ShapeDtypeStruct((sizes[x], block, block), LOW) for x in used],
        in_specs=[SMEM] * n_order
        + [pl.BlockSpec((tokens, height), lambda j: (0, 0))]
        + right_specs
        + [ANY] * len(known),
        out_specs=[ANY] * len(used),
        input_output_aliases={first_known + j: used.index(x) for j, x in enumerate(known)},
        scratch_shapes=[
            pltpu.VMEM((2, per_step, block, block), LOW),
            pltpu.SemaphoreType.DMA((2,)),
        ]
        + ([pltpu.VMEM((tokens, taken_width), LOW)] if joined else []),
        compiler_params=pltpu.CompilerParams(vmem_limit_bytes=VMEM_LIMIT),
        cost_estimate=pl.CostEstimate(
            flops=4 * tokens * height * wide * block * steps,
            bytes_accessed=2 * (tokens * (height + width) + height * width),
            transcendentals=0,
        ),
        name="grad_blocks",
    )(*([] if order is None else [order]), left, *rights, *[buffers[x] for x in known])
    merged = list(buffers)
    for x, value in zip(used, results):
        merged[x] = value
    return merged


def grad_strips(strips, buffer, block):
    def body(*refs):
        out, stage, sem = refs[-3:]
        at = 0
        for i, (_, _, _, half, blocks) in enumerate(strips):
            right = refs[2 * i + 1]
            part = lax.dot_general(
                refs[2 * i][...],
                right[...] if half is None else right[0],
                (((0,), (0,)), ((), ())),
                preferred_element_type=F32,
            ).astype(LOW)
            for c, spot in blocks:
                stage[at] = part[:, c * block : (c + 1) * block]
                pltpu.make_async_copy(stage.at[at], out.at[spot], sem).start()
                at += 1
        pltpu.make_async_copy(stage, stage, sem).wait()

    specs, values = [], []
    for left, row, right, half, blocks in strips:
        tokens = left.shape[0]
        wide = (max(c for c, _ in blocks) + 1) * block
        specs.append(pl.BlockSpec((tokens, block), lambda j, row=row: (0, row)))
        if half is None:
            specs.append(pl.BlockSpec((tokens, wide), lambda j: (0, 0)))
        else:
            specs.append(pl.BlockSpec((1, tokens, wide), lambda j, half=half: (half, 0, 0)))
        values += [left, right]
    count = sum(len(blocks) for *_, blocks in strips)
    return pl.pallas_call(
        body,
        grid=(1,),
        in_specs=specs + [ANY],
        out_specs=ANY,
        out_shape=jax.ShapeDtypeStruct(buffer.shape, LOW),
        input_output_aliases={len(specs): 0},
        scratch_shapes=[pltpu.VMEM((count, block, block), LOW), pltpu.SemaphoreType.DMA],
        compiler_params=pltpu.CompilerParams(vmem_limit_bytes=VMEM_LIMIT),
        cost_estimate=pl.CostEstimate(
            flops=4 * count * values[0].shape[0] * block**2,
            bytes_accessed=4 * count * block * values[0].shape[0],
            transcendentals=0,
        ),
        name="grad_strips",
    )(*values, buffer)


def feed_forward(pieces, weights, hidden_grad, block):
    share, width = pieces[0].shape
    count = len(pieces)
    rows = share * count
    half = rows // 2
    hidden = weights.shape[1] // 2
    steps = hidden // block
    tile = 2 * block

    def body(*refs):
        gate_w, up_w, grad_ref, row_w = refs[count : count + 4]
        hid_ref, out_ref, joined, kept_ref, sent_ref, held = refs[count + 4 :]
        t = pl.program_id(0)

        @pl.when(t == 0)
        def _():
            fill(joined, refs[:count], None)

        @pl.when(t < steps)
        def _():
            both = dot(joined[...], jnp.concatenate([gate_w[...], up_w[...]], axis=1))
            gate, up = both[:, :block], both[:, block:]
            grad = grad_ref[...]
            sig = jax.nn.sigmoid(gate)
            act = gate * sig
            hid_ref[...] = (act * up).astype(LOW)
            here = pl.ds(pl.multiple_of(t * block, block), block)
            gate_grad = (grad * up * sig * (1.0 + gate * (1.0 - sig))).astype(LOW)
            up_grad = (grad * act).astype(LOW)
            out_ref[0] = gate_grad
            out_ref[1] = up_grad
            held[0, :, here] = gate_grad
            held[1, :, here] = up_grad

        @pl.when(t >= steps)
        def _():
            total = dot_turned(held[0], row_w[:, :hidden]) + dot_turned(held[1], row_w[:, hidden:])
            total = total.astype(LOW)
            kept_ref[...] = total[:half]
            sent_ref[...] = total[half:]

    def first(j):
        return jnp.minimum(j, steps - 1)

    def second(j):
        return jnp.maximum(j - steps, 0)

    hid, grads, joined, kept, sent = pl.pallas_call(
        body,
        grid=(steps + width // tile,),
        in_specs=[pl.BlockSpec((share, width), lambda j: (0, 0))] * count
        + [
            pl.BlockSpec((width, block), lambda j: (0, first(j))),
            pl.BlockSpec((width, block), lambda j: (0, steps + first(j))),
            pl.BlockSpec((rows, block), lambda j: (0, first(j))),
            pl.BlockSpec((tile, 2 * hidden), lambda j: (second(j), 0)),
        ],
        out_specs=[
            pl.BlockSpec((rows, block), lambda j: (0, first(j))),
            pl.BlockSpec((2, rows, block), lambda j: (0, 0, first(j))),
            pl.BlockSpec((rows, width), lambda j: (0, 0)),
            pl.BlockSpec((half, tile), lambda j: (0, second(j))),
            pl.BlockSpec((half, tile), lambda j: (0, second(j))),
        ],
        out_shape=[
            jax.ShapeDtypeStruct((rows, hidden), LOW),
            jax.ShapeDtypeStruct((2, rows, hidden), LOW),
            jax.ShapeDtypeStruct((rows, width), LOW),
            jax.ShapeDtypeStruct((half, width), LOW),
            jax.ShapeDtypeStruct((half, width), LOW),
        ],
        scratch_shapes=[pltpu.VMEM((2, rows, hidden), LOW)],
        compiler_params=pltpu.CompilerParams(vmem_limit_bytes=VMEM_LIMIT),
        cost_estimate=pl.CostEstimate(
            flops=8 * rows * width * hidden,
            bytes_accessed=2 * rows * width + 8 * width * hidden + 10 * rows * hidden,
            transcendentals=rows * hidden,
        ),
        name="feed_forward",
    )(*pieces, weights, weights, hidden_grad, weights)
    return hid, grads, joined, sent, kept


def project_rows(parts, weights, order, turned, tile):
    stacked = parts[0].ndim == 3
    rows = parts[0].shape[-2]
    half = rows // 2
    widths = [parts[0].shape[2]] * parts[0].shape[0] if stacked else [x.shape[1] for x in parts]
    starts = [sum(widths[:i]) for i in range(len(widths))]
    width = weights.shape[0] if turned else weights.shape[1]
    depth = sum(widths)
    share = rows // 4
    n_order = 0 if order is None else 1

    def body(*refs):
        part_refs = refs[n_order : n_order + len(parts)]
        w_ref, kept_ref, sent_ref = refs[n_order + len(parts) : n_order + len(parts) + 3]
        if n_order:
            joined = refs[-1]

            @pl.when(pl.program_id(0) == 0)
            def _():
                for i in range(4):
                    take = pl.ds(pl.multiple_of(refs[0][i] * share, share), share)
                    for part, at, size in zip(part_refs, starts, widths):
                        joined[i * share : (i + 1) * share, at : at + size] = part[take]

            pieces = [(joined[...], 0, depth)]
        elif stacked:
            pieces = [(part_refs[0][i], at, widths[i]) for i, at in enumerate(starts)]
        else:
            pieces = [(p[...], at, size) for p, at, size in zip(part_refs, starts, widths)]
        total = None
        for value, at, size in pieces:
            if turned:
                one = dot_turned(value, w_ref[:, at : at + size])
            else:
                one = dot(value, w_ref[at : at + size])
            total = one if total is None else total + one
        total = total.astype(LOW)
        kept_ref[...] = total[:half]
        sent_ref[...] = total[half:]

    whole = [pl.BlockSpec(x.shape, lambda j, n=x.ndim: (0,) * n) for x in parts]
    if turned:
        weight_spec = pl.BlockSpec((tile, depth), lambda j: (j, 0))
    else:
        weight_spec = pl.BlockSpec((depth, tile), lambda j: (0, j))
    kept, sent = pl.pallas_call(
        body,
        grid=(width // tile,),
        in_specs=[SMEM] * n_order + whole + [weight_spec],
        out_specs=[pl.BlockSpec((half, tile), lambda j: (0, j))] * 2,
        out_shape=[jax.ShapeDtypeStruct((half, width), LOW)] * 2,
        scratch_shapes=[pltpu.VMEM((rows, depth), LOW)] * n_order,
        compiler_params=pltpu.CompilerParams(vmem_limit_bytes=VMEM_LIMIT),
        cost_estimate=pl.CostEstimate(
            flops=2 * rows * depth * width,
            bytes_accessed=2 * (rows * depth + depth * width + rows * width),
            transcendentals=0,
        ),
        name="project_rows",
    )(*([order] if n_order else []), *parts, weights)
    return sent, kept


def down_back(grads, weights):
    rows, depth = grads.shape
    hidden = weights.shape[0]
    tile = 2 * LANES
    full, rest = divmod(hidden, tile)

    def body(g_ref, w_ref, *refs):
        o_ref = refs[-1]
        t = pl.program_id(0)

        @pl.when(t < full)
        def _():
            o_ref[...] = dot_turned(g_ref[...], w_ref[...])

        if rest:

            @pl.when(t == full)
            def _():
                o_ref[:, :rest] = dot_turned(g_ref[...], refs[0][...])

    assert rest == 0 or hidden % rest == 0
    specs = [
        pl.BlockSpec((rows, depth), lambda j: (0, 0)),
        pl.BlockSpec((tile, depth), lambda j: (jnp.minimum(j, full - 1), 0)),
    ]
    if rest:
        specs.append(pl.BlockSpec((rest, depth), lambda j: (hidden // rest - 1, 0)))
    return pl.pallas_call(
        body,
        grid=(full + (rest > 0),),
        in_specs=specs,
        out_specs=pl.BlockSpec((rows, tile), lambda j: (0, j)),
        out_shape=jax.ShapeDtypeStruct((rows, hidden), F32),
        compiler_params=pltpu.CompilerParams(vmem_limit_bytes=VMEM_LIMIT),
        cost_estimate=pl.CostEstimate(
            flops=2 * rows * depth * hidden,
            bytes_accessed=2 * depth * (rows + hidden) + 4 * rows * hidden,
            transcendentals=0,
        ),
        name="down_back",
    )(grads, *([weights] * len(specs[1:])))


def to_heads(pieces, weights, order):
    share = pieces[0].shape[0]
    width = weights.shape[0]

    rows = share * len(pieces)
    depth = weights.shape[1]
    tile = 2 * LANES

    def body(order_ref, *refs):
        w_ref, out_ref = refs[-2:]
        for i, piece in enumerate(refs[:-2]):
            put = pl.ds(pl.multiple_of(order_ref[i] * share, share), share)
            out_ref[put] = dot_turned(piece[...], w_ref[...]).astype(LOW)

    return pl.pallas_call(
        body,
        grid=(width // tile,),
        in_specs=[SMEM]
        + [pl.BlockSpec((share, depth), lambda j: (0, 0))] * len(pieces)
        + [pl.BlockSpec((tile, depth), lambda j: (j, 0))],
        out_specs=pl.BlockSpec((rows, tile), lambda j: (0, j)),
        out_shape=jax.ShapeDtypeStruct((rows, width), LOW),
        compiler_params=pltpu.CompilerParams(vmem_limit_bytes=VMEM_LIMIT),
        cost_estimate=pl.CostEstimate(
            flops=2 * rows * width * depth,
            bytes_accessed=2 * (rows + width) * depth,
            transcendentals=0,
        ),
        name="to_heads",
    )(order, *pieces, weights)


LANES = 128
QUERIES = 256
LONGEST = 512


def turn(values, cos, sin):
    lane = lax.broadcasted_iota(jnp.int32, values.shape, 1)
    other = jnp.where(
        lane % HD < HD // 2,
        pltpu.roll(values, LANES - HD // 2, 1),
        pltpu.roll(values, HD // 2, 1),
    )
    return values * cos + other * sin


def key_tables(cos, sin):
    lane = lax.broadcasted_iota(jnp.int32, cos.shape, 1)
    return jnp.where(lane < HD, cos, 1.0), jnp.where(lane < HD, sin, 0.0)


def project_heads(inputs, weights, cos, sin):
    rows, depth = inputs.shape
    width = weights.shape[1]
    assert width % LANES == 0 and HD == 64

    def body(x_ref, w_ref, cos_ref, sin_ref, q_ref, kv_ref):
        t = pl.program_id(0)

        def one(i, carry):
            here = pl.ds(pl.multiple_of(i * QUERIES, QUERIES), QUERIES)
            raw = dot(x_ref[here], w_ref[...])

            @pl.when(t < steps - 1)
            def _():
                turned = turn(raw, cos_ref[here], sin_ref[here])
                q_ref[here] = turned.astype(LOW) * LOW(HD**-0.5)

            @pl.when(t == steps - 1)
            def _():
                kv_ref[here] = turn(raw, *key_tables(cos_ref[here], sin_ref[here])).astype(LOW)

            return carry

        lax.fori_loop(0, rows // QUERIES, one, 0)

    steps = width // LANES
    whole = pl.BlockSpec((rows, LANES), lambda j: (0, 0))
    return pl.pallas_call(
        body,
        grid=(steps,),
        in_specs=[
            pl.BlockSpec((rows, depth), lambda j: (0, 0)),
            pl.BlockSpec((depth, LANES), lambda j: (0, j)),
            whole,
            whole,
        ],
        out_specs=[pl.BlockSpec((rows, LANES), lambda j: (0, jnp.minimum(j, steps - 2))), whole],
        out_shape=[
            jax.ShapeDtypeStruct((rows, width - LANES), LOW),
            jax.ShapeDtypeStruct((rows, LANES), LOW),
        ],
        compiler_params=pltpu.CompilerParams(vmem_limit_bytes=VMEM_LIMIT),
        cost_estimate=pl.CostEstimate(
            flops=2 * rows * depth * width,
            bytes_accessed=2 * (rows * depth + depth * width + rows * width),
            transcendentals=0,
        ),
        name="project_heads",
    )(inputs, weights, cos, sin)


def keep_keys(padded, kv_ref):
    padded[:LONGEST] = jnp.zeros((LONGEST, LANES), LOW)
    padded[LONGEST:] = kv_ref[...]


def visible(start_ref, at):
    shape = (LONGEST + QUERIES, QUERIES)
    key = at - LONGEST + lax.broadcasted_iota(jnp.int32, shape, 0)
    query = at + lax.broadcasted_iota(jnp.int32, shape, 1)
    return (key >= start_ref[:, pl.ds(at, QUERIES)]) & (key <= query)


def attend(queries, kv, starts):
    rows, width = queries.shape
    groups = width // LANES

    def body(start_ref, q_ref, kv_ref, o_ref, log_ref, padded):
        @pl.when(pl.program_id(0) == 0)
        def _():
            keep_keys(padded, kv_ref)

        def one(i, carry):
            at = pl.multiple_of(i * QUERIES, QUERIES)
            here = pl.ds(at, QUERIES)
            seen = visible(start_ref, at)
            window = padded[pl.ds(at, LONGEST + QUERIES)]
            keys, values = window[:, :HD], window[:, HD:]
            for h in range(LANES // HD):
                query = q_ref[here, h * HD : (h + 1) * HD]
                scores = jnp.where(seen, dot_turned(keys, query), -1e30)
                top = jnp.max(scores, axis=0, keepdims=True)
                expo = jnp.exp(scores - top)
                total = jnp.sum(expo, axis=0, keepdims=True)
                probs = (expo * (1.0 / total)).astype(LOW)
                o_ref[here, h * HD : (h + 1) * HD] = lax.dot_general(
                    probs, values, (((0,), (0,)), ((), ())), preferred_element_type=F32
                ).astype(LOW)
                log_ref[0, h : h + 1, here] = top + jnp.log(total)
            return carry

        lax.fori_loop(0, rows // QUERIES, one, 0)

    column = pl.BlockSpec((rows, LANES), lambda j: (0, j))
    return pl.pallas_call(
        body,
        grid=(groups,),
        in_specs=[
            pl.BlockSpec((1, rows), lambda j: (0, 0)),
            column,
            pl.BlockSpec((rows, LANES), lambda j: (0, 0)),
        ],
        out_specs=[column, pl.BlockSpec((1, LANES // HD, rows), lambda j: (j, 0, 0))],
        out_shape=[
            jax.ShapeDtypeStruct((rows, width), LOW),
            jax.ShapeDtypeStruct((groups, LANES // HD, rows), F32),
        ],
        scratch_shapes=[pltpu.VMEM((LONGEST + rows, LANES), LOW)],
        compiler_params=pltpu.CompilerParams(vmem_limit_bytes=VMEM_LIMIT),
        cost_estimate=pl.CostEstimate(
            flops=30 * rows * rows * width,
            bytes_accessed=4 * rows * width,
            transcendentals=rows * rows * width // HD,
        ),
        name="attend",
    )(starts, queries, kv)


def attend_back(queries, kv, starts, logs, grads, cos, sin):
    rows, width = queries.shape
    groups = width // LANES

    def body(
        start_ref, q_ref, kv_ref, log_ref, g_ref, cos_ref, sin_ref, dq_ref, sum_ref, acc, padded
    ):
        @pl.when(pl.program_id(0) == 0)
        def _():
            keep_keys(padded, kv_ref)
            acc[...] = jnp.zeros_like(acc)

        def one(i, carry):
            at = pl.multiple_of(i * QUERIES, QUERIES)
            here = pl.ds(at, QUERIES)
            there = pl.ds(at, LONGEST + QUERIES)
            seen = visible(start_ref, at)
            window = padded[there]
            keys, values = window[:, :HD], window[:, HD:]
            parts = []
            key_part, value_part = 0.0, 0.0
            for h in range(LANES // HD):
                query = q_ref[here, h * HD : (h + 1) * HD]
                grad = g_ref[here, h * HD : (h + 1) * HD]
                scores = jnp.where(seen, dot_turned(keys, query), -1e30)
                probs = jnp.exp(scores - log_ref[0, h : h + 1, here])
                value_part += dot(probs.astype(LOW), grad)
                prob_grads = dot_turned(values, grad)
                inner = jnp.sum(probs * prob_grads, axis=0, keepdims=True)
                score_grads = (probs * (prob_grads - inner)).astype(LOW)
                key_part += dot(score_grads, query)
                parts.append(
                    lax.dot_general(
                        score_grads, keys, (((0,), (0,)), ((), ())), preferred_element_type=F32
                    )
                )
            acc[there] += jnp.concatenate([key_part, value_part], axis=1)
            dq_ref[here] = turn(
                jnp.concatenate(parts, axis=1) * HD**-0.5, cos_ref[here], -sin_ref[here]
            ).astype(LOW)
            return carry

        lax.fori_loop(0, rows // QUERIES, one, 0)

        @pl.when(pl.program_id(0) == groups - 1)
        def _():
            key_cos, key_sin = key_tables(cos_ref[...], sin_ref[...])
            sum_ref[...] = turn(acc[LONGEST:], key_cos, -key_sin).astype(LOW)

    column = pl.BlockSpec((rows, LANES), lambda j: (0, j))
    whole = pl.BlockSpec((rows, LANES), lambda j: (0, 0))
    return pl.pallas_call(
        body,
        grid=(groups,),
        in_specs=[
            pl.BlockSpec((1, rows), lambda j: (0, 0)),
            column,
            whole,
            pl.BlockSpec((1, LANES // HD, rows), lambda j: (j, 0, 0)),
            column,
            whole,
            whole,
        ],
        out_specs=[column, whole],
        out_shape=[
            jax.ShapeDtypeStruct((rows, width), LOW),
            jax.ShapeDtypeStruct((rows, LANES), LOW),
        ],
        scratch_shapes=[
            pltpu.VMEM((LONGEST + rows, LANES), F32),
            pltpu.VMEM((LONGEST + rows, LANES), LOW),
        ],
        compiler_params=pltpu.CompilerParams(vmem_limit_bytes=VMEM_LIMIT),
        cost_estimate=pl.CostEstimate(
            flops=80 * rows * rows * width,
            bytes_accessed=16 * rows * width,
            transcendentals=rows * rows * width // HD,
        ),
        name="attend_back",
    )(starts, queries, kv, logs, grads, cos, sin)


def shampoo(sums, places, factor, weights, ema, left, right, left_roots, right_roots, before):
    count, block, _ = sums.shape
    group = 3 if count % 3 == 0 else 2 if count % 2 == 0 else 1
    steps = count // group
    depth = min(4, steps)
    extra = [] if before is None else list(before)

    def mm(a, b, dims):
        return lax.dot_general(
            a.astype(LOW), b.astype(LOW), (dims, ((), ())), preferred_element_type=F32
        )

    def body(places_ref, g_ref, *refs):
        ins, outs = refs[:6], refs[6 + len(extra) : 11 + len(extra)]
        given, made, sem_in, sem_out = refs[11 + len(extra) :]

        def load(t, slot):
            for u in range(group):
                place = places_ref[t * group + u]
                for i, ref in enumerate(ins):
                    pltpu.make_async_copy(
                        ref.at[place], given.at[slot, u, i], sem_in.at[slot]
                    ).start()

        def wait(buffer, slot, sems):
            pltpu.make_async_copy(buffer.at[slot], buffer.at[slot], sems.at[slot]).wait()

        for t in range(depth):
            load(t, t)

        def step(t, carry):
            slot = lax.rem(t, depth)
            wait(given, slot, sem_in)

            @pl.when(t >= depth)
            def _():
                wait(made, slot, sem_out)

            both = 0.5 * factor * factor
            for u in range(group):
                low = g_ref[t * group + u]
                made[slot, u, 0] = low.astype(F32) * factor
                made[slot, u, 3] = 0.5 * given[slot, u, 2] + both * mm(low, low, ((1,), (1,)))
                made[slot, u, 4] = 0.5 * given[slot, u, 3] + both * mm(low, low, ((0,), (0,)))
                part = mm(low, given[slot, u, 5], ((1,), (0,))) * factor
                fresh = given[slot, u, 0] - weight_rate * mm(given[slot, u, 4], part, ((1,), (0,)))
                made[slot, u, 1] = fresh
                made[slot, u, 2] = (
                    average_decay * given[slot, u, 1] + (1.0 - average_decay) * fresh
                )
            for u in range(group):
                place = places_ref[t * group + u]
                for i, ref in enumerate(outs):
                    pltpu.make_async_copy(
                        made.at[slot, u, i], ref.at[place], sem_out.at[slot]
                    ).start()

            @pl.when(t + depth < steps)
            def _():
                load(t + depth, slot)

            return carry

        lax.fori_loop(0, steps, step, 0)
        for t in range(steps - depth, steps):
            wait(made, t % depth, sem_out)

    return pl.pallas_call(
        body,
        out_shape=[jax.ShapeDtypeStruct(weights.shape, F32)] * 5,
        in_specs=[SMEM, VMEM] + [ANY] * (6 + len(extra)),
        out_specs=[ANY] * 5,
        input_output_aliases={8 + i: i for i in range(len(extra))},
        scratch_shapes=[
            pltpu.VMEM((depth, group, 6, block, block), F32),
            pltpu.VMEM((depth, group, 5, block, block), F32),
            pltpu.SemaphoreType.DMA((depth,)),
            pltpu.SemaphoreType.DMA((depth,)),
        ],
        compiler_params=pltpu.CompilerParams(vmem_limit_bytes=VMEM_LIMIT),
        cost_estimate=pl.CostEstimate(
            flops=8 * count * block**3,
            bytes_accessed=46 * count * block * block,
            transcendentals=0,
        ),
        name="shampoo",
    )(places, sums, weights, ema, left, right, left_roots, right_roots, *extra)


def rows_call(body, ins, outs, name, step=128, work=10):
    rows = max(x.shape[0] for x in ins)

    def spec(x):
        if x.shape[0] == rows:
            return pl.BlockSpec((step, x.shape[1]), lambda j: (j, 0))
        return pl.BlockSpec(x.shape, lambda j: (0, 0))

    return pl.pallas_call(
        body,
        grid=(rows // step,),
        in_specs=[spec(x) for x in ins],
        out_specs=[spec(x) for x in outs],
        out_shape=outs,
        compiler_params=pltpu.CompilerParams(vmem_limit_bytes=VMEM_LIMIT),
        cost_estimate=pl.CostEstimate(
            flops=work * rows * ins[0].shape[1],
            bytes_accessed=sum(x.size * x.dtype.itemsize for x in list(ins) + list(outs)),
            transcendentals=0,
        ),
        name=name,
    )(*ins)


def add_near(kept, got):
    share = kept.shape[0] // 2
    width = kept.shape[1]
    step = 128

    def body(a_ref, c_ref, b_ref, d_ref, mine_ref, other_ref):
        mine_ref[...] = a_ref[...].astype(F32) + b_ref[...].astype(F32)
        other_ref[...] = (c_ref[...].astype(F32) + d_ref[...].astype(F32)).astype(LOW)

    first = pl.BlockSpec((step, width), lambda j: (j, 0))
    second = pl.BlockSpec((step, width), lambda j: (share // step + j, 0))
    return pl.pallas_call(
        body,
        grid=(share // step,),
        in_specs=[first, second, first, second],
        out_specs=[first] * 2,
        out_shape=[
            jax.ShapeDtypeStruct((share, width), F32),
            jax.ShapeDtypeStruct((share, width), LOW),
        ],
        compiler_params=pltpu.CompilerParams(vmem_limit_bytes=VMEM_LIMIT),
        cost_estimate=pl.CostEstimate(
            flops=2 * share * width, bytes_accessed=14 * share * width, transcendentals=0
        ),
        name="add_near",
    )(kept, kept, got, got)


def second_norm(tokens, mine, got, gain):
    def body(x_ref, a_ref, b_ref, gain_ref, middle_ref, low_ref):
        middle = x_ref[...].astype(F32) + (a_ref[...] + b_ref[...].astype(F32))
        middle_ref[...] = middle
        scale = lax.rsqrt(jnp.mean(middle * middle, axis=-1, keepdims=True) + 1e-05)
        low_ref[...] = (middle * scale * gain_ref[...]).astype(LOW)

    return rows_call(
        body,
        [tokens, mine, got, gain],
        [jax.ShapeDtypeStruct(tokens.shape, F32), jax.ShapeDtypeStruct(tokens.shape, LOW)],
        "second_norm",
    )


def first_norm(tokens, gain):
    def body(x_ref, gain_ref, low_ref):
        x = x_ref[...].astype(F32)
        scale = lax.rsqrt(jnp.mean(x * x, axis=-1, keepdims=True) + 1e-05)
        low_ref[...] = (x * scale * gain_ref[...]).astype(LOW)

    return rows_call(
        body,
        [tokens, gain],
        [jax.ShapeDtypeStruct(tokens.shape, LOW)],
        "first_norm",
    )[0]


def norm_back(values, mine, got, gain, residual):
    def body(x_ref, a_ref, b_ref, gain_ref, r_ref, out_ref, low_ref, sum_ref):
        x = x_ref[...].astype(F32)
        grad = a_ref[...] + b_ref[...].astype(F32)
        scale = lax.rsqrt(jnp.mean(x * x, axis=-1, keepdims=True) + 1e-05)
        unit = x * scale
        scaled = grad * gain_ref[...]
        out = r_ref[...].astype(F32) + scale * (
            scaled - unit * jnp.mean(scaled * unit, axis=-1, keepdims=True)
        )
        out_ref[...] = out
        low_ref[...] = out.astype(LOW)

        @pl.when(pl.program_id(0) == 0)
        def _():
            sum_ref[...] = jnp.zeros_like(sum_ref)

        sum_ref[...] += jnp.sum(grad * unit, axis=0, keepdims=True)

    shape = values.shape
    return rows_call(
        body,
        [values, mine, got, gain, residual],
        [
            jax.ShapeDtypeStruct(shape, F32),
            jax.ShapeDtypeStruct(shape, LOW),
            jax.ShapeDtypeStruct((1, shape[1]), F32),
        ],
        "norm_back",
        work=1000000,
    )


def doc_positions(doc_ids):
    length = doc_ids.shape[-1]
    offsets = jnp.arange(length, dtype=jnp.int32)
    starts = jnp.concatenate(
        [jnp.ones(doc_ids.shape[:-1] + (1,), jnp.bool_), doc_ids[..., 1:] != doc_ids[..., :-1]],
        axis=-1,
    )
    first_index = lax.cummax(jnp.where(starts, offsets, 0), axis=doc_ids.ndim - 1)
    return offsets - first_index


def rope_tables(positions, head_size):
    half_size = head_size // 2
    exponent = jnp.arange(half_size, dtype=F32) * (2.0 / head_size)
    inverse = jnp.power(F32(10000.0), -exponent)
    angles = positions.astype(F32)[..., None] * inverse
    cos, sin = jnp.cos(angles), jnp.sin(angles)
    repeats = LANES // head_size
    return (
        jnp.concatenate([cos, cos] * repeats, axis=-1),
        jnp.concatenate([-sin, sin] * repeats, axis=-1),
    )


def after(value, *others):
    return lax.optimization_barrier((value,) + others)[0]


def dot(left, right):
    return jnp.dot(left, right, preferred_element_type=F32)


def dot_turned(left, right):
    return lax.dot_general(left, right, (((1,), (1,)), ((), ())), preferred_element_type=F32)


EXCHANGE = (0, 2, 1, 3)


def on_device(
    tokens_in,
    cotangent,
    select_mask,
    doc_ids,
    norm_gains,
    weight_blocks,
    ema_blocks,
    left_stats,
    right_stats,
    left_roots,
    right_roots,
):
    mp_count = lax.axis_size("mp")
    dp_count = lax.axis_size("dp")
    sequences, length, model_width = tokens_in.shape
    assert sequences == 1 and mp_count == 4 and dp_count & (dp_count - 1) == 0
    rows = sequences * length
    own, block, _ = weight_blocks.shape
    query_cols = HEADS * HD // mp_count
    key_cols = KV_HEADS * HD // mp_count
    hidden_cols = FF // mp_count
    assert KV_HEADS == mp_count and length % QUERIES == 0
    row_blocks = model_width // block
    attn_blocks = (query_cols + 2 * key_cols) // block
    hidden_blocks = hidden_cols // block
    in_blocks = attn_blocks + 2 * hidden_blocks
    out_attn_blocks = query_cols // block
    share = rows // mp_count
    m_index = lax.axis_index("mp")
    d_index = lax.axis_index("dp")

    plan = Layout(dp_count, own, row_blocks, attn_blocks, in_blocks, out_attn_blocks)
    order = lax.dynamic_slice_in_dim(jnp.asarray(plan.order), d_index, 1, 0).reshape(-1)
    shapes = [
        (model_width, attn_blocks * block),
        (query_cols, model_width),
        (model_width, 2 * hidden_cols),
        (hidden_cols, model_width),
    ]

    def partner(values, bit):
        return lax.ppermute(values, "mp", [(i, i ^ bit) for i in range(mp_count)])

    def true_share(values, group):
        return lax.dynamic_slice_in_dim(values, (m_index ^ group) * share, share, 0)

    def to_exchange(values):
        return jnp.concatenate([true_share(values, g) for g in EXCHANGE], axis=0)

    def to_true(parts):
        by_group = [parts[EXCHANGE.index(g)] for g in range(4)]
        low, high = m_index & 1, m_index & 2
        pairs = []
        for a, b in ((0, 1), (2, 3)):
            pairs.append(
                (
                    jnp.where(low == 0, by_group[a], by_group[b]),
                    jnp.where(low == 0, by_group[b], by_group[a]),
                )
            )
        flat = []
        for first, second in ((0, 1), (1, 0)):
            for i in range(2):
                flat.append(jnp.where(high == 0, pairs[first][i], pairs[second][i]))
        return jnp.concatenate(flat, axis=0)

    def near_sum(sent, kept):
        return add_near(kept, partner(sent, 1))

    def spread_share(mine, *cover):
        far = partner(mine, 2)
        near = partner(mine, 1)
        if cover:
            far = after(far, *cover)
        return [mine, far, near, partner(far, 1)]

    sorted_low = list(sort_blocks(weight_blocks, order, plan.chunks[:1]))
    if len(plan.chunks) > 1:
        sorted_low += sort_blocks(
            weight_blocks, after(order, *sorted_low), plan.chunks[1:]
        )
    gathered = [
        lax.all_gather(chunk, "dp", axis=0, tiled=True, axis_index_groups=[plan.ring])
        for chunk in sorted_low
    ]
    none = np.zeros((0, 3), np.int32)
    last = len(gathered) - 1

    def place(x, source, which, matrices):
        tables = [plan.of_chunk(x, i) if i in which else none for i in range(4)]
        return place_blocks(source, tables, shapes, matrices)

    matrices = place(0, gathered[0], (0, 1, 2, 3), [None] * 4)
    w_qkv = matrices[0]
    if last >= 1:
        matrices = place(1, gathered[1], (1,), matrices)
    w_attn_out = matrices[1]

    positions = doc_positions(doc_ids)
    starts = jnp.arange(length, dtype=jnp.int32)[None] - positions
    cos, sin = rope_tables(positions[0], HD)

    tokens_low = tokens_in.reshape(rows, model_width)
    first_in = first_norm(tokens_low, norm_gains[:1])
    out_grad = cotangent.reshape(rows, model_width) * select_mask.astype(LOW).reshape(rows, 1)
    own_tokens = true_share(tokens_low, 0)
    own_grad = true_share(out_grad, 0)
    mlp_grad = to_exchange(out_grad)
    tokens_local = to_exchange(tokens_low)
    unit_scale = lax.rsqrt(
        jnp.mean(jnp.square(tokens_local.astype(F32)), axis=-1, keepdims=True) + 1e-05
    )

    shares = (m_index ^ jnp.array(EXCHANGE, jnp.int32)).astype(jnp.int32)
    queries, kv = project_heads(first_in, w_qkv, cos, sin)
    kv, mlp_grad, own_tokens, own_grad, tokens_local, unit_scale = lax.optimization_barrier(
        (kv, mlp_grad, own_tokens, own_grad, tokens_local, unit_scale)
    )
    mixed, logs = attend(queries, kv, starts)
    attended_sent, attended_kept = project_rows([mixed], w_attn_out, shares, False, 512)
    mine, other = near_sum(attended_sent, attended_kept)
    if last >= 1:
        matrices = place(1, after(gathered[1], other), (2, 3), matrices)
        mine, *matrices[2:] = lax.optimization_barrier((mine, *matrices[2:]))
    middle, second_low = second_norm(own_tokens, mine, partner(other, 2), norm_gains[1:])
    if last >= 2:
        matrices = place(2, after(gathered[2], second_low), (2, 3), matrices)
    w_gateup, w_down = matrices[2:]
    hidden_grad = down_back(mlp_grad, w_down)
    second_pieces = spread_share(second_low, hidden_grad)
    hidden, gateup_grad, second_in, second_sent, second_kept = feed_forward(
        second_pieces, w_gateup, hidden_grad, block
    )

    sizes = [dp_count * n for _, n in plan.chunks]
    sums = [None] * len(sizes)
    reduced = [None] * len(sizes)

    def scatter(x):
        reduced[x] = lax.psum_scatter(
            sums[x], "dp", scatter_dimension=0, tiled=True, axis_index_groups=[plan.ring]
        )

    def known(values):
        return [x for x in values if x is not None]

    cuts = {2: 0, 3: 0}
    sent = set()
    if last >= 2:
        cuts = {2: plan.first_late[2], 3: plan.first_late[3] // 2}
        sent = {(last, spot) for *_, spot in plan.strips}
    def down_grads(sums, hidden, span):
        table = plan.of_matrix(3, hidden_blocks, row_blocks)
        return grad_blocks(
            hidden, [mlp_grad], None, False, table, 2, sums, sizes, block, span, sent
        )

    def gateup_grads(sums, second_in, span):
        table = plan.of_matrix(2, row_blocks, 2 * hidden_blocks)
        return grad_blocks(
            second_in, [gateup_grad], None, True, table, 2, sums, sizes, block, span, sent
        )

    sums = down_grads(sums, after(hidden, second_sent), (cuts[3], row_blocks // 2))
    mine, other = near_sum(second_sent, after(second_kept, *known(sums)))
    if sent:
        strips = {}
        for matrix, r, c, spot in plan.strips:
            half = c // hidden_blocks if matrix == 2 else None
            at = c if half is None else c % hidden_blocks
            strips.setdefault((matrix, r, half), []).append((at, spot))
        sums[last] = grad_strips(
            [
                (
                    after(second_in, other) if matrix == 2 else hidden,
                    r,
                    gateup_grad if matrix == 2 else mlp_grad,
                    half,
                    blocks,
                )
                for (matrix, r, half), blocks in strips.items()
            ],
            sums[last],
            block,
        )

    sums = gateup_grads(sums, after(second_in, other), (cuts[2], hidden_blocks))
    if last >= 2:
        scatter(2)
    got = partner(other, 2)
    mine = after(mine, *known(sums[:2]))
    middle_grad, attn_low, second_gain = norm_back(
        middle, mine, got, norm_gains[1:], own_grad
    )
    sums = gateup_grads(sums, after(second_in, attn_low), (0, cuts[2]))
    sums = down_grads(sums, after(hidden, attn_low), (0, cuts[3]))
    attn_grad = spread_share(attn_low, *known(sums[:2]))
    sums = grad_blocks(
        mixed,
        attn_grad,
        shares,
        False,
        plan.of_matrix(1, out_attn_blocks, row_blocks),
        4,
        sums,
        sizes,
        block,
    )
    if last >= 1:
        scatter(1)

    feed_sent, feed_kept = project_rows(
        [after(hidden, *known(sums[:2]))], w_down, None, False, 512
    )
    feed_mine, feed_other = near_sum(feed_sent, feed_kept)
    mixed_grad = to_heads(attn_grad, after(w_attn_out, feed_other), shares)
    query_grad, kv_grad = attend_back(queries, kv, starts, logs, mixed_grad, cos, sin)
    feed_part = after(feed_mine, query_grad) + partner(feed_other, 2).astype(F32)
    out_low = (middle + feed_part).astype(LOW)
    qkv_grads = [query_grad, kv_grad]
    first_sent, first_kept = project_rows(
        [after(query_grad, out_low), kv_grad], w_qkv, shares, True, 512
    )
    mine, other = near_sum(first_sent, first_kept)

    half = rows // 2
    first_gain = sum(
        jnp.sum(part.astype(F32) * (x.astype(F32) * scale), axis=0, keepdims=True)
        for part, x, scale in (
            (first_kept, tokens_local[:half], unit_scale[:half]),
            (first_sent, tokens_local[half:], unit_scale[half:]),
        )
    )
    gain_sums = jnp.concatenate([first_gain, second_gain], axis=0)
    gain_sums = gain_sums + partner(gain_sums, 2)
    other = after(other, gain_sums)
    sums = grad_blocks(
        after(first_in, other),
        qkv_grads,
        None,
        False,
        plan.of_matrix(0, row_blocks, attn_blocks),
        1,
        sums,
        sizes,
        block,
    )
    scatter(0)
    factor = float(rows * dp_count) ** (-0.5)

    def update(x, state, *others):
        start, count = plan.chunks[x]
        return shampoo(
            reduced[x],
            after(lax.slice_in_dim(order, start, start + count), *others),
            factor,
            weight_blocks,
            ema_blocks,
            left_stats,
            right_stats,
            left_roots,
            right_roots,
            state,
        )

    _, input_low, _ = norm_back(
        own_tokens,
        after(mine, sums[0]),
        partner(other, 2),
        norm_gains[:1],
        middle_grad,
    )
    state = None
    if last >= 2:
        state = update(2, state, input_low)
    if last >= 1:
        state = update(1, state, input_low)
    gain_sums = after(gain_sums, input_low, *(state or ()))
    gain_sums = gain_sums + partner(gain_sums, 1)
    bit = 1
    while bit < dp_count:
        gain_sums = gain_sums + lax.ppermute(
            gain_sums, "dp", [(i, i ^ bit) for i in range(dp_count)]
        )
        bit *= 2
    input_parts = spread_share(input_low, *(state or ()))
    gain_share = model_width // dp_count
    gain_grads = factor * lax.dynamic_slice_in_dim(gain_sums, d_index * gain_share, gain_share, 1)
    old_gains = lax.dynamic_slice_in_dim(norm_gains, d_index * gain_share, gain_share, 1)
    new_gains = old_gains - gain_rate * gain_grads
    out_parts = spread_share(after(out_low, input_low), *(state or ()))
    block_out = to_true(out_parts).reshape(sequences, length, model_width)
    input_grad = to_true(input_parts).astype(F32).reshape(sequences, length, model_width)
    grads, new_weights, new_ema, new_left, new_right = update(
        0, state, input_grad, block_out, new_gains
    )
    return (
        block_out,
        input_grad,
        grads,
        new_weights,
        new_ema,
        new_left,
        new_right,
        gain_grads,
        new_gains,
    )


def solution(mesh):
    in_specs = (
        P("dp", None, None),
        P("dp", None, None),
        P("dp", None),
        P("dp", None),
        P(),
        P(("dp", "mp"), None, None),
        P(("dp", "mp"), None, None),
        P(("dp", "mp"), None, None),
        P(("dp", "mp"), None, None),
        P(("dp", "mp"), None, None),
        P(("dp", "mp"), None, None),
    )
    out_specs = (
        P("dp", None, None),
        P("dp", None, None),
        P(("dp", "mp"), None, None),
        P(("dp", "mp"), None, None),
        P(("dp", "mp"), None, None),
        P(("dp", "mp"), None, None),
        P(("dp", "mp"), None, None),
        P(None, "dp"),
        P(None, "dp"),
    )
    return jax.shard_map(
        on_device, mesh=mesh, in_specs=in_specs, out_specs=out_specs, check_vma=False
    )
```

```python
import functools

import jax
import jax.numpy as jnp
import numpy as np
from jax import lax
from jax.experimental import pallas as pl
from jax.experimental.pallas import tpu as pltpu
from jax.sharding import PartitionSpec as P

HEADS = 32
KV_HEADS = 4
HD = 64
FF = 5632
LOW = jnp.bfloat16
F32 = jnp.float32

weight_rate = 1.0
gain_rate = 0.2
average_decay = 0.9
VMEM_LIMIT = 60 * 1024 * 1024


def ring_order(count):
    return list(range(0, count, 2)) + list(range(1, count, 2))[::-1]


class Layout:
    def __init__(self, dp, own, rows, attn_cols, in_cols, out_attn_rows):
        self.dp, self.own = dp, own
        self.ring = ring_order(dp)
        n_in = rows * in_cols
        units = (in_cols - attn_cols) // 2
        kinds, spots, keys = [], [], []
        for k in range(dp * own):
            if k < n_in:
                r, c = divmod(k, in_cols)
                if c < attn_cols:
                    kinds.append(0), spots.append((0, r, c)), keys.append((0, k))
                else:
                    c -= attn_cols
                    kinds.append(2), spots.append((2, r, c)), keys.append((2, c % units / units, k))
            else:
                r, c = divmod(k - n_in, rows)
                if r < out_attn_rows:
                    kinds.append(1), spots.append((1, r, c)), keys.append((1, k))
                else:
                    kinds.append(2), spots.append((3, r - out_attn_rows, c))
                    keys.append((2, c / rows, k))
        self.order = np.zeros((dp, own), np.int32)
        for d in range(dp):
            self.order[d] = sorted(range(own), key=lambda l: keys[d * own + l])
        count = np.array(kinds).reshape(dp, own)
        first = int((count == 0).sum(1).max())
        second = int((count <= 1).sum(1).max())
        bounds = [0, first, max(first, second), own]
        self.chunks = [(a, b - a) for a, b in zip(bounds[:-1], bounds[1:]) if b > a]
        self.table = []
        for p, d in enumerate(self.ring):
            for j, l in enumerate(self.order[d]):
                (x,) = [i for i, (a, n) in enumerate(self.chunks) if a <= j < a + n]
                a, n = self.chunks[x]
                self.table.append(spots[d * own + int(l)] + (x, p * n + j - a))
        mixed = [p for p, d in enumerate(self.ring) if (count[d] == 1).any()]
        last, size = len(self.chunks) - 1, self.chunks[-1][1]
        late = [t for t in self.table if t[3] == last]
        self.first_late = {}
        for m, cols in ((2, units), (3, rows)):
            own_late = [c % cols for i, r, c, x, s in late if i == m and s // size not in mixed]
            self.first_late[m] = min(own_late, default=cols)
        self.strips = sorted(
            (m, r, c, s)
            for m, r, c, x, s in late
            if m >= 2 and s // size in mixed and c % (units if m == 2 else rows) < self.first_late[m]
        )

    def of_chunk(self, x, matrix):
        rows = [(s, r, c) for m, r, c, y, s in self.table if y == x and m == matrix]
        return np.array(sorted(rows), np.int32).reshape(-1, 3)

    def of_matrix(self, matrix, rows, cols):
        out = np.zeros((cols, rows, 2), np.int32)
        for m, r, c, x, s in self.table:
            if m == matrix:
                out[c, r] = (x, s)
        return out


def held(values):
    return pltpu.with_memory_space_constraint(values, pltpu.VMEM)


ANY = pl.BlockSpec(memory_space=pl.ANY)
SMEM = pl.BlockSpec(memory_space=pltpu.SMEM)
VMEM = pl.BlockSpec(memory_space=pltpu.VMEM)


def sort_blocks(weights, order, chunks):
    block = weights.shape[1:]
    total = sum(n for _, n in chunks)
    begin = chunks[0][0]

    def body(order_ref, w_ref, *refs):
        outs, (given, sem) = refs[: len(chunks)], refs[len(chunks) :]

        def load(j, carry):
            pltpu.make_async_copy(w_ref.at[order_ref[begin + j]], given.at[j], sem).start()
            return carry

        lax.fori_loop(0, total, load, 0)
        pltpu.make_async_copy(given, given, sem).wait()
        for (start, count), out in zip(chunks, outs):

            def one(j, carry, start=start, out=out):
                out[j] = given[start - begin + j].astype(LOW)
                return carry

            lax.fori_loop(0, count, one, 0)

    return pl.pallas_call(
        body,
        out_shape=[jax.ShapeDtypeStruct((n,) + block, LOW) for _, n in chunks],
        in_specs=[SMEM, ANY],
        out_specs=[VMEM] * len(chunks),
        scratch_shapes=[pltpu.VMEM((total,) + block, F32), pltpu.SemaphoreType.DMA],
        compiler_params=pltpu.CompilerParams(vmem_limit_bytes=VMEM_LIMIT),
        name="sort_blocks",
    )(order, weights)


def place_blocks(gathered, tables, shapes, partial):
    block = gathered.shape[-1]
    used = [i for i, t in enumerate(tables) if len(t)]
    if not used:
        return partial
    count = sum(len(tables[i]) for i in used)
    known = [i for i in used if partial[i] is not None]

    def body(*refs):
        table_refs = refs[: len(used)]
        src = refs[len(used)]
        outs = refs[len(used) + 1 + len(known) : -3]
        stage, sem_in, sem_out = refs[-3:]
        at = 0
        for i, table_ref in zip(used, table_refs):

            def load(j, carry, table_ref=table_ref, at=at):
                pltpu.make_async_copy(src.at[table_ref[3 * j]], stage.at[at + j], sem_in).start()
                return carry

            lax.fori_loop(0, len(tables[i]), load, 0)
            at += len(tables[i])
        pltpu.make_async_copy(stage, stage, sem_in).wait()
        at = 0
        for i, table_ref, out in zip(used, table_refs, outs):

            def put(j, carry, table_ref=table_ref, out=out, at=at):
                row = pl.multiple_of(table_ref[3 * j + 1] * block, block)
                col = pl.multiple_of(table_ref[3 * j + 2] * block, block)
                pltpu.make_async_copy(
                    stage.at[at + j], out.at[pl.ds(row, block), pl.ds(col, block)], sem_out
                ).start()
                return carry

            lax.fori_loop(0, len(tables[i]), put, 0)
            at += len(tables[i])
        pltpu.make_async_copy(stage, stage, sem_out).wait()

    results = pl.pallas_call(
        body,
        out_shape=[jax.ShapeDtypeStruct(shapes[i], LOW) for i in used],
        in_specs=[SMEM] * len(used) + [ANY] * (1 + len(known)),
        out_specs=[ANY] * len(used),
        input_output_aliases={len(used) + 1 + j: used.index(i) for j, i in enumerate(known)},
        scratch_shapes=[
            pltpu.VMEM((count, block, block), LOW),
            pltpu.SemaphoreType.DMA,
            pltpu.SemaphoreType.DMA,
        ],
        compiler_params=pltpu.CompilerParams(vmem_limit_bytes=VMEM_LIMIT),
        cost_estimate=pl.CostEstimate(
            flops=0, bytes_accessed=4 * count * block * block, transcendentals=0
        ),
        name="place_blocks",
    )(
        *[jnp.asarray(tables[i].reshape(-1)) for i in used],
        gathered,
        *[partial[i] for i in known],
    )
    merged = list(partial)
    for i, value in zip(used, results):
        merged[i] = value
    return merged


def fill(scratch, pieces, order_ref):
    count = pieces[0].shape[0]
    for i, piece in enumerate(pieces):
        if order_ref is None:
            scratch[i * count : (i + 1) * count] = piece[...]
        else:
            scratch[pl.ds(pl.multiple_of(order_ref[i] * count, count), count)] = piece[...]


def grad_blocks(
    left, rights, order, pairs, table, wide, buffers, sizes, block, span=None, done=()
):
    tokens, height = left.shape
    by_column = len(rights) > 1 and rights[0].shape[0] == tokens
    width = sum(x.shape[-1] for x in rights) if by_column else rights[0].shape[-1]
    if pairs:
        width *= 2
    rows, cols = height // block, width // block
    if pairs:
        table = np.stack([table[: cols // 2], table[cols // 2 :]], 1).reshape(table.shape)
        wide = 2
    first, end = (0, cols // wide) if span is None else span
    steps = end - first
    if steps <= 0:
        return buffers
    assert not by_column or wide == 1
    per_step = rows * wide
    targets = [
        [(j, x, spot) for j, (x, spot) in enumerate(step) if (x, spot) not in done]
        for step in table.reshape(cols // wide, per_step, 2).tolist()[first:end]
    ]
    assert all(targets)
    used = sorted({x for step in targets for _, x, _ in step})
    known = [x for x in used if buffers[x] is not None]
    n_order = 0 if order is None else 1
    joined = len(rights) > 1
    first_known = n_order + 1 + len(rights)
    first_out = first_known + len(known)

    def body(*refs):
        left_ref = refs[n_order]
        right_refs = refs[n_order + 1 : first_known]
        outs = refs[first_out : first_out + len(used)]
        stage, sems = refs[first_out + len(used) : first_out + len(used) + 2]
        t = pl.program_id(0)
        slot = lax.rem(t, 2)
        if joined:
            right_ref = refs[-1]
            if by_column:
                step = 0
                for piece in right_refs:
                    for at in range(0, piece.shape[1], block):

                        @pl.when(t + first == step)
                        def _(piece=piece, at=at):
                            right_ref[...] = piece[:, at : at + block]

                        step += 1
            else:
                fill(right_ref, right_refs, refs[0] if n_order else None)
            taken = right_ref[...]
        elif pairs:
            taken = jnp.concatenate([right_refs[0][0], right_refs[0][1]], axis=1)
        else:
            taken = right_refs[0][...]

        def finish(step):
            sent = stage.at[step % 2, : len(targets[step])]
            pltpu.make_async_copy(sent, sent, sems.at[step % 2]).wait()

        for step in range(2, steps):

            @pl.when(t == step)
            def _(step=step):
                finish(step - 2)

        def some(i, carry):
            at = pl.multiple_of(i * (few * block), block)
            part = lax.dot_general(
                left_ref[:, pl.ds(at, few * block)],
                taken,
                (((0,), (0,)), ((), ())),
                preferred_element_type=F32,
            ).astype(LOW)
            for r in range(few):
                for c in range(wide):
                    stage[slot, c * rows + i * few + r] = part[
                        r * block : (r + 1) * block, c * block : (c + 1) * block
                    ]
            return carry

        parts = 1 if first > 0 or rows < 8 else 2
        few = rows // parts if rows % parts == 0 else rows
        lax.fori_loop(0, rows // few, some, 0)
        for step in range(steps):

            @pl.when(t == step)
            def _(step=step):
                for j, x, spot in targets[step]:
                    pltpu.make_async_copy(
                        stage.at[step % 2, j], outs[used.index(x)].at[spot], sems.at[step % 2]
                    ).start()

        @pl.when(t == steps - 1)
        def _():
            for step in range(max(0, steps - 2), steps):
                finish(step)

    taken_width = wide * block
    if pairs:
        right_specs = [pl.BlockSpec((2, tokens, block), lambda j: (0, 0, first + j))]
    elif by_column:
        right_specs = [pl.BlockSpec(x.shape, lambda j: (0, 0)) for x in rights]
    else:
        right_specs = [
            pl.BlockSpec((x.shape[0], taken_width), lambda j: (0, first + j)) for x in rights
        ]
    results = pl.pallas_call(
        body,
        grid=(steps,),
        out_shape=[jax.ShapeDtypeStruct((sizes[x], block, block), LOW) for x in used],
        in_specs=[SMEM] * n_order
        + [pl.BlockSpec((tokens, height), lambda j: (0, 0))]
        + right_specs
        + [ANY] * len(known),
        out_specs=[ANY] * len(used),
        input_output_aliases={first_known + j: used.index(x) for j, x in enumerate(known)},
        scratch_shapes=[
            pltpu.VMEM((2, per_step, block, block), LOW),
            pltpu.SemaphoreType.DMA((2,)),
        ]
        + ([pltpu.VMEM((tokens, taken_width), LOW)] if joined else []),
        compiler_params=pltpu.CompilerParams(vmem_limit_bytes=VMEM_LIMIT),
        cost_estimate=pl.CostEstimate(
            flops=4 * tokens * height * wide * block * steps,
            bytes_accessed=2 * (tokens * (height + width) + height * width),
            transcendentals=0,
        ),
        name="grad_blocks",
    )(*([] if order is None else [order]), left, *rights, *[buffers[x] for x in known])
    merged = list(buffers)
    for x, value in zip(used, results):
        merged[x] = value
    return merged


def grad_strips(strips, buffer, block):
    def body(*refs):
        out, stage, sem = refs[-3:]
        at = 0
        for i, (_, _, _, half, blocks) in enumerate(strips):
            right = refs[2 * i + 1]
            part = lax.dot_general(
                refs[2 * i][...],
                right[...] if half is None else right[0],
                (((0,), (0,)), ((), ())),
                preferred_element_type=F32,
            ).astype(LOW)
            for c, spot in blocks:
                stage[at] = part[:, c * block : (c + 1) * block]
                pltpu.make_async_copy(stage.at[at], out.at[spot], sem).start()
                at += 1
        pltpu.make_async_copy(stage, stage, sem).wait()

    specs, values = [], []
    for left, row, right, half, blocks in strips:
        tokens = left.shape[0]
        wide = (max(c for c, _ in blocks) + 1) * block
        specs.append(pl.BlockSpec((tokens, block), lambda j, row=row: (0, row)))
        if half is None:
            specs.append(pl.BlockSpec((tokens, wide), lambda j: (0, 0)))
        else:
            specs.append(pl.BlockSpec((1, tokens, wide), lambda j, half=half: (half, 0, 0)))
        values += [left, right]
    count = sum(len(blocks) for *_, blocks in strips)
    return pl.pallas_call(
        body,
        grid=(1,),
        in_specs=specs + [ANY],
        out_specs=ANY,
        out_shape=jax.ShapeDtypeStruct(buffer.shape, LOW),
        input_output_aliases={len(specs): 0},
        scratch_shapes=[pltpu.VMEM((count, block, block), LOW), pltpu.SemaphoreType.DMA],
        compiler_params=pltpu.CompilerParams(vmem_limit_bytes=VMEM_LIMIT),
        cost_estimate=pl.CostEstimate(
            flops=4 * count * values[0].shape[0] * block**2,
            bytes_accessed=4 * count * block * values[0].shape[0],
            transcendentals=0,
        ),
        name="grad_strips",
    )(*values, buffer)


def feed_forward(pieces, weights, hidden_grad, block):
    share, width = pieces[0].shape
    count = len(pieces)
    rows = share * count
    half = rows // 2
    hidden = weights.shape[1] // 2
    steps = hidden // block
    tile = 2 * block

    def body(*refs):
        gate_w, up_w, grad_ref, row_w = refs[count : count + 4]
        hid_ref, out_ref, joined, kept_ref, sent_ref, held = refs[count + 4 :]
        t = pl.program_id(0)

        @pl.when(t == 0)
        def _():
            fill(joined, refs[:count], None)

        @pl.when(t < steps)
        def _():
            both = dot(joined[...], jnp.concatenate([gate_w[...], up_w[...]], axis=1))
            gate, up = both[:, :block], both[:, block:]
            grad = grad_ref[...]
            sig = jax.nn.sigmoid(gate)
            act = gate * sig
            hid_ref[...] = (act * up).astype(LOW)
            here = pl.ds(pl.multiple_of(t * block, block), block)
            gate_grad = (grad * up * sig * (1.0 + gate * (1.0 - sig))).astype(LOW)
            up_grad = (grad * act).astype(LOW)
            out_ref[0] = gate_grad
            out_ref[1] = up_grad
            held[0, :, here] = gate_grad
            held[1, :, here] = up_grad

        @pl.when(t >= steps)
        def _():
            total = dot_turned(held[0], row_w[:, :hidden]) + dot_turned(held[1], row_w[:, hidden:])
            total = total.astype(LOW)
            kept_ref[...] = total[:half]
            sent_ref[...] = total[half:]

    def first(j):
        return jnp.minimum(j, steps - 1)

    def second(j):
        return jnp.maximum(j - steps, 0)

    hid, grads, joined, kept, sent = pl.pallas_call(
        body,
        grid=(steps + width // tile,),
        in_specs=[pl.BlockSpec((share, width), lambda j: (0, 0))]
        + [VMEM] * (count - 1)
        + [
            pl.BlockSpec((width, block), lambda j: (0, first(j))),
            pl.BlockSpec((width, block), lambda j: (0, steps + first(j))),
            pl.BlockSpec((rows, block), lambda j: (0, first(j))),
            pl.BlockSpec((tile, 2 * hidden), lambda j: (second(j), 0)),
        ],
        out_specs=[
            pl.BlockSpec((rows, block), lambda j: (0, first(j))),
            pl.BlockSpec((2, rows, block), lambda j: (0, 0, first(j))),
            pl.BlockSpec((rows, width), lambda j: (0, 0)),
            pl.BlockSpec((half, tile), lambda j: (0, second(j))),
            pl.BlockSpec((half, tile), lambda j: (0, second(j))),
        ],
        out_shape=[
            jax.ShapeDtypeStruct((rows, hidden), LOW),
            jax.ShapeDtypeStruct((2, rows, hidden), LOW),
            jax.ShapeDtypeStruct((rows, width), LOW),
            jax.ShapeDtypeStruct((half, width), LOW),
            jax.ShapeDtypeStruct((half, width), LOW),
        ],
        scratch_shapes=[pltpu.VMEM((2, rows, hidden), LOW)],
        compiler_params=pltpu.CompilerParams(vmem_limit_bytes=48 * 1024 * 1024),
        cost_estimate=pl.CostEstimate(
            flops=8 * rows * width * hidden,
            bytes_accessed=2 * rows * width + 8 * width * hidden + 10 * rows * hidden,
            transcendentals=rows * hidden,
        ),
        name="feed_forward",
    )(pieces[0], *[held(x) for x in pieces[1:]], weights, weights, hidden_grad, weights)
    return hid, grads, joined, sent, kept


def project_rows(parts, weights, order, turned, tile):
    stacked = parts[0].ndim == 3
    rows = parts[0].shape[-2]
    half = rows // 2
    widths = [parts[0].shape[2]] * parts[0].shape[0] if stacked else [x.shape[1] for x in parts]
    starts = [sum(widths[:i]) for i in range(len(widths))]
    width = weights.shape[0] if turned else weights.shape[1]
    depth = sum(widths)
    share = rows // 4
    n_order = 0 if order is None else 1

    def body(*refs):
        part_refs = refs[n_order : n_order + len(parts)]
        w_ref, kept_ref, sent_ref = refs[n_order + len(parts) : n_order + len(parts) + 3]
        if n_order:
            joined = refs[-1]

            @pl.when(pl.program_id(0) == 0)
            def _():
                for i in range(4):
                    take = pl.ds(pl.multiple_of(refs[0][i] * share, share), share)
                    for part, at, size in zip(part_refs, starts, widths):
                        joined[i * share : (i + 1) * share, at : at + size] = part[take]

            pieces = [(joined[...], 0, depth)]
        elif stacked:
            pieces = [(part_refs[0][i], at, widths[i]) for i, at in enumerate(starts)]
        else:
            pieces = [(p[...], at, size) for p, at, size in zip(part_refs, starts, widths)]
        total = None
        for value, at, size in pieces:
            if turned:
                one = dot_turned(value, w_ref[:, at : at + size])
            else:
                one = dot(value, w_ref[at : at + size])
            total = one if total is None else total + one
        total = total.astype(LOW)
        kept_ref[...] = total[:half]
        sent_ref[...] = total[half:]

    whole = [pl.BlockSpec(x.shape, lambda j, n=x.ndim: (0,) * n) for x in parts]
    if turned:
        weight_spec = pl.BlockSpec((tile, depth), lambda j: (j, 0))
    else:
        weight_spec = pl.BlockSpec((depth, tile), lambda j: (0, j))
    kept, sent = pl.pallas_call(
        body,
        grid=(width // tile,),
        in_specs=[SMEM] * n_order + whole + [weight_spec],
        out_specs=[pl.BlockSpec((half, tile), lambda j: (0, j))] * 2,
        out_shape=[jax.ShapeDtypeStruct((half, width), LOW)] * 2,
        scratch_shapes=[pltpu.VMEM((rows, depth), LOW)] * n_order,
        compiler_params=pltpu.CompilerParams(vmem_limit_bytes=VMEM_LIMIT),
        cost_estimate=pl.CostEstimate(
            flops=2 * rows * depth * width,
            bytes_accessed=2 * (rows * depth + depth * width + rows * width),
            transcendentals=0,
        ),
        name="project_rows",
    )(*([order] if n_order else []), *parts, weights)
    return sent, kept


def down_back(grads, weights):
    rows, depth = grads.shape
    hidden = weights.shape[0]
    tile = 2 * LANES
    full, rest = divmod(hidden, tile)

    def body(g_ref, w_ref, *refs):
        o_ref = refs[-1]
        t = pl.program_id(0)

        @pl.when(t < full)
        def _():
            o_ref[...] = dot_turned(g_ref[...], w_ref[...])

        if rest:

            @pl.when(t == full)
            def _():
                o_ref[:, :rest] = dot_turned(g_ref[...], refs[0][...])

    assert rest == 0 or hidden % rest == 0
    specs = [
        pl.BlockSpec((rows, depth), lambda j: (0, 0)),
        pl.BlockSpec((tile, depth), lambda j: (jnp.minimum(j, full - 1), 0)),
    ]
    if rest:
        specs.append(pl.BlockSpec((rest, depth), lambda j: (hidden // rest - 1, 0)))
    return pl.pallas_call(
        body,
        grid=(full + (rest > 0),),
        in_specs=specs,
        out_specs=pl.BlockSpec((rows, tile), lambda j: (0, j)),
        out_shape=jax.ShapeDtypeStruct((rows, hidden), F32),
        compiler_params=pltpu.CompilerParams(vmem_limit_bytes=VMEM_LIMIT),
        cost_estimate=pl.CostEstimate(
            flops=2 * rows * depth * hidden,
            bytes_accessed=2 * depth * (rows + hidden) + 4 * rows * hidden,
            transcendentals=0,
        ),
        name="down_back",
    )(grads, *([weights] * len(specs[1:])))


def to_heads(pieces, weights, order):
    share = pieces[0].shape[0]
    width = weights.shape[0]

    rows = share * len(pieces)
    depth = weights.shape[1]
    tile = 2 * LANES

    def body(order_ref, *refs):
        w_ref, out_ref = refs[-2:]
        for i, piece in enumerate(refs[:-2]):
            put = pl.ds(pl.multiple_of(order_ref[i] * share, share), share)
            out_ref[put] = dot_turned(piece[...], w_ref[...]).astype(LOW)

    return pl.pallas_call(
        body,
        grid=(width // tile,),
        in_specs=[SMEM]
        + [pl.BlockSpec((share, depth), lambda j: (0, 0))] * len(pieces)
        + [pl.BlockSpec((tile, depth), lambda j: (j, 0))],
        out_specs=pl.BlockSpec((rows, tile), lambda j: (0, j)),
        out_shape=jax.ShapeDtypeStruct((rows, width), LOW),
        compiler_params=pltpu.CompilerParams(vmem_limit_bytes=VMEM_LIMIT),
        cost_estimate=pl.CostEstimate(
            flops=2 * rows * width * depth,
            bytes_accessed=2 * (rows + width) * depth,
            transcendentals=0,
        ),
        name="to_heads",
    )(order, *pieces, weights)


LANES = 128
QUERIES = 256
LONGEST = 512


def turn(values, cos, sin):
    lane = lax.broadcasted_iota(jnp.int32, values.shape, 1)
    other = jnp.where(
        lane % HD < HD // 2,
        pltpu.roll(values, LANES - HD // 2, 1),
        pltpu.roll(values, HD // 2, 1),
    )
    return values * cos + other * sin


def key_tables(cos, sin):
    lane = lax.broadcasted_iota(jnp.int32, cos.shape, 1)
    return jnp.where(lane < HD, cos, 1.0), jnp.where(lane < HD, sin, 0.0)


def project_heads(inputs, weights, cos, sin):
    rows, depth = inputs.shape
    width = weights.shape[1]
    assert width % LANES == 0 and HD == 64

    def body(x_ref, w_ref, cos_ref, sin_ref, q_ref, kv_ref):
        t = pl.program_id(0)

        def one(i, carry):
            here = pl.ds(pl.multiple_of(i * QUERIES, QUERIES), QUERIES)
            raw = dot(x_ref[here], w_ref[...])

            @pl.when(t < steps - 1)
            def _():
                turned = turn(raw, cos_ref[here], sin_ref[here])
                q_ref[here] = turned.astype(LOW) * LOW(HD**-0.5)

            @pl.when(t == steps - 1)
            def _():
                kv_ref[here] = turn(raw, *key_tables(cos_ref[here], sin_ref[here])).astype(LOW)

            return carry

        lax.fori_loop(0, rows // QUERIES, one, 0)

    steps = width // LANES
    whole = pl.BlockSpec((rows, LANES), lambda j: (0, 0))
    return pl.pallas_call(
        body,
        grid=(steps,),
        in_specs=[
            pl.BlockSpec((rows, depth), lambda j: (0, 0)),
            pl.BlockSpec((depth, LANES), lambda j: (0, j)),
            whole,
            whole,
        ],
        out_specs=[pl.BlockSpec((rows, LANES), lambda j: (0, jnp.minimum(j, steps - 2))), whole],
        out_shape=[
            jax.ShapeDtypeStruct((rows, width - LANES), LOW),
            jax.ShapeDtypeStruct((rows, LANES), LOW),
        ],
        compiler_params=pltpu.CompilerParams(vmem_limit_bytes=VMEM_LIMIT),
        cost_estimate=pl.CostEstimate(
            flops=2 * rows * depth * width,
            bytes_accessed=2 * (rows * depth + depth * width + rows * width),
            transcendentals=0,
        ),
        name="project_heads",
    )(inputs, weights, cos, sin)


def keep_keys(padded, kv_ref):
    padded[:LONGEST] = jnp.zeros((LONGEST, LANES), LOW)
    padded[LONGEST:] = kv_ref[...]


def visible(start_ref, at):
    shape = (LONGEST + QUERIES, QUERIES)
    key = at - LONGEST + lax.broadcasted_iota(jnp.int32, shape, 0)
    query = at + lax.broadcasted_iota(jnp.int32, shape, 1)
    return (key >= start_ref[:, pl.ds(at, QUERIES)]) & (key <= query)


def attend(queries, kv, starts):
    rows, width = queries.shape
    groups = width // LANES

    def body(start_ref, q_ref, kv_ref, o_ref, log_ref, padded):
        @pl.when(pl.program_id(0) == 0)
        def _():
            keep_keys(padded, kv_ref)

        def one(i, carry):
            at = pl.multiple_of(i * QUERIES, QUERIES)
            here = pl.ds(at, QUERIES)
            seen = visible(start_ref, at)
            window = padded[pl.ds(at, LONGEST + QUERIES)]
            keys, values = window[:, :HD], window[:, HD:]
            for h in range(LANES // HD):
                query = q_ref[here, h * HD : (h + 1) * HD]
                scores = jnp.where(seen, dot_turned(keys, query), -1e30)
                top = jnp.max(scores, axis=0, keepdims=True)
                expo = jnp.exp(scores - top)
                total = jnp.sum(expo, axis=0, keepdims=True)
                probs = (expo * (1.0 / total)).astype(LOW)
                o_ref[here, h * HD : (h + 1) * HD] = lax.dot_general(
                    probs, values, (((0,), (0,)), ((), ())), preferred_element_type=F32
                ).astype(LOW)
                log_ref[0, h : h + 1, here] = top + jnp.log(total)
            return carry

        lax.fori_loop(0, rows // QUERIES, one, 0)

    column = pl.BlockSpec((rows, LANES), lambda j: (0, j))
    return pl.pallas_call(
        body,
        grid=(groups,),
        in_specs=[
            pl.BlockSpec((1, rows), lambda j: (0, 0)),
            column,
            pl.BlockSpec((rows, LANES), lambda j: (0, 0)),
        ],
        out_specs=[column, pl.BlockSpec((1, LANES // HD, rows), lambda j: (j, 0, 0))],
        out_shape=[
            jax.ShapeDtypeStruct((rows, width), LOW),
            jax.ShapeDtypeStruct((groups, LANES // HD, rows), F32),
        ],
        scratch_shapes=[pltpu.VMEM((LONGEST + rows, LANES), LOW)],
        compiler_params=pltpu.CompilerParams(vmem_limit_bytes=VMEM_LIMIT),
        cost_estimate=pl.CostEstimate(
            flops=30 * rows * rows * width,
            bytes_accessed=4 * rows * width,
            transcendentals=rows * rows * width // HD,
        ),
        name="attend",
    )(starts, queries, kv)


def attend_back(queries, kv, starts, logs, grads, cos, sin):
    rows, width = queries.shape
    groups = width // LANES

    def body(
        start_ref, q_ref, kv_ref, log_ref, g_ref, cos_ref, sin_ref, dq_ref, sum_ref, acc, padded
    ):
        @pl.when(pl.program_id(0) == 0)
        def _():
            keep_keys(padded, kv_ref)
            acc[...] = jnp.zeros_like(acc)

        def one(i, carry):
            at = pl.multiple_of(i * QUERIES, QUERIES)
            here = pl.ds(at, QUERIES)
            there = pl.ds(at, LONGEST + QUERIES)
            seen = visible(start_ref, at)
            window = padded[there]
            keys, values = window[:, :HD], window[:, HD:]
            parts = []
            key_part, value_part = 0.0, 0.0
            for h in range(LANES // HD):
                query = q_ref[here, h * HD : (h + 1) * HD]
                grad = g_ref[here, h * HD : (h + 1) * HD]
                scores = jnp.where(seen, dot_turned(keys, query), -1e30)
                probs = jnp.exp(scores - log_ref[0, h : h + 1, here])
                value_part += dot(probs.astype(LOW), grad)
                prob_grads = dot_turned(values, grad)
                inner = jnp.sum(probs * prob_grads, axis=0, keepdims=True)
                score_grads = (probs * (prob_grads - inner)).astype(LOW)
                key_part += dot(score_grads, query)
                parts.append(
                    lax.dot_general(
                        score_grads, keys, (((0,), (0,)), ((), ())), preferred_element_type=F32
                    )
                )
            acc[there] += jnp.concatenate([key_part, value_part], axis=1)
            dq_ref[here] = turn(
                jnp.concatenate(parts, axis=1) * HD**-0.5, cos_ref[here], -sin_ref[here]
            ).astype(LOW)
            return carry

        lax.fori_loop(0, rows // QUERIES, one, 0)

        @pl.when(pl.program_id(0) == groups - 1)
        def _():
            key_cos, key_sin = key_tables(cos_ref[...], sin_ref[...])
            sum_ref[...] = turn(acc[LONGEST:], key_cos, -key_sin).astype(LOW)

    column = pl.BlockSpec((rows, LANES), lambda j: (0, j))
    whole = pl.BlockSpec((rows, LANES), lambda j: (0, 0))
    return pl.pallas_call(
        body,
        grid=(groups,),
        in_specs=[
            pl.BlockSpec((1, rows), lambda j: (0, 0)),
            column,
            whole,
            pl.BlockSpec((1, LANES // HD, rows), lambda j: (j, 0, 0)),
            column,
            whole,
            whole,
        ],
        out_specs=[column, whole],
        out_shape=[
            jax.ShapeDtypeStruct((rows, width), LOW),
            jax.ShapeDtypeStruct((rows, LANES), LOW),
        ],
        scratch_shapes=[
            pltpu.VMEM((LONGEST + rows, LANES), F32),
            pltpu.VMEM((LONGEST + rows, LANES), LOW),
        ],
        compiler_params=pltpu.CompilerParams(vmem_limit_bytes=VMEM_LIMIT),
        cost_estimate=pl.CostEstimate(
            flops=80 * rows * rows * width,
            bytes_accessed=16 * rows * width,
            transcendentals=rows * rows * width // HD,
        ),
        name="attend_back",
    )(starts, queries, kv, logs, grads, cos, sin)


def shampoo(sums, places, factor, weights, ema, left, right, left_roots, right_roots, before):
    count, block, _ = sums.shape
    group = 3 if count % 3 == 0 else 2 if count % 2 == 0 else 1
    steps = count // group
    depth = min(4, steps)
    extra = [] if before is None else list(before)

    def mm(a, b, dims):
        return lax.dot_general(
            a.astype(LOW), b.astype(LOW), (dims, ((), ())), preferred_element_type=F32
        )

    def body(places_ref, g_ref, *refs):
        ins, outs = refs[:6], refs[6 + len(extra) : 11 + len(extra)]
        given, made, sem_in, sem_out = refs[11 + len(extra) :]

        def load(t, slot):
            for u in range(group):
                place = places_ref[t * group + u]
                for i, ref in enumerate(ins):
                    pltpu.make_async_copy(
                        ref.at[place], given.at[slot, u, i], sem_in.at[slot]
                    ).start()

        def wait(buffer, slot, sems):
            pltpu.make_async_copy(buffer.at[slot], buffer.at[slot], sems.at[slot]).wait()

        for t in range(depth):
            load(t, t)

        def step(t, carry):
            slot = lax.rem(t, depth)
            wait(given, slot, sem_in)

            @pl.when(t >= depth)
            def _():
                wait(made, slot, sem_out)

            both = 0.5 * factor * factor
            for u in range(group):
                low = g_ref[t * group + u]
                made[slot, u, 0] = low.astype(F32) * factor
                made[slot, u, 3] = 0.5 * given[slot, u, 2] + both * mm(low, low, ((1,), (1,)))
                made[slot, u, 4] = 0.5 * given[slot, u, 3] + both * mm(low, low, ((0,), (0,)))
                part = mm(low, given[slot, u, 5], ((1,), (0,))) * factor
                fresh = given[slot, u, 0] - weight_rate * mm(given[slot, u, 4], part, ((1,), (0,)))
                made[slot, u, 1] = fresh
                made[slot, u, 2] = (
                    average_decay * given[slot, u, 1] + (1.0 - average_decay) * fresh
                )
            for u in range(group):
                place = places_ref[t * group + u]
                for i, ref in enumerate(outs):
                    pltpu.make_async_copy(
                        made.at[slot, u, i], ref.at[place], sem_out.at[slot]
                    ).start()

            @pl.when(t + depth < steps)
            def _():
                load(t + depth, slot)

            return carry

        lax.fori_loop(0, steps, step, 0)
        for t in range(steps - depth, steps):
            wait(made, t % depth, sem_out)

    return pl.pallas_call(
        body,
        out_shape=[jax.ShapeDtypeStruct(weights.shape, F32)] * 5,
        in_specs=[SMEM, VMEM] + [ANY] * (6 + len(extra)),
        out_specs=[ANY] * 5,
        input_output_aliases={8 + i: i for i in range(len(extra))},
        scratch_shapes=[
            pltpu.VMEM((depth, group, 6, block, block), F32),
            pltpu.VMEM((depth, group, 5, block, block), F32),
            pltpu.SemaphoreType.DMA((depth,)),
            pltpu.SemaphoreType.DMA((depth,)),
        ],
        compiler_params=pltpu.CompilerParams(vmem_limit_bytes=VMEM_LIMIT),
        cost_estimate=pl.CostEstimate(
            flops=8 * count * block**3,
            bytes_accessed=46 * count * block * block,
            transcendentals=0,
        ),
        name="shampoo",
    )(places, sums, weights, ema, left, right, left_roots, right_roots, *extra)


def rows_call(body, ins, outs, name, step=128, work=10, here=None):
    rows = max(x.shape[0] for x in ins)

    def spec(x):
        if x.shape[0] == rows:
            return pl.BlockSpec((step, x.shape[1]), lambda j: (j, 0))
        return pl.BlockSpec(x.shape, lambda j: (0, 0))

    return pl.pallas_call(
        body,
        grid=(rows // step,),
        in_specs=[VMEM if i == here else spec(x) for i, x in enumerate(ins)],
        out_specs=[spec(x) for x in outs],
        out_shape=outs,
        compiler_params=pltpu.CompilerParams(vmem_limit_bytes=VMEM_LIMIT),
        cost_estimate=pl.CostEstimate(
            flops=work * rows * ins[0].shape[1],
            bytes_accessed=sum(x.size * x.dtype.itemsize for x in list(ins) + list(outs)),
            transcendentals=0,
        ),
        name=name,
    )(*ins)


def add_near(kept, got):
    share = kept.shape[0] // 2
    width = kept.shape[1]
    step = 128

    def body(a_ref, c_ref, got_ref, mine_ref, other_ref):
        at = pl.multiple_of(pl.program_id(0) * step, step)
        near, far = got_ref[pl.ds(at, step)], got_ref[pl.ds(share + at, step)]
        mine_ref[...] = a_ref[...].astype(F32) + near.astype(F32)
        other_ref[...] = (c_ref[...].astype(F32) + far.astype(F32)).astype(LOW)

    first = pl.BlockSpec((step, width), lambda j: (j, 0))
    second = pl.BlockSpec((step, width), lambda j: (share // step + j, 0))
    return pl.pallas_call(
        body,
        grid=(share // step,),
        in_specs=[first, second, VMEM],
        out_specs=[first] * 2,
        out_shape=[
            jax.ShapeDtypeStruct((share, width), F32),
            jax.ShapeDtypeStruct((share, width), LOW),
        ],
        compiler_params=pltpu.CompilerParams(vmem_limit_bytes=VMEM_LIMIT),
        cost_estimate=pl.CostEstimate(
            flops=2 * share * width, bytes_accessed=14 * share * width, transcendentals=0
        ),
        name="add_near",
    )(kept, kept, held(got))


def second_norm(tokens, mine, got, gain):
    step = 128

    def body(x_ref, a_ref, b_ref, gain_ref, middle_ref, low_ref):
        got = b_ref[pl.ds(pl.multiple_of(pl.program_id(0) * step, step), step)]
        middle = x_ref[...].astype(F32) + (a_ref[...] + got.astype(F32))
        middle_ref[...] = middle
        scale = lax.rsqrt(jnp.mean(middle * middle, axis=-1, keepdims=True) + 1e-05)
        low_ref[...] = (middle * scale * gain_ref[...]).astype(LOW)

    return rows_call(
        body,
        [tokens, mine, held(got), gain],
        [jax.ShapeDtypeStruct(tokens.shape, F32), jax.ShapeDtypeStruct(tokens.shape, LOW)],
        "second_norm",
        step,
        here=2,
    )


def first_norm(tokens, gain):
    def body(x_ref, gain_ref, low_ref):
        x = x_ref[...].astype(F32)
        scale = lax.rsqrt(jnp.mean(x * x, axis=-1, keepdims=True) + 1e-05)
        low_ref[...] = (x * scale * gain_ref[...]).astype(LOW)

    return rows_call(
        body,
        [tokens, gain],
        [jax.ShapeDtypeStruct(tokens.shape, LOW)],
        "first_norm",
    )[0]


def norm_back(values, mine, got, gain, residual):
    step = 128

    def body(x_ref, a_ref, b_ref, gain_ref, r_ref, out_ref, low_ref, sum_ref):
        x = x_ref[...].astype(F32)
        got = b_ref[pl.ds(pl.multiple_of(pl.program_id(0) * step, step), step)]
        grad = a_ref[...] + got.astype(F32)
        scale = lax.rsqrt(jnp.mean(x * x, axis=-1, keepdims=True) + 1e-05)
        unit = x * scale
        scaled = grad * gain_ref[...]
        out = r_ref[...].astype(F32) + scale * (
            scaled - unit * jnp.mean(scaled * unit, axis=-1, keepdims=True)
        )
        out_ref[...] = out
        low_ref[...] = out.astype(LOW)

        @pl.when(pl.program_id(0) == 0)
        def _():
            sum_ref[...] = jnp.zeros_like(sum_ref)

        sum_ref[...] += jnp.sum(grad * unit, axis=0, keepdims=True)

    shape = values.shape
    return rows_call(
        body,
        [values, mine, held(got), gain, residual],
        [
            jax.ShapeDtypeStruct(shape, F32),
            jax.ShapeDtypeStruct(shape, LOW),
            jax.ShapeDtypeStruct((1, shape[1]), F32),
        ],
        "norm_back",
        step,
        here=2,
        work=1000000,
    )


def doc_positions(doc_ids):
    length = doc_ids.shape[-1]
    offsets = jnp.arange(length, dtype=jnp.int32)
    starts = jnp.concatenate(
        [jnp.ones(doc_ids.shape[:-1] + (1,), jnp.bool_), doc_ids[..., 1:] != doc_ids[..., :-1]],
        axis=-1,
    )
    first_index = lax.cummax(jnp.where(starts, offsets, 0), axis=doc_ids.ndim - 1)
    return offsets - first_index


def rope_tables(positions, head_size):
    half_size = head_size // 2
    exponent = jnp.arange(half_size, dtype=F32) * (2.0 / head_size)
    inverse = jnp.power(F32(10000.0), -exponent)
    angles = positions.astype(F32)[..., None] * inverse
    cos, sin = jnp.cos(angles), jnp.sin(angles)
    repeats = LANES // head_size
    return (
        jnp.concatenate([cos, cos] * repeats, axis=-1),
        jnp.concatenate([-sin, sin] * repeats, axis=-1),
    )


def after(value, *others):
    return lax.optimization_barrier((value,) + others)[0]


def dot(left, right):
    return jnp.dot(left, right, preferred_element_type=F32)


def dot_turned(left, right):
    return lax.dot_general(left, right, (((1,), (1,)), ((), ())), preferred_element_type=F32)


EXCHANGE = (0, 2, 1, 3)


def on_device(
    tokens_in,
    cotangent,
    select_mask,
    doc_ids,
    norm_gains,
    weight_blocks,
    ema_blocks,
    left_stats,
    right_stats,
    left_roots,
    right_roots,
):
    mp_count = lax.axis_size("mp")
    dp_count = lax.axis_size("dp")
    sequences, length, model_width = tokens_in.shape
    assert sequences == 1 and mp_count == 4 and dp_count & (dp_count - 1) == 0
    rows = sequences * length
    own, block, _ = weight_blocks.shape
    query_cols = HEADS * HD // mp_count
    key_cols = KV_HEADS * HD // mp_count
    hidden_cols = FF // mp_count
    assert KV_HEADS == mp_count and length % QUERIES == 0
    row_blocks = model_width // block
    attn_blocks = (query_cols + 2 * key_cols) // block
    hidden_blocks = hidden_cols // block
    in_blocks = attn_blocks + 2 * hidden_blocks
    out_attn_blocks = query_cols // block
    share = rows // mp_count
    m_index = lax.axis_index("mp")
    d_index = lax.axis_index("dp")

    plan = Layout(dp_count, own, row_blocks, attn_blocks, in_blocks, out_attn_blocks)
    order = lax.dynamic_slice_in_dim(jnp.asarray(plan.order), d_index, 1, 0).reshape(-1)
    shapes = [
        (model_width, attn_blocks * block),
        (query_cols, model_width),
        (model_width, 2 * hidden_cols),
        (hidden_cols, model_width),
    ]

    def partner(values, bit):
        return lax.ppermute(values, "mp", [(i, i ^ bit) for i in range(mp_count)])

    def true_share(values, group):
        return lax.dynamic_slice_in_dim(values, (m_index ^ group) * share, share, 0)

    def to_exchange(values):
        return jnp.concatenate([true_share(values, g) for g in EXCHANGE], axis=0)

    def to_true(parts):
        by_group = [parts[EXCHANGE.index(g)] for g in range(4)]
        low, high = m_index & 1, m_index & 2
        pairs = []
        for a, b in ((0, 1), (2, 3)):
            pairs.append(
                (
                    jnp.where(low == 0, by_group[a], by_group[b]),
                    jnp.where(low == 0, by_group[b], by_group[a]),
                )
            )
        flat = []
        for first, second in ((0, 1), (1, 0)):
            for i in range(2):
                flat.append(jnp.where(high == 0, pairs[first][i], pairs[second][i]))
        return jnp.concatenate(flat, axis=0)

    def near_sum(sent, kept):
        return add_near(kept, partner(sent, 1))

    def spread_share(mine, *cover):
        far = partner(mine, 2)
        near = partner(mine, 1)
        if cover:
            far = after(far, *cover)
        return [mine, far, near, partner(far, 1)]

    sorted_low = list(sort_blocks(weight_blocks, order, plan.chunks[:1]))
    if len(plan.chunks) > 1:
        sorted_low += sort_blocks(
            weight_blocks, after(order, *sorted_low), plan.chunks[1:]
        )
    gathered = [
        lax.all_gather(chunk, "dp", axis=0, tiled=True, axis_index_groups=[plan.ring])
        for chunk in sorted_low
    ]
    none = np.zeros((0, 3), np.int32)
    last = len(gathered) - 1

    def place(x, source, which, matrices):
        tables = [plan.of_chunk(x, i) if i in which else none for i in range(4)]
        return place_blocks(source, tables, shapes, matrices)

    matrices = place(0, gathered[0], (0, 1, 2, 3), [None] * 4)
    w_qkv = matrices[0]
    if last >= 1:
        matrices = place(1, gathered[1], (1,), matrices)
    w_attn_out = matrices[1]

    positions = doc_positions(doc_ids)
    starts = jnp.arange(length, dtype=jnp.int32)[None] - positions
    cos, sin = rope_tables(positions[0], HD)

    tokens_low = tokens_in.reshape(rows, model_width)
    first_in = first_norm(tokens_low, norm_gains[:1])
    out_grad = cotangent.reshape(rows, model_width) * select_mask.astype(LOW).reshape(rows, 1)
    own_tokens = true_share(tokens_low, 0)
    own_grad = true_share(out_grad, 0)
    mlp_grad = to_exchange(out_grad)
    tokens_local = to_exchange(tokens_low)
    unit_scale = lax.rsqrt(
        jnp.mean(jnp.square(tokens_local.astype(F32)), axis=-1, keepdims=True) + 1e-05
    )

    shares = (m_index ^ jnp.array(EXCHANGE, jnp.int32)).astype(jnp.int32)
    queries, kv = project_heads(first_in, w_qkv, cos, sin)
    kv, mlp_grad, own_tokens, own_grad, tokens_local, unit_scale = lax.optimization_barrier(
        (kv, mlp_grad, own_tokens, own_grad, tokens_local, unit_scale)
    )
    mixed, logs = attend(queries, kv, starts)
    attended_sent, attended_kept = project_rows([mixed], w_attn_out, shares, False, 512)
    mine, other = near_sum(attended_sent, attended_kept)
    if last >= 1:
        matrices = place(1, after(gathered[1], other), (2, 3), matrices)
        mine, *matrices[2:] = lax.optimization_barrier((mine, *matrices[2:]))
    middle, second_low = second_norm(own_tokens, mine, partner(other, 2), norm_gains[1:])
    if last >= 2:
        matrices = place(2, after(gathered[2], second_low), (2, 3), matrices)
    w_gateup, w_down = matrices[2:]
    hidden_grad = down_back(mlp_grad, w_down)
    second_pieces = spread_share(second_low, hidden_grad)
    hidden, gateup_grad, second_in, second_sent, second_kept = feed_forward(
        second_pieces, w_gateup, hidden_grad, block
    )

    sizes = [dp_count * n for _, n in plan.chunks]
    sums = [None] * len(sizes)
    reduced = [None] * len(sizes)

    def scatter(x):
        reduced[x] = lax.psum_scatter(
            sums[x], "dp", scatter_dimension=0, tiled=True, axis_index_groups=[plan.ring]
        )

    def known(values):
        return [x for x in values if x is not None]

    cuts = {2: 0, 3: 0}
    sent = set()
    if last >= 2:
        cuts = {2: plan.first_late[2], 3: plan.first_late[3] // 2}
        sent = {(last, spot) for *_, spot in plan.strips}
    def down_grads(sums, hidden, span):
        table = plan.of_matrix(3, hidden_blocks, row_blocks)
        return grad_blocks(
            hidden, [mlp_grad], None, False, table, 2, sums, sizes, block, span, sent
        )

    def gateup_grads(sums, second_in, span):
        table = plan.of_matrix(2, row_blocks, 2 * hidden_blocks)
        return grad_blocks(
            second_in, [gateup_grad], None, True, table, 2, sums, sizes, block, span, sent
        )

    sums = down_grads(sums, after(hidden, second_sent), (cuts[3], row_blocks // 2))
    mine, other = near_sum(second_sent, after(second_kept, *known(sums)))
    if sent:
        strips = {}
        for matrix, r, c, spot in plan.strips:
            half = c // hidden_blocks if matrix == 2 else None
            at = c if half is None else c % hidden_blocks
            strips.setdefault((matrix, r, half), []).append((at, spot))
        sums[last] = grad_strips(
            [
                (
                    after(second_in, other) if matrix == 2 else hidden,
                    r,
                    gateup_grad if matrix == 2 else mlp_grad,
                    half,
                    blocks,
                )
                for (matrix, r, half), blocks in strips.items()
            ],
            sums[last],
            block,
        )

    sums = gateup_grads(sums, after(second_in, other), (cuts[2], hidden_blocks))
    if last >= 2:
        scatter(2)
    got = partner(other, 2)
    mine = after(mine, *known(sums[:2]))
    middle_grad, attn_low, second_gain = norm_back(
        middle, mine, got, norm_gains[1:], own_grad
    )
    sums = gateup_grads(sums, after(second_in, attn_low), (0, cuts[2]))
    sums = down_grads(sums, after(hidden, attn_low), (0, cuts[3]))
    attn_grad = spread_share(attn_low, *known(sums[:2]))
    sums = grad_blocks(
        mixed,
        attn_grad,
        shares,
        False,
        plan.of_matrix(1, out_attn_blocks, row_blocks),
        4,
        sums,
        sizes,
        block,
    )
    if last >= 1:
        scatter(1)

    feed_sent, feed_kept = project_rows(
        [after(hidden, *known(sums[:2]))], w_down, None, False, 512
    )
    feed_mine, feed_other = near_sum(feed_sent, feed_kept)
    mixed_grad = to_heads(attn_grad, after(w_attn_out, feed_other), shares)
    query_grad, kv_grad = attend_back(queries, kv, starts, logs, mixed_grad, cos, sin)
    feed_part = after(feed_mine, query_grad) + partner(feed_other, 2).astype(F32)
    out_low = (middle + feed_part).astype(LOW)
    qkv_grads = [query_grad, kv_grad]
    first_sent, first_kept = project_rows(
        [after(query_grad, out_low), kv_grad], w_qkv, shares, True, 512
    )
    mine, other = near_sum(first_sent, first_kept)

    half = rows // 2
    first_gain = sum(
        jnp.sum(part.astype(F32) * (x.astype(F32) * scale), axis=0, keepdims=True)
        for part, x, scale in (
            (first_kept, tokens_local[:half], unit_scale[:half]),
            (first_sent, tokens_local[half:], unit_scale[half:]),
        )
    )
    gain_sums = jnp.concatenate([first_gain, second_gain], axis=0)
    gain_sums = gain_sums + partner(gain_sums, 2)
    other = after(other, gain_sums)
    sums = grad_blocks(
        after(first_in, other),
        qkv_grads,
        None,
        False,
        plan.of_matrix(0, row_blocks, attn_blocks),
        1,
        sums,
        sizes,
        block,
    )
    scatter(0)
    factor = float(rows * dp_count) ** (-0.5)

    def update(x, state, *others):
        start, count = plan.chunks[x]
        return shampoo(
            reduced[x],
            after(lax.slice_in_dim(order, start, start + count), *others),
            factor,
            weight_blocks,
            ema_blocks,
            left_stats,
            right_stats,
            left_roots,
            right_roots,
            state,
        )

    _, input_low, _ = norm_back(
        own_tokens,
        after(mine, sums[0]),
        partner(other, 2),
        norm_gains[:1],
        middle_grad,
    )
    state = None
    if last >= 2:
        state = update(2, state, input_low)
    if last >= 1:
        state = update(1, state, input_low)
    gain_sums = after(gain_sums, input_low, *(state or ()))
    gain_sums = gain_sums + partner(gain_sums, 1)
    bit = 1
    while bit < dp_count:
        gain_sums = gain_sums + lax.ppermute(
            gain_sums, "dp", [(i, i ^ bit) for i in range(dp_count)]
        )
        bit *= 2
    input_parts = spread_share(input_low, *(state or ()))
    gain_share = model_width // dp_count
    gain_grads = factor * lax.dynamic_slice_in_dim(gain_sums, d_index * gain_share, gain_share, 1)
    old_gains = lax.dynamic_slice_in_dim(norm_gains, d_index * gain_share, gain_share, 1)
    new_gains = old_gains - gain_rate * gain_grads
    out_parts = spread_share(after(out_low, input_low), *(state or ()))
    block_out = to_true(out_parts).reshape(sequences, length, model_width)
    input_grad = to_true(input_parts).astype(F32).reshape(sequences, length, model_width)
    grads, new_weights, new_ema, new_left, new_right = update(
        0, state, input_grad, block_out, new_gains
    )
    return (
        block_out,
        input_grad,
        grads,
        new_weights,
        new_ema,
        new_left,
        new_right,
        gain_grads,
        new_gains,
    )


def solution(mesh):
    in_specs = (
        P("dp", None, None),
        P("dp", None, None),
        P("dp", None),
        P("dp", None),
        P(),
        P(("dp", "mp"), None, None),
        P(("dp", "mp"), None, None),
        P(("dp", "mp"), None, None),
        P(("dp", "mp"), None, None),
        P(("dp", "mp"), None, None),
        P(("dp", "mp"), None, None),
    )
    out_specs = (
        P("dp", None, None),
        P("dp", None, None),
        P(("dp", "mp"), None, None),
        P(("dp", "mp"), None, None),
        P(("dp", "mp"), None, None),
        P(("dp", "mp"), None, None),
        P(("dp", "mp"), None, None),
        P(None, "dp"),
        P(None, "dp"),
    )
    return jax.shard_map(
        on_device, mesh=mesh, in_specs=in_specs, out_specs=out_specs, check_vma=False
    )
```

```python
import functools

import jax
import jax.numpy as jnp
import numpy as np
from jax import lax
from jax.experimental import pallas as pl
from jax.experimental.pallas import tpu as pltpu
from jax.sharding import PartitionSpec as P

HEADS = 32
KV_HEADS = 4
HD = 64
FF = 5632
LOW = jnp.bfloat16
F32 = jnp.float32

weight_rate = 1.0
gain_rate = 0.2
average_decay = 0.9
VMEM_LIMIT = 60 * 1024 * 1024


def ring_order(count):
    return list(range(0, count, 2)) + list(range(1, count, 2))[::-1]


class Layout:
    def __init__(self, dp, own, rows, attn_cols, in_cols, out_attn_rows):
        self.dp, self.own = dp, own
        self.ring = ring_order(dp)
        n_in = rows * in_cols
        units = (in_cols - attn_cols) // 2
        kinds, spots, keys = [], [], []
        for k in range(dp * own):
            if k < n_in:
                r, c = divmod(k, in_cols)
                if c < attn_cols:
                    kinds.append(0), spots.append((0, r, c)), keys.append((0, k))
                else:
                    c -= attn_cols
                    kinds.append(2), spots.append((2, r, c)), keys.append((2, c % units / units, k))
            else:
                r, c = divmod(k - n_in, rows)
                if r < out_attn_rows:
                    kinds.append(1), spots.append((1, r, c)), keys.append((1, k))
                else:
                    kinds.append(2), spots.append((3, r - out_attn_rows, c))
                    keys.append((2, c / rows, k))
        self.order = np.zeros((dp, own), np.int32)
        for d in range(dp):
            self.order[d] = sorted(range(own), key=lambda l: keys[d * own + l])
        count = np.array(kinds).reshape(dp, own)
        first = int((count == 0).sum(1).max())
        second = int((count <= 1).sum(1).max())
        bounds = [0, first, max(first, second), own]
        self.chunks = [(a, b - a) for a, b in zip(bounds[:-1], bounds[1:]) if b > a]
        self.table = []
        for p, d in enumerate(self.ring):
            for j, l in enumerate(self.order[d]):
                (x,) = [i for i, (a, n) in enumerate(self.chunks) if a <= j < a + n]
                a, n = self.chunks[x]
                self.table.append(spots[d * own + int(l)] + (x, p * n + j - a))
        mixed = [p for p, d in enumerate(self.ring) if (count[d] == 1).any()]
        last, size = len(self.chunks) - 1, self.chunks[-1][1]
        late = [t for t in self.table if t[3] == last]
        self.first_late = {}
        for m, cols in ((2, units), (3, rows)):
            own_late = [c % cols for i, r, c, x, s in late if i == m and s // size not in mixed]
            self.first_late[m] = min(own_late, default=cols)
        self.strips = sorted(
            (m, r, c, s)
            for m, r, c, x, s in late
            if m >= 2 and s // size in mixed and c % (units if m == 2 else rows) < self.first_late[m]
        )

    def of_chunk(self, x, matrix):
        rows = [(s, r, c) for m, r, c, y, s in self.table if y == x and m == matrix]
        return np.array(sorted(rows), np.int32).reshape(-1, 3)

    def of_matrix(self, matrix, rows, cols):
        out = np.zeros((cols, rows, 2), np.int32)
        for m, r, c, x, s in self.table:
            if m == matrix:
                out[c, r] = (x, s)
        return out


def held(values):
    return pltpu.with_memory_space_constraint(values, pltpu.VMEM)


ANY = pl.BlockSpec(memory_space=pl.ANY)
SMEM = pl.BlockSpec(memory_space=pltpu.SMEM)
VMEM = pl.BlockSpec(memory_space=pltpu.VMEM)


def sort_blocks(weights, order, chunks):
    block = weights.shape[1:]
    total = sum(n for _, n in chunks)
    begin = chunks[0][0]

    def body(order_ref, w_ref, *refs):
        outs, (given, sem) = refs[: len(chunks)], refs[len(chunks) :]

        def load(j, carry):
            pltpu.make_async_copy(w_ref.at[order_ref[begin + j]], given.at[j], sem).start()
            return carry

        lax.fori_loop(0, total, load, 0)
        pltpu.make_async_copy(given, given, sem).wait()
        for (start, count), out in zip(chunks, outs):

            def one(j, carry, start=start, out=out):
                out[j] = given[start - begin + j].astype(LOW)
                return carry

            lax.fori_loop(0, count, one, 0)

    return pl.pallas_call(
        body,
        out_shape=[jax.ShapeDtypeStruct((n,) + block, LOW) for _, n in chunks],
        in_specs=[SMEM, ANY],
        out_specs=[VMEM] * len(chunks),
        scratch_shapes=[pltpu.VMEM((total,) + block, F32), pltpu.SemaphoreType.DMA],
        compiler_params=pltpu.CompilerParams(vmem_limit_bytes=VMEM_LIMIT),
        name="sort_blocks",
    )(order, weights)


def place_blocks(gathered, tables, shapes, partial):
    block = gathered.shape[-1]
    used = [i for i, t in enumerate(tables) if len(t)]
    if not used:
        return partial
    count = sum(len(tables[i]) for i in used)
    known = [i for i in used if partial[i] is not None]

    def body(*refs):
        table_refs = refs[: len(used)]
        src = refs[len(used)]
        outs = refs[len(used) + 1 + len(known) : -3]
        stage, sem_in, sem_out = refs[-3:]
        at = 0
        for i, table_ref in zip(used, table_refs):

            def load(j, carry, table_ref=table_ref, at=at):
                pltpu.make_async_copy(src.at[table_ref[3 * j]], stage.at[at + j], sem_in).start()
                return carry

            lax.fori_loop(0, len(tables[i]), load, 0)
            at += len(tables[i])
        pltpu.make_async_copy(stage, stage, sem_in).wait()
        at = 0
        for i, table_ref, out in zip(used, table_refs, outs):

            def put(j, carry, table_ref=table_ref, out=out, at=at):
                row = pl.multiple_of(table_ref[3 * j + 1] * block, block)
                col = pl.multiple_of(table_ref[3 * j + 2] * block, block)
                pltpu.make_async_copy(
                    stage.at[at + j], out.at[pl.ds(row, block), pl.ds(col, block)], sem_out
                ).start()
                return carry

            lax.fori_loop(0, len(tables[i]), put, 0)
            at += len(tables[i])
        pltpu.make_async_copy(stage, stage, sem_out).wait()

    results = pl.pallas_call(
        body,
        out_shape=[jax.ShapeDtypeStruct(shapes[i], LOW) for i in used],
        in_specs=[SMEM] * len(used) + [ANY] * (1 + len(known)),
        out_specs=[ANY] * len(used),
        input_output_aliases={len(used) + 1 + j: used.index(i) for j, i in enumerate(known)},
        scratch_shapes=[
            pltpu.VMEM((count, block, block), LOW),
            pltpu.SemaphoreType.DMA,
            pltpu.SemaphoreType.DMA,
        ],
        compiler_params=pltpu.CompilerParams(vmem_limit_bytes=VMEM_LIMIT),
        cost_estimate=pl.CostEstimate(
            flops=0, bytes_accessed=4 * count * block * block, transcendentals=0
        ),
        name="place_blocks",
    )(
        *[jnp.asarray(tables[i].reshape(-1)) for i in used],
        gathered,
        *[partial[i] for i in known],
    )
    merged = list(partial)
    for i, value in zip(used, results):
        merged[i] = value
    return merged


def fill(scratch, pieces, order_ref):
    count = pieces[0].shape[0]
    for i, piece in enumerate(pieces):
        if order_ref is None:
            scratch[i * count : (i + 1) * count] = piece[...]
        else:
            scratch[pl.ds(pl.multiple_of(order_ref[i] * count, count), count)] = piece[...]


def grad_blocks(
    left, rights, order, pairs, table, wide, buffers, sizes, block, span=None, done=()
):
    tokens, height = left.shape
    by_column = len(rights) > 1 and rights[0].shape[0] == tokens
    width = sum(x.shape[-1] for x in rights) if by_column else rights[0].shape[-1]
    if pairs:
        width *= 2
    rows, cols = height // block, width // block
    if pairs:
        table = np.stack([table[: cols // 2], table[cols // 2 :]], 1).reshape(table.shape)
        wide = 2
    first, end = (0, cols // wide) if span is None else span
    steps = end - first
    if steps <= 0:
        return buffers
    assert not by_column or wide == 1
    per_step = rows * wide
    targets = [
        [(j, x, spot) for j, (x, spot) in enumerate(step) if (x, spot) not in done]
        for step in table.reshape(cols // wide, per_step, 2).tolist()[first:end]
    ]
    assert all(targets)
    used = sorted({x for step in targets for _, x, _ in step})
    known = [x for x in used if buffers[x] is not None]
    n_order = 0 if order is None else 1
    joined = len(rights) > 1
    first_known = n_order + 1 + len(rights)
    first_out = first_known + len(known)

    def body(*refs):
        left_ref = refs[n_order]
        right_refs = refs[n_order + 1 : first_known]
        outs = refs[first_out : first_out + len(used)]
        stage, sems = refs[first_out + len(used) : first_out + len(used) + 2]
        t = pl.program_id(0)
        slot = lax.rem(t, 2)
        if joined:
            right_ref = refs[-1]
            if by_column:
                step = 0
                for piece in right_refs:
                    for at in range(0, piece.shape[1], block):

                        @pl.when(t + first == step)
                        def _(piece=piece, at=at):
                            right_ref[...] = piece[:, at : at + block]

                        step += 1
            else:
                fill(right_ref, right_refs, refs[0] if n_order else None)
            taken = right_ref[...]
        elif pairs:
            taken = jnp.concatenate([right_refs[0][0], right_refs[0][1]], axis=1)
        else:
            taken = right_refs[0][...]

        def finish(step):
            sent = stage.at[step % 2, : len(targets[step])]
            pltpu.make_async_copy(sent, sent, sems.at[step % 2]).wait()

        for step in range(2, steps):

            @pl.when(t == step)
            def _(step=step):
                finish(step - 2)

        def some(i, carry):
            at = pl.multiple_of(i * (few * block), block)
            part = lax.dot_general(
                left_ref[:, pl.ds(at, few * block)],
                taken,
                (((0,), (0,)), ((), ())),
                preferred_element_type=F32,
            ).astype(LOW)
            for r in range(few):
                for c in range(wide):
                    stage[slot, c * rows + i * few + r] = part[
                        r * block : (r + 1) * block, c * block : (c + 1) * block
                    ]
            return carry

        parts = 1 if first > 0 or rows < 8 else 2
        few = rows // parts if rows % parts == 0 else rows
        lax.fori_loop(0, rows // few, some, 0)
        for step in range(steps):

            @pl.when(t == step)
            def _(step=step):
                for j, x, spot in targets[step]:
                    pltpu.make_async_copy(
                        stage.at[step % 2, j], outs[used.index(x)].at[spot], sems.at[step % 2]
                    ).start()

        @pl.when(t == steps - 1)
        def _():
            for step in range(max(0, steps - 2), steps):
                finish(step)

    taken_width = wide * block
    if pairs:
        right_specs = [pl.BlockSpec((2, tokens, block), lambda j: (0, 0, first + j))]
    elif by_column:
        right_specs = [pl.BlockSpec(x.shape, lambda j: (0, 0)) for x in rights]
    else:
        right_specs = [
            pl.BlockSpec((x.shape[0], taken_width), lambda j: (0, first + j)) for x in rights
        ]
    results = pl.pallas_call(
        body,
        grid=(steps,),
        out_shape=[jax.ShapeDtypeStruct((sizes[x], block, block), LOW) for x in used],
        in_specs=[SMEM] * n_order
        + [pl.BlockSpec((tokens, height), lambda j: (0, 0))]
        + right_specs
        + [ANY] * len(known),
        out_specs=[ANY] * len(used),
        input_output_aliases={first_known + j: used.index(x) for j, x in enumerate(known)},
        scratch_shapes=[
            pltpu.VMEM((2, per_step, block, block), LOW),
            pltpu.SemaphoreType.DMA((2,)),
        ]
        + ([pltpu.VMEM((tokens, taken_width), LOW)] if joined else []),
        compiler_params=pltpu.CompilerParams(vmem_limit_bytes=VMEM_LIMIT),
        cost_estimate=pl.CostEstimate(
            flops=4 * tokens * height * wide * block * steps,
            bytes_accessed=2 * (tokens * (height + width) + height * width),
            transcendentals=0,
        ),
        name="grad_blocks",
    )(*([] if order is None else [order]), left, *rights, *[buffers[x] for x in known])
    merged = list(buffers)
    for x, value in zip(used, results):
        merged[x] = value
    return merged


def grad_strips(strips, buffer, block):
    def body(*refs):
        out, stage, sem = refs[-3:]
        at = 0
        for i, (_, _, _, half, blocks) in enumerate(strips):
            right = refs[2 * i + 1]
            part = lax.dot_general(
                refs[2 * i][...],
                right[...] if half is None else right[0],
                (((0,), (0,)), ((), ())),
                preferred_element_type=F32,
            ).astype(LOW)
            for c, spot in blocks:
                stage[at] = part[:, c * block : (c + 1) * block]
                pltpu.make_async_copy(stage.at[at], out.at[spot], sem).start()
                at += 1
        pltpu.make_async_copy(stage, stage, sem).wait()

    specs, values = [], []
    for left, row, right, half, blocks in strips:
        tokens = left.shape[0]
        wide = (max(c for c, _ in blocks) + 1) * block
        specs.append(pl.BlockSpec((tokens, block), lambda j, row=row: (0, row)))
        if half is None:
            specs.append(pl.BlockSpec((tokens, wide), lambda j: (0, 0)))
        else:
            specs.append(pl.BlockSpec((1, tokens, wide), lambda j, half=half: (half, 0, 0)))
        values += [left, right]
    count = sum(len(blocks) for *_, blocks in strips)
    return pl.pallas_call(
        body,
        grid=(1,),
        in_specs=specs + [ANY],
        out_specs=ANY,
        out_shape=jax.ShapeDtypeStruct(buffer.shape, LOW),
        input_output_aliases={len(specs): 0},
        scratch_shapes=[pltpu.VMEM((count, block, block), LOW), pltpu.SemaphoreType.DMA],
        compiler_params=pltpu.CompilerParams(vmem_limit_bytes=VMEM_LIMIT),
        cost_estimate=pl.CostEstimate(
            flops=4 * count * values[0].shape[0] * block**2,
            bytes_accessed=4 * count * block * values[0].shape[0],
            transcendentals=0,
        ),
        name="grad_strips",
    )(*values, buffer)


def feed_forward(pieces, weights, hidden_grad, block):
    share, width = pieces[0].shape
    count = len(pieces)
    rows = share * count
    half = rows // 2
    hidden = weights.shape[1] // 2
    steps = hidden // block
    tile = 2 * block

    def body(*refs):
        gate_w, up_w, grad_ref, row_w = refs[count : count + 4]
        hid_ref, out_ref, joined, kept_ref, sent_ref, held = refs[count + 4 :]
        t = pl.program_id(0)

        @pl.when(t == 0)
        def _():
            fill(joined, refs[:count], None)

        @pl.when(t < steps)
        def _():
            both = dot(joined[...], jnp.concatenate([gate_w[...], up_w[...]], axis=1))
            gate, up = both[:, :block], both[:, block:]
            grad = grad_ref[...]
            sig = jax.nn.sigmoid(gate)
            act = gate * sig
            hid_ref[...] = (act * up).astype(LOW)
            here = pl.ds(pl.multiple_of(t * block, block), block)
            gate_grad = (grad * up * sig * (1.0 + gate * (1.0 - sig))).astype(LOW)
            up_grad = (grad * act).astype(LOW)
            out_ref[0] = gate_grad
            out_ref[1] = up_grad
            held[0, :, here] = gate_grad
            held[1, :, here] = up_grad

        @pl.when(t >= steps)
        def _():
            total = dot_turned(held[0], row_w[:, :hidden]) + dot_turned(held[1], row_w[:, hidden:])
            total = total.astype(LOW)
            kept_ref[...] = total[:half]
            sent_ref[...] = total[half:]

    def first(j):
        return jnp.minimum(j, steps - 1)

    def second(j):
        return jnp.maximum(j - steps, 0)

    hid, grads, joined, kept, sent = pl.pallas_call(
        body,
        grid=(steps + width // tile,),
        in_specs=[pl.BlockSpec((share, width), lambda j: (0, 0))]
        + [VMEM] * (count - 1)
        + [
            pl.BlockSpec((width, block), lambda j: (0, first(j))),
            pl.BlockSpec((width, block), lambda j: (0, steps + first(j))),
            pl.BlockSpec((rows, block), lambda j: (0, first(j))),
            pl.BlockSpec((tile, 2 * hidden), lambda j: (second(j), 0)),
        ],
        out_specs=[
            pl.BlockSpec((rows, block), lambda j: (0, first(j))),
            pl.BlockSpec((2, rows, block), lambda j: (0, 0, first(j))),
            pl.BlockSpec((rows, width), lambda j: (0, 0)),
            pl.BlockSpec((half, tile), lambda j: (0, second(j))),
            pl.BlockSpec((half, tile), lambda j: (0, second(j))),
        ],
        out_shape=[
            jax.ShapeDtypeStruct((rows, hidden), LOW),
            jax.ShapeDtypeStruct((2, rows, hidden), LOW),
            jax.ShapeDtypeStruct((rows, width), LOW),
            jax.ShapeDtypeStruct((half, width), LOW),
            jax.ShapeDtypeStruct((half, width), LOW),
        ],
        scratch_shapes=[pltpu.VMEM((2, rows, hidden), LOW)],
        compiler_params=pltpu.CompilerParams(vmem_limit_bytes=48 * 1024 * 1024),
        cost_estimate=pl.CostEstimate(
            flops=8 * rows * width * hidden,
            bytes_accessed=2 * rows * width + 8 * width * hidden + 10 * rows * hidden,
            transcendentals=rows * hidden,
        ),
        name="feed_forward",
    )(pieces[0], *[held(x) for x in pieces[1:]], weights, weights, hidden_grad, weights)
    return hid, grads, joined, sent, kept


def project_rows(parts, weights, order, turned, tile):
    stacked = parts[0].ndim == 3
    rows = parts[0].shape[-2]
    half = rows // 2
    widths = [parts[0].shape[2]] * parts[0].shape[0] if stacked else [x.shape[1] for x in parts]
    starts = [sum(widths[:i]) for i in range(len(widths))]
    width = weights.shape[0] if turned else weights.shape[1]
    depth = sum(widths)
    share = rows // 4
    n_order = 0 if order is None else 1

    def body(*refs):
        part_refs = refs[n_order : n_order + len(parts)]
        w_ref, kept_ref, sent_ref = refs[n_order + len(parts) : n_order + len(parts) + 3]
        if n_order:
            joined = refs[-1]

            @pl.when(pl.program_id(0) == 0)
            def _():
                for i in range(4):
                    take = pl.ds(pl.multiple_of(refs[0][i] * share, share), share)
                    for part, at, size in zip(part_refs, starts, widths):
                        joined[i * share : (i + 1) * share, at : at + size] = part[take]

            pieces = [(joined[...], 0, depth)]
        elif stacked:
            pieces = [(part_refs[0][i], at, widths[i]) for i, at in enumerate(starts)]
        else:
            pieces = [(p[...], at, size) for p, at, size in zip(part_refs, starts, widths)]
        total = None
        for value, at, size in pieces:
            if turned:
                one = dot_turned(value, w_ref[:, at : at + size])
            else:
                one = dot(value, w_ref[at : at + size])
            total = one if total is None else total + one
        total = total.astype(LOW)
        kept_ref[...] = total[:half]
        sent_ref[...] = total[half:]

    whole = [pl.BlockSpec(x.shape, lambda j, n=x.ndim: (0,) * n) for x in parts]
    if turned:
        weight_spec = pl.BlockSpec((tile, depth), lambda j: (j, 0))
    else:
        weight_spec = pl.BlockSpec((depth, tile), lambda j: (0, j))
    kept, sent = pl.pallas_call(
        body,
        grid=(width // tile,),
        in_specs=[SMEM] * n_order + whole + [weight_spec],
        out_specs=[pl.BlockSpec((half, tile), lambda j: (0, j))] * 2,
        out_shape=[jax.ShapeDtypeStruct((half, width), LOW)] * 2,
        scratch_shapes=[pltpu.VMEM((rows, depth), LOW)] * n_order,
        compiler_params=pltpu.CompilerParams(vmem_limit_bytes=VMEM_LIMIT),
        cost_estimate=pl.CostEstimate(
            flops=2 * rows * depth * width,
            bytes_accessed=2 * (rows * depth + depth * width + rows * width),
            transcendentals=0,
        ),
        name="project_rows",
    )(*([order] if n_order else []), *parts, weights)
    return sent, kept


def down_back(grads, weights):
    rows, depth = grads.shape
    hidden = weights.shape[0]
    tile = 2 * LANES
    full, rest = divmod(hidden, tile)

    def body(g_ref, w_ref, *refs):
        o_ref = refs[-1]
        t = pl.program_id(0)

        @pl.when(t < full)
        def _():
            o_ref[...] = dot_turned(g_ref[...], w_ref[...])

        if rest:

            @pl.when(t == full)
            def _():
                o_ref[:, :rest] = dot_turned(g_ref[...], refs[0][...])

    assert rest == 0 or hidden % rest == 0
    specs = [
        pl.BlockSpec((rows, depth), lambda j: (0, 0)),
        pl.BlockSpec((tile, depth), lambda j: (jnp.minimum(j, full - 1), 0)),
    ]
    if rest:
        specs.append(pl.BlockSpec((rest, depth), lambda j: (hidden // rest - 1, 0)))
    return pl.pallas_call(
        body,
        grid=(full + (rest > 0),),
        in_specs=specs,
        out_specs=pl.BlockSpec((rows, tile), lambda j: (0, j)),
        out_shape=jax.ShapeDtypeStruct((rows, hidden), F32),
        compiler_params=pltpu.CompilerParams(vmem_limit_bytes=VMEM_LIMIT),
        cost_estimate=pl.CostEstimate(
            flops=2 * rows * depth * hidden,
            bytes_accessed=2 * depth * (rows + hidden) + 4 * rows * hidden,
            transcendentals=0,
        ),
        name="down_back",
    )(grads, *([weights] * len(specs[1:])))


def to_heads(pieces, weights, order):
    share = pieces[0].shape[0]
    width = weights.shape[0]

    rows = share * len(pieces)
    depth = weights.shape[1]
    tile = 2 * LANES

    def body(order_ref, *refs):
        w_ref, out_ref = refs[-2:]
        for i, piece in enumerate(refs[:-2]):
            put = pl.ds(pl.multiple_of(order_ref[i] * share, share), share)
            out_ref[put] = dot_turned(piece[...], w_ref[...]).astype(LOW)

    return pl.pallas_call(
        body,
        grid=(width // tile,),
        in_specs=[SMEM]
        + [pl.BlockSpec((share, depth), lambda j: (0, 0))] * len(pieces)
        + [pl.BlockSpec((tile, depth), lambda j: (j, 0))],
        out_specs=pl.BlockSpec((rows, tile), lambda j: (0, j)),
        out_shape=jax.ShapeDtypeStruct((rows, width), LOW),
        compiler_params=pltpu.CompilerParams(vmem_limit_bytes=VMEM_LIMIT),
        cost_estimate=pl.CostEstimate(
            flops=2 * rows * width * depth,
            bytes_accessed=2 * (rows + width) * depth,
            transcendentals=0,
        ),
        name="to_heads",
    )(order, *pieces, weights)


LANES = 128
QUERIES = 256
LONGEST = 512


def turn(values, cos, sin):
    lane = lax.broadcasted_iota(jnp.int32, values.shape, 1)
    other = jnp.where(
        lane % HD < HD // 2,
        pltpu.roll(values, LANES - HD // 2, 1),
        pltpu.roll(values, HD // 2, 1),
    )
    return values * cos + other * sin


def key_tables(cos, sin):
    lane = lax.broadcasted_iota(jnp.int32, cos.shape, 1)
    return jnp.where(lane < HD, cos, 1.0), jnp.where(lane < HD, sin, 0.0)


def project_heads(inputs, weights, cos, sin):
    rows, depth = inputs.shape
    width = weights.shape[1]
    assert width % LANES == 0 and HD == 64

    def body(x_ref, w_ref, cos_ref, sin_ref, q_ref, kv_ref):
        t = pl.program_id(0)

        def one(i, carry):
            here = pl.ds(pl.multiple_of(i * QUERIES, QUERIES), QUERIES)
            raw = dot(x_ref[here], w_ref[...])

            @pl.when(t < steps - 1)
            def _():
                turned = turn(raw, cos_ref[here], sin_ref[here])
                q_ref[here] = turned.astype(LOW) * LOW(HD**-0.5)

            @pl.when(t == steps - 1)
            def _():
                kv_ref[here] = turn(raw, *key_tables(cos_ref[here], sin_ref[here])).astype(LOW)

            return carry

        lax.fori_loop(0, rows // QUERIES, one, 0)

    steps = width // LANES
    whole = pl.BlockSpec((rows, LANES), lambda j: (0, 0))
    return pl.pallas_call(
        body,
        grid=(steps,),
        in_specs=[
            pl.BlockSpec((rows, depth), lambda j: (0, 0)),
            pl.BlockSpec((depth, LANES), lambda j: (0, j)),
            whole,
            whole,
        ],
        out_specs=[pl.BlockSpec((rows, LANES), lambda j: (0, jnp.minimum(j, steps - 2))), whole],
        out_shape=[
            jax.ShapeDtypeStruct((rows, width - LANES), LOW),
            jax.ShapeDtypeStruct((rows, LANES), LOW),
        ],
        compiler_params=pltpu.CompilerParams(vmem_limit_bytes=VMEM_LIMIT),
        cost_estimate=pl.CostEstimate(
            flops=2 * rows * depth * width,
            bytes_accessed=2 * (rows * depth + depth * width + rows * width),
            transcendentals=0,
        ),
        name="project_heads",
    )(inputs, weights, cos, sin)


def keep_keys(padded, kv_ref):
    padded[:LONGEST] = jnp.zeros((LONGEST, LANES), LOW)
    padded[LONGEST:] = kv_ref[...]


def visible(start_ref, at):
    shape = (LONGEST + QUERIES, QUERIES)
    key = at - LONGEST + lax.broadcasted_iota(jnp.int32, shape, 0)
    query = at + lax.broadcasted_iota(jnp.int32, shape, 1)
    return (key >= start_ref[:, pl.ds(at, QUERIES)]) & (key <= query)


def attend(queries, kv, starts):
    rows, width = queries.shape
    groups = width // LANES

    def body(start_ref, q_ref, kv_ref, o_ref, log_ref, padded):
        @pl.when(pl.program_id(0) == 0)
        def _():
            keep_keys(padded, kv_ref)

        def one(i, carry):
            at = pl.multiple_of(i * QUERIES, QUERIES)
            here = pl.ds(at, QUERIES)
            seen = visible(start_ref, at)
            window = padded[pl.ds(at, LONGEST + QUERIES)]
            keys, values = window[:, :HD], window[:, HD:]
            for h in range(LANES // HD):
                query = q_ref[here, h * HD : (h + 1) * HD]
                scores = jnp.where(seen, dot_turned(keys, query), -1e30)
                top = jnp.max(scores, axis=0, keepdims=True)
                expo = jnp.exp(scores - top)
                total = jnp.sum(expo, axis=0, keepdims=True)
                probs = (expo * (1.0 / total)).astype(LOW)
                o_ref[here, h * HD : (h + 1) * HD] = lax.dot_general(
                    probs, values, (((0,), (0,)), ((), ())), preferred_element_type=F32
                ).astype(LOW)
                log_ref[0, h : h + 1, here] = top + jnp.log(total)
            return carry

        lax.fori_loop(0, rows // QUERIES, one, 0)

    column = pl.BlockSpec((rows, LANES), lambda j: (0, j))
    return pl.pallas_call(
        body,
        grid=(groups,),
        in_specs=[
            pl.BlockSpec((1, rows), lambda j: (0, 0)),
            column,
            pl.BlockSpec((rows, LANES), lambda j: (0, 0)),
        ],
        out_specs=[column, pl.BlockSpec((1, LANES // HD, rows), lambda j: (j, 0, 0))],
        out_shape=[
            jax.ShapeDtypeStruct((rows, width), LOW),
            jax.ShapeDtypeStruct((groups, LANES // HD, rows), F32),
        ],
        scratch_shapes=[pltpu.VMEM((LONGEST + rows, LANES), LOW)],
        compiler_params=pltpu.CompilerParams(vmem_limit_bytes=VMEM_LIMIT),
        cost_estimate=pl.CostEstimate(
            flops=30 * rows * rows * width,
            bytes_accessed=4 * rows * width,
            transcendentals=rows * rows * width // HD,
        ),
        name="attend",
    )(starts, queries, kv)


def attend_back(queries, kv, starts, logs, grads, cos, sin):
    rows, width = queries.shape
    groups = width // LANES

    def body(
        start_ref, q_ref, kv_ref, log_ref, g_ref, cos_ref, sin_ref, dq_ref, sum_ref, acc, padded
    ):
        @pl.when(pl.program_id(0) == 0)
        def _():
            keep_keys(padded, kv_ref)
            acc[...] = jnp.zeros_like(acc)

        def one(i, carry):
            at = pl.multiple_of(i * QUERIES, QUERIES)
            here = pl.ds(at, QUERIES)
            there = pl.ds(at, LONGEST + QUERIES)
            seen = visible(start_ref, at)
            window = padded[there]
            keys, values = window[:, :HD], window[:, HD:]
            parts = []
            key_part, value_part = 0.0, 0.0
            for h in range(LANES // HD):
                query = q_ref[here, h * HD : (h + 1) * HD]
                grad = g_ref[here, h * HD : (h + 1) * HD]
                scores = jnp.where(seen, dot_turned(keys, query), -1e30)
                probs = jnp.exp(scores - log_ref[0, h : h + 1, here])
                value_part += dot(probs.astype(LOW), grad)
                prob_grads = dot_turned(values, grad)
                inner = jnp.sum(probs * prob_grads, axis=0, keepdims=True)
                score_grads = (probs * (prob_grads - inner)).astype(LOW)
                key_part += dot(score_grads, query)
                parts.append(
                    lax.dot_general(
                        score_grads, keys, (((0,), (0,)), ((), ())), preferred_element_type=F32
                    )
                )
            acc[there] += jnp.concatenate([key_part, value_part], axis=1)
            dq_ref[here] = turn(
                jnp.concatenate(parts, axis=1) * HD**-0.5, cos_ref[here], -sin_ref[here]
            ).astype(LOW)
            return carry

        lax.fori_loop(0, rows // QUERIES, one, 0)

        @pl.when(pl.program_id(0) == groups - 1)
        def _():
            key_cos, key_sin = key_tables(cos_ref[...], sin_ref[...])
            sum_ref[...] = turn(acc[LONGEST:], key_cos, -key_sin).astype(LOW)

    column = pl.BlockSpec((rows, LANES), lambda j: (0, j))
    whole = pl.BlockSpec((rows, LANES), lambda j: (0, 0))
    return pl.pallas_call(
        body,
        grid=(groups,),
        in_specs=[
            pl.BlockSpec((1, rows), lambda j: (0, 0)),
            column,
            whole,
            pl.BlockSpec((1, LANES // HD, rows), lambda j: (j, 0, 0)),
            column,
            whole,
            whole,
        ],
        out_specs=[column, whole],
        out_shape=[
            jax.ShapeDtypeStruct((rows, width), LOW),
            jax.ShapeDtypeStruct((rows, LANES), LOW),
        ],
        scratch_shapes=[
            pltpu.VMEM((LONGEST + rows, LANES), F32),
            pltpu.VMEM((LONGEST + rows, LANES), LOW),
        ],
        compiler_params=pltpu.CompilerParams(vmem_limit_bytes=VMEM_LIMIT),
        cost_estimate=pl.CostEstimate(
            flops=80 * rows * rows * width,
            bytes_accessed=16 * rows * width,
            transcendentals=rows * rows * width // HD,
        ),
        name="attend_back",
    )(starts, queries, kv, logs, grads, cos, sin)


def shampoo(sums, places, factor, weights, ema, left, right, left_roots, right_roots, before):
    count, block, _ = sums.shape
    group = 3 if count % 3 == 0 else 2 if count % 2 == 0 else 1
    steps = count // group
    depth = min(6, steps)
    extra = [] if before is None else list(before)

    def mm(a, b, dims):
        return lax.dot_general(
            a.astype(LOW), b.astype(LOW), (dims, ((), ())), preferred_element_type=F32
        )

    def body(places_ref, g_ref, *refs):
        ins, outs = refs[:6], refs[6 + len(extra) : 11 + len(extra)]
        given, made, sem_in, sem_out = refs[11 + len(extra) :]

        def load(t, slot):
            for u in range(group):
                place = places_ref[t * group + u]
                for i, ref in enumerate(ins):
                    pltpu.make_async_copy(
                        ref.at[place], given.at[slot, u, i], sem_in.at[slot]
                    ).start()

        def wait(buffer, slot, sems):
            pltpu.make_async_copy(buffer.at[slot], buffer.at[slot], sems.at[slot]).wait()

        for t in range(depth):
            load(t, t)

        def step(t, carry):
            slot = lax.rem(t, depth)
            wait(given, slot, sem_in)

            @pl.when(t >= depth)
            def _():
                wait(made, slot, sem_out)

            both = 0.5 * factor * factor
            for u in range(group):
                low = g_ref[t * group + u]
                made[slot, u, 0] = low.astype(F32) * factor
                made[slot, u, 3] = 0.5 * given[slot, u, 2] + both * mm(low, low, ((1,), (1,)))
                made[slot, u, 4] = 0.5 * given[slot, u, 3] + both * mm(low, low, ((0,), (0,)))
                part = mm(low, given[slot, u, 5], ((1,), (0,))) * factor
                fresh = given[slot, u, 0] - weight_rate * mm(given[slot, u, 4], part, ((1,), (0,)))
                made[slot, u, 1] = fresh
                made[slot, u, 2] = (
                    average_decay * given[slot, u, 1] + (1.0 - average_decay) * fresh
                )
            for u in range(group):
                place = places_ref[t * group + u]
                for i, ref in enumerate(outs):
                    pltpu.make_async_copy(
                        made.at[slot, u, i], ref.at[place], sem_out.at[slot]
                    ).start()

            @pl.when(t + depth < steps)
            def _():
                load(t + depth, slot)

            return carry

        lax.fori_loop(0, steps, step, 0)
        for t in range(steps - depth, steps):
            wait(made, t % depth, sem_out)

    return pl.pallas_call(
        body,
        out_shape=[jax.ShapeDtypeStruct(weights.shape, F32)] * 5,
        in_specs=[SMEM, VMEM] + [ANY] * (6 + len(extra)),
        out_specs=[ANY] * 5,
        input_output_aliases={8 + i: i for i in range(len(extra))},
        scratch_shapes=[
            pltpu.VMEM((depth, group, 6, block, block), F32),
            pltpu.VMEM((depth, group, 5, block, block), F32),
            pltpu.SemaphoreType.DMA((depth,)),
            pltpu.SemaphoreType.DMA((depth,)),
        ],
        compiler_params=pltpu.CompilerParams(vmem_limit_bytes=VMEM_LIMIT),
        cost_estimate=pl.CostEstimate(
            flops=8 * count * block**3,
            bytes_accessed=46 * count * block * block,
            transcendentals=0,
        ),
        name="shampoo",
    )(places, sums, weights, ema, left, right, left_roots, right_roots, *extra)


def rows_call(body, ins, outs, name, step=128, work=10, here=None):
    rows = max(x.shape[0] for x in ins)

    def spec(x):
        if x.shape[0] == rows:
            return pl.BlockSpec((step, x.shape[1]), lambda j: (j, 0))
        return pl.BlockSpec(x.shape, lambda j: (0, 0))

    return pl.pallas_call(
        body,
        grid=(rows // step,),
        in_specs=[VMEM if i == here else spec(x) for i, x in enumerate(ins)],
        out_specs=[spec(x) for x in outs],
        out_shape=outs,
        compiler_params=pltpu.CompilerParams(vmem_limit_bytes=VMEM_LIMIT),
        cost_estimate=pl.CostEstimate(
            flops=work * rows * ins[0].shape[1],
            bytes_accessed=sum(x.size * x.dtype.itemsize for x in list(ins) + list(outs)),
            transcendentals=0,
        ),
        name=name,
    )(*ins)


def add_near(kept, got):
    share = kept.shape[0] // 2
    width = kept.shape[1]
    step = 128

    def body(a_ref, c_ref, got_ref, mine_ref, other_ref):
        at = pl.multiple_of(pl.program_id(0) * step, step)
        near, far = got_ref[pl.ds(at, step)], got_ref[pl.ds(share + at, step)]
        mine_ref[...] = a_ref[...].astype(F32) + near.astype(F32)
        other_ref[...] = (c_ref[...].astype(F32) + far.astype(F32)).astype(LOW)

    first = pl.BlockSpec((step, width), lambda j: (j, 0))
    second = pl.BlockSpec((step, width), lambda j: (share // step + j, 0))
    return pl.pallas_call(
        body,
        grid=(share // step,),
        in_specs=[first, second, VMEM],
        out_specs=[first] * 2,
        out_shape=[
            jax.ShapeDtypeStruct((share, width), F32),
            jax.ShapeDtypeStruct((share, width), LOW),
        ],
        compiler_params=pltpu.CompilerParams(vmem_limit_bytes=VMEM_LIMIT),
        cost_estimate=pl.CostEstimate(
            flops=2 * share * width, bytes_accessed=14 * share * width, transcendentals=0
        ),
        name="add_near",
    )(kept, kept, held(got))


def second_norm(tokens, mine, got, gain):
    step = 128

    def body(x_ref, a_ref, b_ref, gain_ref, middle_ref, low_ref):
        got = b_ref[pl.ds(pl.multiple_of(pl.program_id(0) * step, step), step)]
        middle = x_ref[...].astype(F32) + (a_ref[...] + got.astype(F32))
        middle_ref[...] = middle
        scale = lax.rsqrt(jnp.mean(middle * middle, axis=-1, keepdims=True) + 1e-05)
        low_ref[...] = (middle * scale * gain_ref[...]).astype(LOW)

    return rows_call(
        body,
        [tokens, mine, held(got), gain],
        [jax.ShapeDtypeStruct(tokens.shape, F32), jax.ShapeDtypeStruct(tokens.shape, LOW)],
        "second_norm",
        step,
        here=2,
    )


def first_norm(tokens, gain):
    def body(x_ref, gain_ref, low_ref):
        x = x_ref[...].astype(F32)
        scale = lax.rsqrt(jnp.mean(x * x, axis=-1, keepdims=True) + 1e-05)
        low_ref[...] = (x * scale * gain_ref[...]).astype(LOW)

    return rows_call(
        body,
        [tokens, gain],
        [jax.ShapeDtypeStruct(tokens.shape, LOW)],
        "first_norm",
    )[0]


def norm_back(values, mine, got, gain, residual):
    step = 128

    def body(x_ref, a_ref, b_ref, gain_ref, r_ref, out_ref, low_ref, sum_ref):
        x = x_ref[...].astype(F32)
        got = b_ref[pl.ds(pl.multiple_of(pl.program_id(0) * step, step), step)]
        grad = a_ref[...] + got.astype(F32)
        scale = lax.rsqrt(jnp.mean(x * x, axis=-1, keepdims=True) + 1e-05)
        unit = x * scale
        scaled = grad * gain_ref[...]
        out = r_ref[...].astype(F32) + scale * (
            scaled - unit * jnp.mean(scaled * unit, axis=-1, keepdims=True)
        )
        out_ref[...] = out
        low_ref[...] = out.astype(LOW)

        @pl.when(pl.program_id(0) == 0)
        def _():
            sum_ref[...] = jnp.zeros_like(sum_ref)

        sum_ref[...] += jnp.sum(grad * unit, axis=0, keepdims=True)

    shape = values.shape
    return rows_call(
        body,
        [values, mine, held(got), gain, residual],
        [
            jax.ShapeDtypeStruct(shape, F32),
            jax.ShapeDtypeStruct(shape, LOW),
            jax.ShapeDtypeStruct((1, shape[1]), F32),
        ],
        "norm_back",
        step,
        here=2,
        work=1000000,
    )


def doc_positions(doc_ids):
    length = doc_ids.shape[-1]
    offsets = jnp.arange(length, dtype=jnp.int32)
    starts = jnp.concatenate(
        [jnp.ones(doc_ids.shape[:-1] + (1,), jnp.bool_), doc_ids[..., 1:] != doc_ids[..., :-1]],
        axis=-1,
    )
    first_index = lax.cummax(jnp.where(starts, offsets, 0), axis=doc_ids.ndim - 1)
    return offsets - first_index


def rope_tables(positions, head_size):
    half_size = head_size // 2
    exponent = jnp.arange(half_size, dtype=F32) * (2.0 / head_size)
    inverse = jnp.power(F32(10000.0), -exponent)
    angles = positions.astype(F32)[..., None] * inverse
    cos, sin = jnp.cos(angles), jnp.sin(angles)
    repeats = LANES // head_size
    return (
        jnp.concatenate([cos, cos] * repeats, axis=-1),
        jnp.concatenate([-sin, sin] * repeats, axis=-1),
    )


def after(value, *others):
    return lax.optimization_barrier((value,) + others)[0]


def dot(left, right):
    return jnp.dot(left, right, preferred_element_type=F32)


def dot_turned(left, right):
    return lax.dot_general(left, right, (((1,), (1,)), ((), ())), preferred_element_type=F32)


EXCHANGE = (0, 2, 1, 3)


def on_device(
    tokens_in,
    cotangent,
    select_mask,
    doc_ids,
    norm_gains,
    weight_blocks,
    ema_blocks,
    left_stats,
    right_stats,
    left_roots,
    right_roots,
):
    mp_count = lax.axis_size("mp")
    dp_count = lax.axis_size("dp")
    sequences, length, model_width = tokens_in.shape
    assert sequences == 1 and mp_count == 4 and dp_count & (dp_count - 1) == 0
    rows = sequences * length
    own, block, _ = weight_blocks.shape
    query_cols = HEADS * HD // mp_count
    key_cols = KV_HEADS * HD // mp_count
    hidden_cols = FF // mp_count
    assert KV_HEADS == mp_count and length % QUERIES == 0
    row_blocks = model_width // block
    attn_blocks = (query_cols + 2 * key_cols) // block
    hidden_blocks = hidden_cols // block
    in_blocks = attn_blocks + 2 * hidden_blocks
    out_attn_blocks = query_cols // block
    share = rows // mp_count
    m_index = lax.axis_index("mp")
    d_index = lax.axis_index("dp")

    plan = Layout(dp_count, own, row_blocks, attn_blocks, in_blocks, out_attn_blocks)
    order = lax.dynamic_slice_in_dim(jnp.asarray(plan.order), d_index, 1, 0).reshape(-1)
    shapes = [
        (model_width, attn_blocks * block),
        (query_cols, model_width),
        (model_width, 2 * hidden_cols),
        (hidden_cols, model_width),
    ]

    def partner(values, bit):
        return lax.ppermute(values, "mp", [(i, i ^ bit) for i in range(mp_count)])

    def true_share(values, group):
        return lax.dynamic_slice_in_dim(values, (m_index ^ group) * share, share, 0)

    def to_exchange(values):
        return jnp.concatenate([true_share(values, g) for g in EXCHANGE], axis=0)

    def to_true(parts):
        by_group = [parts[EXCHANGE.index(g)] for g in range(4)]
        low, high = m_index & 1, m_index & 2
        pairs = []
        for a, b in ((0, 1), (2, 3)):
            pairs.append(
                (
                    jnp.where(low == 0, by_group[a], by_group[b]),
                    jnp.where(low == 0, by_group[b], by_group[a]),
                )
            )
        flat = []
        for first, second in ((0, 1), (1, 0)):
            for i in range(2):
                flat.append(jnp.where(high == 0, pairs[first][i], pairs[second][i]))
        return jnp.concatenate(flat, axis=0)

    def near_sum(sent, kept):
        return add_near(kept, partner(sent, 1))

    def spread_share(mine, *cover):
        far = partner(mine, 2)
        near = partner(mine, 1)
        if cover:
            far = after(far, *cover)
        return [mine, far, near, partner(far, 1)]

    sorted_low = list(sort_blocks(weight_blocks, order, plan.chunks[:1]))
    if len(plan.chunks) > 1:
        sorted_low += sort_blocks(
            weight_blocks, after(order, *sorted_low), plan.chunks[1:]
        )
    gathered = [
        lax.all_gather(chunk, "dp", axis=0, tiled=True, axis_index_groups=[plan.ring])
        for chunk in sorted_low
    ]
    none = np.zeros((0, 3), np.int32)
    last = len(gathered) - 1

    def place(x, source, which, matrices):
        tables = [plan.of_chunk(x, i) if i in which else none for i in range(4)]
        return place_blocks(source, tables, shapes, matrices)

    matrices = place(0, gathered[0], (0, 1, 2, 3), [None] * 4)
    w_qkv = matrices[0]
    if last >= 1:
        matrices = place(1, gathered[1], (1,), matrices)
    w_attn_out = matrices[1]

    positions = doc_positions(doc_ids)
    starts = jnp.arange(length, dtype=jnp.int32)[None] - positions
    cos, sin = rope_tables(positions[0], HD)

    tokens_low = tokens_in.reshape(rows, model_width)
    first_in = first_norm(tokens_low, norm_gains[:1])
    out_grad = cotangent.reshape(rows, model_width) * select_mask.astype(LOW).reshape(rows, 1)
    own_tokens = true_share(tokens_low, 0)
    own_grad = true_share(out_grad, 0)
    mlp_grad = to_exchange(out_grad)
    tokens_local = to_exchange(tokens_low)
    unit_scale = lax.rsqrt(
        jnp.mean(jnp.square(tokens_local.astype(F32)), axis=-1, keepdims=True) + 1e-05
    )

    shares = (m_index ^ jnp.array(EXCHANGE, jnp.int32)).astype(jnp.int32)
    queries, kv = project_heads(first_in, w_qkv, cos, sin)
    kv, mlp_grad, own_tokens, own_grad, tokens_local, unit_scale = lax.optimization_barrier(
        (kv, mlp_grad, own_tokens, own_grad, tokens_local, unit_scale)
    )
    mixed, logs = attend(queries, kv, starts)
    attended_sent, attended_kept = project_rows([mixed], w_attn_out, shares, False, 512)
    mine, other = near_sum(attended_sent, attended_kept)
    if last >= 1:
        matrices = place(1, after(gathered[1], other), (2, 3), matrices)
        mine, *matrices[2:] = lax.optimization_barrier((mine, *matrices[2:]))
    middle, second_low = second_norm(own_tokens, mine, partner(other, 2), norm_gains[1:])
    if last >= 2:
        matrices = place(2, after(gathered[2], second_low), (2, 3), matrices)
    w_gateup, w_down = matrices[2:]
    hidden_grad = down_back(mlp_grad, w_down)
    second_pieces = spread_share(second_low, hidden_grad)
    hidden, gateup_grad, second_in, second_sent, second_kept = feed_forward(
        second_pieces, w_gateup, hidden_grad, block
    )

    sizes = [dp_count * n for _, n in plan.chunks]
    sums = [None] * len(sizes)
    reduced = [None] * len(sizes)

    def scatter(x):
        reduced[x] = lax.psum_scatter(
            sums[x], "dp", scatter_dimension=0, tiled=True, axis_index_groups=[plan.ring]
        )

    def known(values):
        return [x for x in values if x is not None]

    cuts = {2: 0, 3: 0}
    sent = set()
    if last >= 2:
        cuts = {2: plan.first_late[2], 3: plan.first_late[3] // 2}
        sent = {(last, spot) for *_, spot in plan.strips}
    def down_grads(sums, hidden, span):
        table = plan.of_matrix(3, hidden_blocks, row_blocks)
        return grad_blocks(
            hidden, [mlp_grad], None, False, table, 2, sums, sizes, block, span, sent
        )

    def gateup_grads(sums, second_in, span):
        table = plan.of_matrix(2, row_blocks, 2 * hidden_blocks)
        return grad_blocks(
            second_in, [gateup_grad], None, True, table, 2, sums, sizes, block, span, sent
        )

    sums = down_grads(sums, after(hidden, second_sent), (cuts[3], row_blocks // 2))
    mine, other = near_sum(second_sent, after(second_kept, *known(sums)))
    if sent:
        strips = {}
        for matrix, r, c, spot in plan.strips:
            half = c // hidden_blocks if matrix == 2 else None
            at = c if half is None else c % hidden_blocks
            strips.setdefault((matrix, r, half), []).append((at, spot))
        sums[last] = grad_strips(
            [
                (
                    after(second_in, other) if matrix == 2 else hidden,
                    r,
                    gateup_grad if matrix == 2 else mlp_grad,
                    half,
                    blocks,
                )
                for (matrix, r, half), blocks in strips.items()
            ],
            sums[last],
            block,
        )

    sums = gateup_grads(sums, after(second_in, other), (cuts[2], hidden_blocks))
    if last >= 2:
        scatter(2)
    got = partner(other, 2)
    mine = after(mine, *known(sums[:2]))
    middle_grad, attn_low, second_gain = norm_back(
        middle, mine, got, norm_gains[1:], own_grad
    )
    sums = gateup_grads(sums, after(second_in, attn_low), (0, cuts[2]))
    sums = down_grads(sums, after(hidden, attn_low), (0, cuts[3]))
    attn_grad = spread_share(attn_low, *known(sums[:2]))
    sums = grad_blocks(
        mixed,
        attn_grad,
        shares,
        False,
        plan.of_matrix(1, out_attn_blocks, row_blocks),
        4,
        sums,
        sizes,
        block,
    )
    if last >= 1:
        scatter(1)

    feed_sent, feed_kept = project_rows(
        [after(hidden, *known(sums[:2]))], w_down, None, False, 512
    )
    feed_mine, feed_other = near_sum(feed_sent, feed_kept)
    mixed_grad = to_heads(attn_grad, after(w_attn_out, feed_other), shares)
    query_grad, kv_grad = attend_back(queries, kv, starts, logs, mixed_grad, cos, sin)
    feed_part = after(feed_mine, query_grad) + partner(feed_other, 2).astype(F32)
    out_low = (middle + feed_part).astype(LOW)
    qkv_grads = [query_grad, kv_grad]
    first_sent, first_kept = project_rows(
        [after(query_grad, out_low), kv_grad], w_qkv, shares, True, 512
    )
    mine, other = near_sum(first_sent, first_kept)

    half = rows // 2
    first_gain = sum(
        jnp.sum(part.astype(F32) * (x.astype(F32) * scale), axis=0, keepdims=True)
        for part, x, scale in (
            (first_kept, tokens_local[:half], unit_scale[:half]),
            (first_sent, tokens_local[half:], unit_scale[half:]),
        )
    )
    gain_sums = jnp.concatenate([first_gain, second_gain], axis=0)
    gain_sums = gain_sums + partner(gain_sums, 2)
    other = after(other, gain_sums)
    sums = grad_blocks(
        after(first_in, other),
        qkv_grads,
        None,
        False,
        plan.of_matrix(0, row_blocks, attn_blocks),
        1,
        sums,
        sizes,
        block,
    )
    scatter(0)
    factor = float(rows * dp_count) ** (-0.5)

    def update(x, state, *others):
        start, count = plan.chunks[x]
        return shampoo(
            reduced[x],
            after(lax.slice_in_dim(order, start, start + count), *others),
            factor,
            weight_blocks,
            ema_blocks,
            left_stats,
            right_stats,
            left_roots,
            right_roots,
            state,
        )

    _, input_low, _ = norm_back(
        own_tokens,
        after(mine, sums[0]),
        partner(other, 2),
        norm_gains[:1],
        middle_grad,
    )
    state = None
    if last >= 2:
        state = update(2, state, input_low)
    if last >= 1:
        state = update(1, state, input_low)
    gain_sums = after(gain_sums, input_low, *(state or ()))
    gain_sums = gain_sums + partner(gain_sums, 1)
    bit = 1
    while bit < dp_count:
        gain_sums = gain_sums + lax.ppermute(
            gain_sums, "dp", [(i, i ^ bit) for i in range(dp_count)]
        )
        bit *= 2
    input_parts = spread_share(input_low, *(state or ()))
    gain_share = model_width // dp_count
    gain_grads = factor * lax.dynamic_slice_in_dim(gain_sums, d_index * gain_share, gain_share, 1)
    old_gains = lax.dynamic_slice_in_dim(norm_gains, d_index * gain_share, gain_share, 1)
    new_gains = old_gains - gain_rate * gain_grads
    out_parts = spread_share(after(out_low, input_low), *(state or ()))
    block_out = to_true(out_parts).reshape(sequences, length, model_width)
    input_grad = to_true(input_parts).astype(F32).reshape(sequences, length, model_width)
    grads, new_weights, new_ema, new_left, new_right = update(
        0, state, input_grad, block_out, new_gains
    )
    return (
        block_out,
        input_grad,
        grads,
        new_weights,
        new_ema,
        new_left,
        new_right,
        gain_grads,
        new_gains,
    )


def solution(mesh):
    in_specs = (
        P("dp", None, None),
        P("dp", None, None),
        P("dp", None),
        P("dp", None),
        P(),
        P(("dp", "mp"), None, None),
        P(("dp", "mp"), None, None),
        P(("dp", "mp"), None, None),
        P(("dp", "mp"), None, None),
        P(("dp", "mp"), None, None),
        P(("dp", "mp"), None, None),
    )
    out_specs = (
        P("dp", None, None),
        P("dp", None, None),
        P(("dp", "mp"), None, None),
        P(("dp", "mp"), None, None),
        P(("dp", "mp"), None, None),
        P(("dp", "mp"), None, None),
        P(("dp", "mp"), None, None),
        P(None, "dp"),
        P(None, "dp"),
    )
    return jax.shard_map(
        on_device, mesh=mesh, in_specs=in_specs, out_specs=out_specs, check_vma=False
    )
```
